32 devices in a mesh: dp: 8 (over z, core), row: 2 (over x), col: 2 (over y).
Axes of the slice: x: 2, y: 2, z: 4, core: 2. Of those that a mesh axis runs over, the one named last changes fastest.
Arguments:
- tokens: float32 [24, 112, 28, 512], P('dp', 'row', 'col'), may hold values from -6 to 6
- position_index: int32 [49, 49], replicated, may hold values from 0 to 168, as said below
- first_gain: float32 [512], P('dp'), may hold values from 0.5 to 1.5
- first_shift: float32 [512], P('dp'), may hold values from -3 to 3
- joint_weight: float32 [512, 1536], P('dp'), may hold values from -0.25 to 0.25
- query_bias: float32 [512], P('dp'), may hold values from -3 to 3
- value_bias: float32 [512], P('dp'), may hold values from -3 to 3
- position_table: float32 [16, 169], P('dp'), may hold values from -4 to 4
- output_weight: float32 [512, 512], P('dp'), may hold values from -1 to 1
- output_bias: float32 [512], P('dp'), may hold values from -3 to 3
- second_gain: float32 [512], P('dp'), may hold values from 0.5 to 1.5
- second_shift: float32 [512], P('dp'), may hold values from -3 to 3
- expand_weight: float32 [512, 2048], P('dp'), may hold values from -0.25 to 0.25
- expand_bias: float32 [2048], P('dp'), may hold values from -3 to 3
- shrink_weight: float32 [2048, 512], P('dp'), may hold values from -0.25 to 0.25
- shrink_bias: float32 [512], P('dp'), may hold values from -3 to 3
- cotangent: float32 [24, 112, 28, 512], P('dp', 'row', 'col'), may hold values from -6 to 6
Outputs:
- result: float32 [24, 112, 28, 512], P('dp', 'row', 'col')
- grad_tokens: float32 [24, 112, 28, 512], P('dp', 'row', 'col')
- grad_first_gain: float32 [512], P('dp')
- grad_first_shift: float32 [512], P('dp')
- grad_joint_weight: float32 [512, 1536], P('dp')
- grad_query_bias: float32 [512], P('dp')
- grad_value_bias: float32 [512], P('dp')
- grad_position_table: float32 [16, 169], P('dp')
- grad_output_weight: float32 [512, 512], P('dp')
- grad_output_bias: float32 [512], P('dp')
- grad_second_gain: float32 [512], P('dp')
- grad_second_shift: float32 [512], P('dp')
- grad_expand_weight: float32 [512, 2048], P('dp')
- grad_expand_bias: float32 [2048], P('dp')
- grad_shrink_weight: float32 [2048, 512], P('dp')
- grad_shrink_bias: float32 [512], P('dp')
The draws below stay inside these ranges and needn't reach their ends.
Inputs may be any that keep to these rules, and one draw needn't show every extreme that they name: position_index[q, k] names the row of position_table for the offset between places q and k of a window; two pairs share a row exactly when their offsets are equal, and every row is named.
All inputs are finite; a program needn't handle non-finite values.
Results may differ from the reference program's by a relative error of at most 0.019.
Values may be sent and summed in bfloat16 or wider, within the bound.
No kernel may reach another device: no remote copies, remote signals or barrier semaphores. Data moves between devices by JAX's collectives and lax.ppermute only.
A program may use at most 256 MiB of HBM per device.

```python
import jax
import jax.numpy as jnp
from jax import lax

C = 512
HEADS = 16
MLP = 2048
HEAD_DIM = 32
WIN = 7
SHIFT = 3
WIN_TOK = 49
BIAS_ROWS = 169
GRID_R = 112
GRID_C = 28
IMAGES = 24


def draw_position_index(key, part):
    places = jnp.arange(WIN * WIN, dtype=jnp.int32)
    row_place = places // WIN
    col_place = places % WIN
    anchor = (row_place[:, None] - row_place[None, :] + WIN - 1) * (2 * WIN - 1)
    anchor = anchor + (col_place[:, None] - col_place[None, :] + WIN - 1)
    labels = jax.random.permutation(key, BIAS_ROWS).astype(jnp.int32)
    return labels[anchor]


def shard_levels(stream_key, extent, pieces, smallest, high):
    factor_of = 1.0
    for axis_at, shards_of in pieces:
        draws = jax.random.uniform(jax.random.fold_in(jax.random.fold_in(stream_key, 6), axis_at), (shards_of,), jnp.float32, smallest / len(pieces), high / len(pieces))
        factor_of = factor_of * jnp.repeat(jnp.exp(draws), extent[axis_at] // shards_of).reshape((-1,) + (1,) * (len(extent) - 1 - axis_at))
    return factor_of


def gaussian(stream_key, dims, width, limit, pieces=(), held_as=jnp.bfloat16):
    gain = shard_levels(stream_key, dims, pieces, -0.22, 0.18) if pieces else 1.0
    entries = jax.random.normal(stream_key, dims, jnp.float32) * width * gain
    return jnp.minimum(jnp.maximum(entries, -limit), limit).astype(held_as)


def setup_inputs(seed: int = 0) -> dict:
    keys = jax.random.split(jax.random.key(seed), 18)
    return {
        "tokens": gaussian(keys[0], (IMAGES, GRID_R, GRID_C, C), 1.0, 6.0, ((0, 8), (1, 2), (2, 2)), jnp.float32),
        "position_index": draw_position_index(jax.random.fold_in(keys[17], 71), 0),
        "first_gain": jnp.clip(1.0 + 0.1 * jax.random.normal(keys[2], (C,), jnp.float32), 0.5, 1.5),
        "first_shift": gaussian(keys[3], (C,), 0.5, 3.0, ((0, 8),), jnp.float32),
        "joint_weight": gaussian(keys[4], (C, 3 * C), C ** -0.5, 0.25, ((0, 8),), jnp.float32),
        "query_bias": gaussian(keys[5], (C,), 0.5, 3.0, ((0, 8),), jnp.float32),
        "value_bias": gaussian(keys[6], (C,), 0.5, 3.0, ((0, 8),), jnp.float32),
        "position_table": gaussian(keys[7], (HEADS, BIAS_ROWS), 1.0, 4.0, ((0, 8),), jnp.float32),
        "output_weight": gaussian(keys[8], (C, C), (C // 16) ** -0.5, 1.0, ((0, 8),), jnp.float32),
        "output_bias": gaussian(keys[9], (C,), 0.5, 3.0, ((0, 8),), jnp.float32),
        "second_gain": jnp.clip(1.0 + 0.1 * jax.random.normal(keys[10], (C,), jnp.float32), 0.5, 1.5),
        "second_shift": gaussian(keys[11], (C,), 0.5, 3.0, ((0, 8),), jnp.float32),
        "expand_weight": gaussian(keys[12], (C, MLP), C ** -0.5, 0.25, ((0, 8),), jnp.float32),
        "expand_bias": gaussian(keys[13], (MLP,), 0.5, 3.0, ((0, 8),), jnp.float32),
        "shrink_weight": gaussian(keys[14], (MLP, C), (MLP // 4) ** -0.5, 0.25, ((0, 8),), jnp.float32),
        "shrink_bias": gaussian(keys[15], (C,), 0.5, 3.0, ((0, 8),), jnp.float32),
        "cotangent": gaussian(keys[16], (IMAGES, GRID_R, GRID_C, C), 1.0, 6.0, ((0, 8), (1, 2), (2, 2)), jnp.float32),
    }


@jax.custom_vjp
def low(v):
    return lax.optimization_barrier(v.astype(jnp.bfloat16)).astype(jnp.float32)

@jax.custom_vjp
def low_back(v):
    return v

def low_keep(v):
    return (low(v), None)

def low_pass(kept, grad):
    return (grad,)

def back_keep(v):
    return (v, None)

def back_low(kept, grad):
    return (low(grad),)
low.defvjp(low_keep, low_pass)
low_back.defvjp(back_keep, back_low)
EPSILON = 1e-05
HIGHEST = lax.Precision.HIGHEST

def rounded_both(values):
    return low(low_back(values))

def layer_norm(values, scaling, offset):
    center = values - lax.optimization_barrier(jnp.mean(values, axis=-1, keepdims=True))
    spread = lax.optimization_barrier(jnp.mean(center * center, axis=-1, keepdims=True))
    return center * lax.rsqrt(spread + EPSILON) * scaling + offset

def to_windows(values):
    height, breadth, feats = values.shape
    values = values.reshape(height // WIN, WIN, breadth // WIN, WIN, feats)
    return values.transpose(0, 2, 1, 3, 4).reshape(-1, WIN * WIN, feats)

def from_windows(values, height, breadth):
    feats = values.shape[-1]
    values = values.reshape(height // WIN, breadth // WIN, WIN, WIN, feats)
    return values.transpose(0, 2, 1, 3, 4).reshape(height, breadth, feats)

def region_band(places, count):
    return jnp.where(places < count - WIN, 0, jnp.where(places < count - SHIFT, 1, 2)).astype(jnp.int32)

def one_image(params, image, region_win, position_index):
    first_gain, first_shift, joint_weight, query_bias, value_bias, position_table, output_weight, output_bias, second_gain, second_shift, expand_weight, expand_bias, shrink_weight, shrink_bias = params
    height, breadth = (image.shape[0], image.shape[1])
    hidden_one = low(layer_norm(image, first_gain, first_shift))
    hidden_one = jnp.roll(hidden_one, (-SHIFT, -SHIFT), axis=(0, 1))
    windowed = to_windows(hidden_one)
    count = windowed.shape[0]
    mixture = jnp.einsum('wtc,cf->wtf', windowed, joint_weight, precision=HIGHEST)
    mixture = mixture + jnp.concatenate([query_bias, jnp.zeros_like(query_bias), value_bias])
    mixture = mixture.reshape(count, WIN_TOK, 3, HEADS, HEAD_DIM)
    queries = rounded_both(mixture[:, :, 0])
    keys_all = rounded_both(mixture[:, :, 1])
    values_all = rounded_both(mixture[:, :, 2])
    raw = low_back(jnp.einsum('wqhd,wkhd->whqk', queries, keys_all, precision=HIGHEST))
    position = position_table[:, position_index]
    masking = jnp.where(region_win[:, :, None] == region_win[:, None, :], 0.0, -100.0)
    score = raw * HEAD_DIM ** (-0.5) + position[None] + masking[:, None]
    probs = low(jax.nn.softmax(score, axis=-1))
    attended = jnp.einsum('whqk,wkhd->wqhd', probs, values_all, precision=HIGHEST)
    attended = rounded_both(attended.reshape(count, WIN_TOK, C))
    branch = low_back(jnp.einsum('wtc,cf->wtf', attended, output_weight, precision=HIGHEST) + output_bias)
    branch = jnp.roll(from_windows(branch, height, breadth), (SHIFT, SHIFT), axis=(0, 1))
    middle = image + branch
    hidden_two = low(layer_norm(middle, second_gain, second_shift))
    before = low_back(jnp.einsum('rcf,fm->rcm', hidden_two, expand_weight, precision=HIGHEST) + expand_bias)
    active = low(jax.nn.gelu(before, approximate=False))
    closing = low_back(jnp.einsum('rcm,mf->rcf', active, shrink_weight, precision=HIGHEST) + shrink_bias)
    return middle + closing

def reference(tokens, position_index, first_gain, first_shift, joint_weight, query_bias, value_bias, position_table, output_weight, output_bias, second_gain, second_shift, expand_weight, expand_bias, shrink_weight, shrink_bias, cotangent):
    band_rows = region_band(jnp.arange(GRID_R, dtype=jnp.int32), GRID_R)
    band_cols = region_band(jnp.arange(GRID_C, dtype=jnp.int32), GRID_C)
    region_label = 3 * band_rows[:, None] + band_cols[None, :]
    region_win = to_windows(region_label[:, :, None])[:, :, 0]
    params = (first_gain, first_shift, joint_weight, query_bias, value_bias, position_table, output_weight, output_bias, second_gain, second_shift, expand_weight, expand_bias, shrink_weight, shrink_bias)

    def forward(params, tokens):
        rounded = tuple((low(param) for param in params))

        def single(image):
            return one_image(rounded, image, region_win, position_index)
        return lax.map(jax.checkpoint(single), tokens)
    result, pullback = jax.vjp(forward, params, tokens)
    grads, grad_tokens = pullback(cotangent)
    return (result, grad_tokens, grads[0], grads[1], grads[2], grads[3], grads[4], grads[5], grads[6], grads[7], grads[8], grads[9], grads[10], grads[11], grads[12], grads[13])
```

```python
import functools

import jax
import jax.numpy as jnp
from jax import lax
from jax.experimental import pallas as pl
from jax.experimental.pallas import tpu as pltpu
from jax.sharding import PartitionSpec as P

WIN = 7
SHIFT = 3
PAD = 8
WT = WIN * PAD
QL = 64
EPSILON = 1e-05
ROOT_HALF = 0.7071067811865476
NORMAL_PEAK = 0.3989422804014327
FAR_BELOW = -1000000000.0
BF = jnp.bfloat16
F32 = jnp.float32
BANDS = 4
VMEM_LIMIT = 60 * 1024 * 1024


def nn(a, b):
    return lax.dot_general(a, b, (((1,), (0,)), ((), ())), preferred_element_type=F32)


def nt(a, b):
    return lax.dot_general(a, b, (((1,), (1,)), ((), ())), preferred_element_type=F32)


def tn(a, b):
    return lax.dot_general(a, b, (((0,), (0,)), ((), ())), preferred_element_type=F32)


def norm_parts(values):
    center = values - jnp.mean(values, axis=-1, keepdims=True)
    inverse = lax.rsqrt(jnp.mean(center * center, axis=-1, keepdims=True) + EPSILON)
    return center * inverse, inverse


def norm_back(upper, normed, inverse, scaling):
    scaled = upper * scaling
    return inverse * (
        scaled
        - jnp.mean(scaled, axis=-1, keepdims=True)
        - normed * jnp.mean(scaled * normed, axis=-1, keepdims=True)
    )


def row_of(band, row):
    return ((2 * band) * WIN + row) * PAD


def extract(half, tile_ref, row_ref, col_ref, out_ref):
    for band in range(BANDS):
        for row in range(WIN):
            place = band * WIN + row
            at = row_of(band, row)
            zero = jnp.zeros((1, tile_ref.shape[-1]), F32)
            out_ref[at + 7 : at + 8, :] = zero
            out_ref[at + WT + 7 : at + WT + 8, :] = zero
            if place < BANDS * WIN - SHIFT:
                src = half * (BANDS * WIN) + (place + SHIFT)
                out_ref[at : at + 7, :] = tile_ref[0, src, 3:10, :]
                out_ref[at + WT : at + WT + 4, :] = tile_ref[0, src, 10:14, :]
            else:
                last = place + SHIFT - BANDS * WIN

                @pl.when(half == 0)
                def _():
                    src = place + SHIFT
                    out_ref[at : at + 7, :] = tile_ref[0, src, 3:10, :]
                    out_ref[at + WT : at + WT + 4, :] = tile_ref[0, src, 10:14, :]

                @pl.when(half != 0)
                def _():
                    out_ref[at : at + 7, :] = row_ref[0, last, 3:10, :]
                    out_ref[at + WT : at + WT + 4, :] = row_ref[0, last, 10:14, :]
        for j in range(SHIFT):
            src = half * (BANDS * WIN) + band * WIN
            for row in range(WIN):
                at = row_of(band, row) + WT + 4 + j
                out_ref[at : at + 1, :] = col_ref[0, j, pl.ds(src + row, 1), :]


def deposit(half, src_ref, tile_ref, row_ref, col_ref):
    for band in range(BANDS):
        for row in range(WIN):
            place = band * WIN + row
            at = row_of(band, row)
            left = src_ref[at : at + 7, :]
            right = src_ref[at + WT : at + WT + 4, :]
            if place < BANDS * WIN - SHIFT:
                dst = half * (BANDS * WIN) + (place + SHIFT)
                tile_ref[0, dst, 3:10, :] = left
                tile_ref[0, dst, 10:14, :] = right
            else:
                last = place + SHIFT - BANDS * WIN

                @pl.when(half == 0)
                def _():
                    dst = place + SHIFT
                    tile_ref[0, dst, 3:10, :] = left
                    tile_ref[0, dst, 10:14, :] = right

                @pl.when(half != 0)
                def _():
                    row_ref[0, last, 3:10, :] = left
                    row_ref[0, last, 10:14, :] = right
        for j in range(SHIFT):
            dst = half * (BANDS * WIN) + band * WIN
            for row in range(WIN):
                at = row_of(band, row) + WT + 4 + j
                col_ref[0, j, pl.ds(dst + row, 1), :] = src_ref[at : at + 1, :]


def spread(rows, head_size, lanes):
    heads = lanes // head_size
    rows = jnp.concatenate([rows, jnp.zeros((QL - WT, lanes), rows.dtype)], axis=0)
    lane = lax.broadcasted_iota(jnp.int32, (QL, lanes), 1) // head_size
    zero = jnp.zeros_like(rows)
    return jnp.concatenate([jnp.where(lane == h, rows, zero) for h in range(heads)], axis=0)


def collapse(wide, head_size, lanes):
    heads = lanes // head_size
    lane = lax.broadcasted_iota(jnp.int32, (WT, lanes), 1) // head_size
    out = wide[0:WT]
    for h in range(1, heads):
        out = jnp.where(lane == h, wide[h * QL : h * QL + WT], out)
    return out


def per_query(scores_low, feats, head_size):
    features = feats.shape[1]
    quad = 128 // head_size
    parts = []
    for g in range(features // 128):
        block = scores_low[:, g * quad * QL : (g + 1) * quad * QL]
        wide = tn(block, feats[:, g * 128 : (g + 1) * 128])
        parts.append(collapse(wide, head_size, 128))
    return jnp.concatenate(parts, axis=1)


def attend_kernel(
    head_size,
    tile_ref,
    row_ref,
    col_ref,
    weight_ref,
    vec_ref,
    bias_ref,
    xp_ref,
    hid_ref,
    qkv_ref,
    prob_ref,
    att_ref,
    mid_ref,
    wide_ref,
):
    half = pl.program_id(1)
    features = tile_ref.shape[-1]
    extract(half, tile_ref, row_ref, col_ref, xp_ref)
    normed, _ = norm_parts(xp_ref[...])
    hidden = (normed * vec_ref[0:1, :] + vec_ref[1:2, :]).astype(BF)
    hid_ref[...] = hidden
    scale = head_size ** (-0.5)
    for part in range(3):
        got = nn(hidden, weight_ref[:, part * features : (part + 1) * features])
        if part == 0:
            got = got + vec_ref[2:3, :]
        if part == 2:
            got = got + vec_ref[3:4, :]
        qkv_ref[:, :, part * features : (part + 1) * features] = got.reshape(
            2 * BANDS, WT, features
        ).astype(BF)

    group = 256
    span = group // head_size * QL
    for w in range(2 * BANDS):
        kind = w % 2
        edge = jnp.where(half == 0, 0, 1) if w // 2 == BANDS - 1 else 0
        for g in range(features // group):
            q = qkv_ref[w, :, g * group : (g + 1) * group]
            k = qkv_ref[w, :, features + g * group : features + (g + 1) * group]
            raw = nt(k, spread(q, head_size, group))
            score = raw * scale + bias_ref[edge, kind, :, g * span : (g + 1) * span]
            highest = jnp.max(score, axis=0, keepdims=True)
            grown = jnp.exp(score - highest)
            total = jnp.sum(grown, axis=0, keepdims=True)
            probs = (grown * (1.0 / total)).astype(BF)
            prob_ref[w, :, g * span : (g + 1) * span] = probs
            v = qkv_ref[w, :, 2 * features + g * group : 2 * features + (g + 1) * group]
            wide_ref[w * WT : (w + 1) * WT, g * group : (g + 1) * group] = per_query(
                probs, v, head_size
            )
    attended = wide_ref[...].astype(BF)
    att_ref[...] = attended
    branch = nn(attended, weight_ref[:, 3 * features :]) + vec_ref[4:5, :]
    mid_ref[...] = xp_ref[...] + branch


def mlp_kernel(
    tile_ref,
    row_ref,
    col_ref,
    mid_ref,
    att_ref,
    weight_ref,
    packed_ref,
    vec_ref,
    ebias_ref,
    res_ref,
    resrow_ref,
    rescol_ref,
    gmid_ref,
    gatt_ref,
    pack_ref,
    sums_ref,
    esum_ref,
    cot_ref,
    we_ref,
    ws_ref,
    ge_ref,
    gs_ref,
    go_ref,
    out_ref,
):
    half = pl.program_id(1)
    step = pl.program_id(0) * pl.num_programs(1) + half
    steps = pl.num_programs(0) * pl.num_programs(1)
    features = tile_ref.shape[-1]
    hidden_units = we_ref.shape[1]
    shards = pack_ref.shape[0]
    deep = features // shards
    blocks = hidden_units // features

    @pl.when(step == 0)
    def _():
        for d in range(shards):
            we_ref[d * deep : (d + 1) * deep, :] = packed_ref[d, 0:deep, :]
            for j in range(blocks):
                at = d * deep * blocks + j * deep
                ws_ref[at : at + deep, :] = packed_ref[
                    d, deep : 2 * deep, j * features : (j + 1) * features
                ]
        ge_ref[...] = jnp.zeros_like(ge_ref)
        gs_ref[...] = jnp.zeros_like(gs_ref)
        go_ref[...] = jnp.zeros_like(go_ref)
        sums_ref[...] = jnp.zeros_like(sums_ref)
        esum_ref[...] = jnp.zeros_like(esum_ref)

    extract(half, tile_ref, row_ref, col_ref, cot_ref)
    mid = mid_ref[...]
    normed, inverse = norm_parts(mid)
    hidden = (normed * vec_ref[5:6, :] + vec_ref[6:7, :]).astype(BF)
    hidden_t = hidden.T
    low = cot_ref[...].astype(BF)
    low_t = low.T
    out = mid + vec_ref[7:8, :]
    ghid = None
    chunk = features
    for c in range(hidden_units // chunk):
        cols = slice(c * chunk, (c + 1) * chunk)
        before = nn(hidden, we_ref[:, cols]) + ebias_ref[0:1, cols]
        phi = 0.5 * (1.0 + lax.erf(before * ROOT_HALF))
        slope = phi + before * (NORMAL_PEAK * jnp.exp(-0.5 * before * before))
        active = (before * phi).astype(BF)
        out = out + nn(active, ws_ref[cols, :])
        gbefore = nt(low, ws_ref[cols, :]) * slope
        esum_ref[0:1, cols] += jnp.sum(gbefore, axis=0, keepdims=True)
        gbefore = gbefore.astype(BF)
        back = nt(gbefore, we_ref[:, cols])
        ghid = back if ghid is None else ghid + back
        gs_ref[:, cols] += nn(low_t, active)
        ge_ref[:, cols] += nn(hidden_t, gbefore)
    out_ref[...] = out
    deposit(half, out_ref, res_ref, resrow_ref, rescol_ref)
    cot = cot_ref[...]
    gmid = cot + norm_back(ghid, normed, inverse, vec_ref[5:6, :])
    gmid_ref[...] = gmid
    gbranch = gmid.astype(BF)
    go_ref[...] += nn(att_ref[...].T, gbranch)
    gatt = nt(gbranch, weight_ref[:, 3 * features :])
    gatt_ref[...] = gatt.reshape(2 * BANDS, WT, features).astype(BF)
    sums_ref[0:1, :] += jnp.sum(gmid, axis=0, keepdims=True)
    sums_ref[1:2, :] += jnp.sum(ghid * normed, axis=0, keepdims=True)
    sums_ref[2:3, :] += jnp.sum(ghid, axis=0, keepdims=True)
    sums_ref[3:4, :] += jnp.sum(cot, axis=0, keepdims=True)

    @pl.when(step == steps - 1)
    def _():
        for d in range(shards):
            pack_ref[d, 0:deep, :] = ge_ref[d * deep : (d + 1) * deep, :].astype(BF)
            for j in range(blocks):
                at = d * deep * blocks + j * deep
                if deep * 2 % 128 == 0 and j % 2 == 0:
                    both = gs_ref[:, at : at + 2 * deep].T
                    pack_ref[d, deep : 2 * deep, j * features : (j + 1) * features] = both[
                        :deep
                    ].astype(BF)
                    pack_ref[d, deep : 2 * deep, (j + 1) * features : (j + 2) * features] = both[
                        deep:
                    ].astype(BF)
                elif deep * 2 % 128 != 0:
                    pack_ref[d, deep : 2 * deep, j * features : (j + 1) * features] = (
                        gs_ref[:, at : at + deep].T.astype(BF)
                    )
                thin = deep // blocks
                pack_ref[d, 2 * deep : 2 * deep + thin, j * features : (j + 1) * features] = go_ref[
                    d * deep + j * thin : d * deep + (j + 1) * thin, :
                ].astype(BF)


def back_kernel(
    head_size,
    xp_ref,
    hid_ref,
    qkv_ref,
    prob_ref,
    gatt_ref,
    gmid_ref,
    weight_ref,
    vec_ref,
    gtok_ref,
    grow_ref,
    gcol_ref,
    gjoint_ref,
    sums_ref,
    table_ref,
    acc_ref,
    wide_ref,
    out_ref,
):
    half = pl.program_id(1)
    step = pl.program_id(0) * pl.num_programs(1) + half
    steps = pl.num_programs(0) * pl.num_programs(1)
    features = xp_ref.shape[-1]
    scale = head_size ** (-0.5)

    @pl.when(step == 0)
    def _():
        acc_ref[...] = jnp.zeros_like(acc_ref)
        sums_ref[...] = jnp.zeros_like(sums_ref)
        table_ref[...] = jnp.zeros_like(table_ref)

    group = 256
    span = group // head_size * QL
    for w in range(2 * BANDS):
        rows = slice(w * WT, (w + 1) * WT)
        for g in range(features // group):
            feats = slice(g * group, (g + 1) * group)
            lanes = slice(g * span, (g + 1) * span)
            q = qkv_ref[w, :, g * group : (g + 1) * group]
            k = qkv_ref[w, :, features + g * group : features + (g + 1) * group]
            v = qkv_ref[w, :, 2 * features + g * group : 2 * features + (g + 1) * group]
            up = spread(gatt_ref[w, :, feats], head_size, group)
            low = prob_ref[w, :, lanes]
            probs = low.astype(F32)
            gprobs = nt(v, up)
            mean = jnp.sum(probs * gprobs, axis=0, keepdims=True)
            gscore = probs * (gprobs - mean)
            table_ref[:, lanes] += gscore
            graw = (gscore * scale).astype(BF)
            wide_ref[rows, g * group : (g + 1) * group] = per_query(graw, k, head_size)
            wide_ref[rows, features + g * group : features + (g + 1) * group] = nn(
                graw, spread(q, head_size, group)
            )
            wide_ref[rows, 2 * features + g * group : 2 * features + (g + 1) * group] = nn(low, up)
    gjoint = wide_ref[...]
    sums_ref[0:1, :] += jnp.sum(gjoint[:, :features], axis=0, keepdims=True)
    sums_ref[1:2, :] += jnp.sum(gjoint[:, 2 * features :], axis=0, keepdims=True)
    gjoint = gjoint.astype(BF)
    acc_ref[...] += nn(hid_ref[...].T, gjoint)
    ghid = nt(gjoint, weight_ref[:, : 3 * features])
    normed, inverse = norm_parts(xp_ref[...])
    sums_ref[2:3, :] += jnp.sum(ghid * normed, axis=0, keepdims=True)
    sums_ref[3:4, :] += jnp.sum(ghid, axis=0, keepdims=True)
    out_ref[...] = gmid_ref[...] + norm_back(ghid, normed, inverse, vec_ref[0:1, :])
    deposit(half, out_ref, gtok_ref, grow_ref, gcol_ref)

    @pl.when(step == steps - 1)
    def _():
        gjoint_ref[...] = acc_ref[...].astype(BF)


def shifted(block, axis, distance):
    count = lax.axis_size(axis)
    return lax.ppermute(block, axis, [((i - distance) % count, i) for i in range(count)])


def roll_in(values):
    leading = values[:, :SHIFT].astype(BF)
    arriving = shifted(leading, "row", -1)
    flank = jnp.concatenate(
        [values[:, SHIFT:, :SHIFT].astype(BF), arriving[:, :, :SHIFT]], axis=1
    ).transpose(0, 2, 1, 3)
    incoming = shifted(flank, "col", -1)
    return arriving.astype(F32), incoming.astype(F32)


def roll_out(tile, rows, cols):
    incoming = shifted(cols.astype(BF), "col", 1).transpose(0, 2, 1, 3)
    trailing = jnp.concatenate([incoming[:, -SHIFT:], rows[:, :, SHIFT:].astype(BF)], axis=2)
    arriving = shifted(trailing, "row", 1)
    tile = lax.dynamic_update_slice(tile, incoming[:, :-SHIFT].astype(F32), (0, SHIFT, 0, 0))
    return lax.dynamic_update_slice(tile, arriving.astype(F32), (0, 0, 0, 0))


def region_band(places, count):
    return jnp.where(places < count - WIN, 0, jnp.where(places < count - SHIFT, 1, 2)).astype(
        jnp.int32
    )


def whole(shape):
    return pl.BlockSpec(shape, lambda i, j: (0,) * len(shape), pipeline_mode=pl.Buffered(1))


def body(
    tokens,
    position_index,
    first_gain,
    first_shift,
    joint_weight,
    query_bias,
    value_bias,
    position_table,
    output_weight,
    output_bias,
    second_gain,
    second_shift,
    expand_weight,
    expand_bias,
    shrink_weight,
    shrink_bias,
    cotangent,
):
    images, height, breadth, features = tokens.shape
    shards = lax.axis_size("dp")
    deep = joint_weight.shape[0]
    table_heads, table_rows = position_table.shape
    heads = table_heads * shards
    head_size = features // heads
    hidden_units = expand_weight.shape[1]
    blocks = hidden_units // features
    halves = height // (WIN * BANDS)
    grid = (images, halves)
    step_rows = 2 * BANDS * WT
    total_rows = images * halves * step_rows
    windows = images * halves * 2 * BANDS
    wide = heads * QL

    small = [
        first_gain,
        first_shift,
        query_bias,
        value_bias,
        output_bias,
        second_gain,
        second_shift,
        shrink_bias,
        expand_bias,
        position_table.reshape(-1),
    ]
    small = jnp.concatenate([s.astype(BF) for s in small])
    small = jnp.pad(small, (0, -small.shape[0] % 128))[None]
    small = lax.all_gather(small, "dp", axis=0, tiled=True)
    vec = small[:, : 8 * deep].reshape(shards, 8, deep).transpose(1, 0, 2).reshape(8, features)
    vec = vec.astype(F32)
    at = 8 * deep
    ebias = small[:, at : at + blocks * deep].reshape(1, hidden_units).astype(F32)
    at += blocks * deep
    table = small[:, at : at + table_heads * table_rows].reshape(heads, table_rows)
    weight_one = lax.all_gather(
        jnp.concatenate([joint_weight, output_weight], axis=1).astype(BF), "dp", axis=0, tiled=True
    )
    thick = jnp.concatenate(
        [shrink_weight[j * deep : (j + 1) * deep] for j in range(blocks)], axis=1
    )
    weight_two = lax.all_gather(
        jnp.concatenate([expand_weight, thick], axis=0).astype(BF)[None], "dp", axis=0, tiled=True
    )

    tok_row, tok_col = roll_in(tokens)
    cot_row, cot_col = roll_in(cotangent)

    paired = position_index.reshape(WIN, WIN, WIN, WIN)
    paired = jnp.pad(paired, ((0, 0), (0, 1), (0, 0), (0, 1)), constant_values=-1)
    paired = jnp.pad(
        paired.reshape(WT, WT).T, ((0, 0), (0, QL - WT)), constant_values=-1
    ).reshape(-1)
    onehot = paired[None, :] == jnp.arange(table_rows, dtype=jnp.int32)[:, None]
    position = jnp.dot(table, onehot.astype(BF), preferred_element_type=F32)
    position = position.reshape(heads, WT, QL).transpose(1, 0, 2)
    grid_rows = height * lax.axis_size("row")
    grid_cols = breadth * lax.axis_size("col")
    row_places = jnp.stack([jnp.arange(WIN), jnp.arange(WIN) + height - WIN]).astype(jnp.int32)
    row_places = row_places + lax.axis_index("row") * height
    col_places = jnp.arange(2 * WIN, dtype=jnp.int32).reshape(2, WIN)
    col_places = col_places + lax.axis_index("col") * breadth
    row_label = region_band(row_places, grid_rows)
    col_label = jnp.pad(region_band(col_places, grid_cols), ((0, 0), (0, 1)))
    label = 3 * row_label[:, None, :, None] + col_label[None, :, None, :]
    label = label.reshape(2, 2, WT)
    label_q = jnp.pad(label, ((0, 0), (0, 0), (0, QL - WT)))
    masking = jnp.where(label[:, :, :, None] == label_q[:, :, None, :], 0.0, -100.0)
    absent = (jnp.arange(WT) % PAD == WIN)[:, None]
    masking = jnp.where(absent, FAR_BELOW, masking).astype(F32)
    bias = (position[None, None] + masking[:, :, :, None, :]).reshape(2, 2, WT, wide)

    tile_spec = pl.BlockSpec((1, height, breadth, features), lambda i, j: (i, 0, 0, 0))
    row_spec = pl.BlockSpec((1, SHIFT, breadth, features), lambda i, j: (i, 0, 0, 0))
    col_spec = pl.BlockSpec((1, SHIFT, height, features), lambda i, j: (i, 0, 0, 0))
    flat_spec = pl.BlockSpec((step_rows, features), lambda i, j: (i * halves + j, 0))

    def window_spec(last):
        return pl.BlockSpec((2 * BANDS, WT, last), lambda i, j: (i * halves + j, 0, 0))

    params = pltpu.CompilerParams(
        dimension_semantics=("arbitrary", "arbitrary"), vmem_limit_bytes=VMEM_LIMIT
    )
    shape = jax.ShapeDtypeStruct
    dense = 2 * total_rows * features * features

    xp, hidden_one, qkv, probs, attended, middle = pl.pallas_call(
        functools.partial(attend_kernel, head_size),
        grid=grid,
        in_specs=[
            tile_spec,
            row_spec,
            col_spec,
            whole((features, 4 * features)),
            whole((8, features)),
            whole((2, 2, WT, wide)),
        ],
        out_specs=[
            flat_spec,
            flat_spec,
            window_spec(3 * features),
            window_spec(wide),
            flat_spec,
            flat_spec,
        ],
        out_shape=[
            shape((total_rows, features), F32),
            shape((total_rows, features), BF),
            shape((windows, WT, 3 * features), BF),
            shape((windows, WT, wide), BF),
            shape((total_rows, features), BF),
            shape((total_rows, features), F32),
        ],
        scratch_shapes=[pltpu.VMEM((step_rows, features), F32)],
        compiler_params=params,
        cost_estimate=pl.CostEstimate(
            flops=6 * dense, bytes_accessed=40_000_000, transcendentals=windows * WT * wide
        ),
        name="attend",
    )(tokens, tok_row, tok_col, weight_one, vec, bias)

    packed_rows = 2 * deep + deep // blocks
    result, res_row, res_col, gmid, gatt, gpack, sums_two, esum = pl.pallas_call(
        mlp_kernel,
        grid=grid,
        in_specs=[
            tile_spec,
            row_spec,
            col_spec,
            flat_spec,
            flat_spec,
            whole((features, 4 * features)),
            whole((shards, 2 * deep, hidden_units)),
            whole((8, features)),
            whole((1, hidden_units)),
        ],
        out_specs=[
            tile_spec,
            row_spec,
            col_spec,
            flat_spec,
            window_spec(features),
            whole((shards, packed_rows, hidden_units)),
            whole((8, features)),
            whole((8, hidden_units)),
        ],
        out_shape=[
            shape(tokens.shape, F32),
            shape((images, SHIFT, breadth, features), F32),
            shape((images, SHIFT, height, features), F32),
            shape((total_rows, features), F32),
            shape((windows, WT, features), BF),
            shape((shards, packed_rows, hidden_units), BF),
            shape((8, features), F32),
            shape((8, hidden_units), F32),
        ],
        scratch_shapes=[
            pltpu.VMEM((step_rows, features), F32),
            pltpu.VMEM((features, hidden_units), BF),
            pltpu.VMEM((hidden_units, features), BF),
            pltpu.VMEM((features, hidden_units), F32),
            pltpu.VMEM((features, hidden_units), F32),
            pltpu.VMEM((features, features), F32),
            pltpu.VMEM((step_rows, features), F32),
        ],
        compiler_params=params,
        cost_estimate=pl.CostEstimate(
            flops=26 * dense,
            bytes_accessed=50_000_000,
            transcendentals=total_rows * hidden_units,
        ),
        name="mlp",
    )(
        cotangent,
        cot_row,
        cot_col,
        middle,
        attended,
        weight_one,
        weight_two,
        vec,
        ebias,
    )

    gtok, gtok_row, gtok_col, gjoint, sums_one, gtable = pl.pallas_call(
        functools.partial(back_kernel, head_size),
        grid=grid,
        in_specs=[
            flat_spec,
            flat_spec,
            window_spec(3 * features),
            window_spec(wide),
            window_spec(features),
            flat_spec,
            whole((features, 4 * features)),
            whole((8, features)),
        ],
        out_specs=[
            tile_spec,
            row_spec,
            col_spec,
            whole((features, 3 * features)),
            whole((8, features)),
            whole((WT, wide)),
        ],
        out_shape=[
            shape(tokens.shape, F32),
            shape((images, SHIFT, breadth, features), F32),
            shape((images, SHIFT, height, features), F32),
            shape((features, 3 * features), BF),
            shape((8, features), F32),
            shape((WT, wide), F32),
        ],
        scratch_shapes=[
            pltpu.VMEM((features, 3 * features), F32),
            pltpu.VMEM((step_rows, 3 * features), F32),
            pltpu.VMEM((step_rows, features), F32),
        ],
        compiler_params=params,
        cost_estimate=pl.CostEstimate(
            flops=12 * dense, bytes_accessed=50_000_000, transcendentals=0
        ),
        name="back",
    )(xp, hidden_one, qkv, probs, gatt, gmid, weight_one, vec)

    final = roll_out(result, res_row, res_col)
    grad_tokens = roll_out(gtok, gtok_row, gtok_col)

    gtable = gtable.reshape(WT, heads, QL).transpose(1, 0, 2).reshape(heads, WT * QL)
    grad_table = lax.dot_general(
        gtable,
        onehot.astype(F32),
        (((1,), (1,)), ((), ())),
        precision=lax.Precision.HIGHEST,
        preferred_element_type=F32,
    )

    gpack = lax.psum_scatter(gpack, "dp", scatter_dimension=0, tiled=True)[0]
    gjoint = lax.psum_scatter(gjoint, "dp", scatter_dimension=0, tiled=True)
    lines = jnp.concatenate([sums_two[:4], sums_one[:4]], axis=0)
    lines = lines.reshape(8, shards, deep).transpose(1, 0, 2).reshape(shards, -1)
    lines = jnp.concatenate(
        [lines, esum[0].reshape(shards, -1), grad_table.reshape(shards, -1)], axis=1
    )
    lines = jnp.pad(lines, ((0, 0), (0, -lines.shape[1] % 128))).astype(BF)
    lines = lax.psum_scatter(lines, "dp", scatter_dimension=0, tiled=True)
    gpack, gjoint, lines = lax.psum((gpack, gjoint, lines), ("row", "col"))
    gpack, gjoint = gpack.astype(F32), gjoint.astype(F32)
    lines = lines[0].astype(F32)
    thin = deep // blocks
    grad_expand = gpack[:deep]
    grad_shrink = jnp.concatenate(
        [gpack[deep : 2 * deep, j * features : (j + 1) * features] for j in range(blocks)], axis=0
    )
    grad_output = jnp.concatenate(
        [gpack[2 * deep :, j * features : (j + 1) * features] for j in range(blocks)], axis=0
    )
    eight = lines[: 8 * deep].reshape(8, deep)
    at = 8 * deep
    grad_expand_bias = lines[at : at + blocks * deep]
    at += blocks * deep
    grad_position = lines[at : at + table_heads * table_rows].reshape(table_heads, table_rows)
    return (
        final,
        grad_tokens,
        eight[6],
        eight[7],
        gjoint,
        eight[4],
        eight[5],
        grad_position,
        grad_output,
        eight[0],
        eight[1],
        eight[2],
        grad_expand,
        grad_expand_bias,
        grad_shrink,
        eight[3],
    )


def solution(mesh):
    tile = P("dp", "row", "col", None)
    flat = P("dp")
    wide = P("dp", None)
    return jax.shard_map(
        body,
        mesh=mesh,
        in_specs=(
            tile,
            P(),
            flat,
            flat,
            wide,
            flat,
            flat,
            wide,
            wide,
            flat,
            flat,
            flat,
            wide,
            flat,
            wide,
            flat,
            tile,
        ),
        out_specs=(
            tile,
            tile,
            flat,
            flat,
            wide,
            flat,
            flat,
            wide,
            wide,
            flat,
            flat,
            flat,
            wide,
            flat,
            wide,
            flat,
        ),
        check_vma=False,
    )
```

```python
import functools

import jax
import jax.numpy as jnp
from jax import lax
from jax.experimental import pallas as pl
from jax.experimental.pallas import tpu as pltpu
from jax.sharding import PartitionSpec as P


WIN = 7
SHIFT = 3
PAD = 8
WT = WIN * PAD
QL = 64
EPSILON = 1e-05
ROOT_HALF = 0.7071067811865476
NORMAL_PEAK = 0.3989422804014327
FAR_BELOW = -1000000000.0
BF = jnp.bfloat16
F32 = jnp.float32
BANDS = 4
LINES = 16
VMEM_LIMIT = 60 * 1024 * 1024


def nn(a, b):
    return lax.dot_general(a, b, (((1,), (0,)), ((), ())), preferred_element_type=F32)


def nt(a, b):
    return lax.dot_general(a, b, (((1,), (1,)), ((), ())), preferred_element_type=F32)


def tn(a, b):
    return lax.dot_general(a, b, (((0,), (0,)), ((), ())), preferred_element_type=F32)


def norm_parts(values):
    center = values - jnp.mean(values, axis=-1, keepdims=True)
    inverse = lax.rsqrt(jnp.mean(center * center, axis=-1, keepdims=True) + EPSILON)
    return center * inverse, inverse


def norm_back(upper, normed, inverse, scaling):
    scaled = upper * scaling
    return inverse * (
        scaled
        - jnp.mean(scaled, axis=-1, keepdims=True)
        - normed * jnp.mean(scaled * normed, axis=-1, keepdims=True)
    )


def row_of(band, col):
    return ((2 * band + col // WIN) * WIN + col % WIN) * PAD


def extract(half, tile_ref, row_ref, col_ref, out_ref):
    _, breadth, height, features = tile_ref.shape
    zero = jnp.zeros((1, features), F32)
    for band in range(BANDS):
        for col in range(breadth):
            at = row_of(band, col)
            out_ref[at + WIN : at + PAD, :] = zero
    for place in range(height // (BANDS * WIN)):

        @pl.when(half == place)
        def _():
            for col in range(breadth):
                local = col < breadth - SHIFT
                for band in range(BANDS):
                    at = row_of(band, col)
                    start = (place * BANDS + band) * WIN + SHIFT
                    count = min(WIN, height - start)
                    rows = slice(start, start + count)
                    out_ref[at : at + count, :] = (
                        tile_ref[0, col + SHIFT, rows, :]
                        if local
                        else col_ref[0, col + SHIFT - breadth, rows, :]
                    )
                    for j in range(WIN - count):
                        out_ref[at + count + j : at + count + j + 1, :] = row_ref[
                            0, j, col : col + 1, :
                        ]


def deposit(half, src_ref, tile_ref, row_ref, col_ref):
    _, breadth, height, _ = tile_ref.shape
    for place in range(height // (BANDS * WIN)):

        @pl.when(half == place)
        def _():
            for col in range(breadth):
                local = col < breadth - SHIFT
                for band in range(BANDS):
                    at = row_of(band, col)
                    start = (place * BANDS + band) * WIN + SHIFT
                    count = min(WIN, height - start)
                    rows = slice(start, start + count)
                    if local:
                        tile_ref[0, col + SHIFT, rows, :] = src_ref[at : at + count, :]
                    else:
                        col_ref[0, col + SHIFT - breadth, rows, :] = src_ref[at : at + count, :]
                    for j in range(WIN - count):
                        row_ref[0, j, col : col + 1, :] = src_ref[
                            at + count + j : at + count + j + 1, :
                        ]


def spread(rows, head_size, lanes):
    heads = lanes // head_size
    rows = jnp.concatenate([rows, jnp.zeros((QL - WT, lanes), rows.dtype)], axis=0)
    lane = lax.broadcasted_iota(jnp.int32, (QL, lanes), 1) // head_size
    zero = jnp.zeros_like(rows)
    return jnp.concatenate([jnp.where(lane == h, rows, zero) for h in range(heads)], axis=0)


def collapse(wide, head_size, lanes):
    heads = lanes // head_size
    lane = lax.broadcasted_iota(jnp.int32, (WT, lanes), 1) // head_size
    out = wide[0:WT]
    for h in range(1, heads):
        out = jnp.where(lane == h, wide[h * QL : h * QL + WT], out)
    return out


def per_query(scores_low, feats, head_size):
    features = feats.shape[1]
    quad = 128 // head_size
    parts = []
    for g in range(features // 128):
        block = scores_low[:, g * quad * QL : (g + 1) * quad * QL]
        wide = tn(block, feats[:, g * 128 : (g + 1) * 128])
        parts.append(collapse(wide, head_size, 128))
    return jnp.concatenate(parts, axis=1)


def attend_kernel(
    head_size,
    tile_ref,
    row_ref,
    col_ref,
    weight_ref,
    vec_ref,
    bias_ref,
    xp_ref,
    hid_ref,
    qkv_ref,
    prob_ref,
    att_ref,
    mid_ref,
    wide_ref,
):
    half = pl.program_id(1)
    features = tile_ref.shape[-1]
    extract(half, tile_ref, row_ref, col_ref, xp_ref)
    normed, _ = norm_parts(xp_ref[...])
    hidden = (normed * vec_ref[0:1, :] + vec_ref[1:2, :]).astype(BF)
    hid_ref[...] = hidden
    scale = head_size ** (-0.5)
    for part in range(3):
        got = nn(hidden, weight_ref[:, part * features : (part + 1) * features])
        if part == 0:
            got = got + vec_ref[2:3, :]
        if part == 2:
            got = got + vec_ref[3:4, :]
        qkv_ref[:, :, part * features : (part + 1) * features] = got.reshape(
            2 * BANDS, WT, features
        ).astype(BF)

    group = 256
    span = group // head_size * QL
    for w in range(2 * BANDS):
        kind = w % 2
        edge = jnp.where(half == 0, 0, 1) if w // 2 == BANDS - 1 else 0
        for g in range(features // group):
            q = qkv_ref[w, :, g * group : (g + 1) * group]
            k = qkv_ref[w, :, features + g * group : features + (g + 1) * group]
            raw = nt(k, spread(q, head_size, group))
            score = raw * scale + bias_ref[edge, kind, :, g * span : (g + 1) * span]
            highest = jnp.max(score, axis=0, keepdims=True)
            grown = jnp.exp(score - highest)
            total = jnp.sum(grown, axis=0, keepdims=True)
            probs = (grown * (1.0 / total)).astype(BF)
            prob_ref[w, :, g * span : (g + 1) * span] = probs
            v = qkv_ref[w, :, 2 * features + g * group : 2 * features + (g + 1) * group]
            wide_ref[w * WT : (w + 1) * WT, g * group : (g + 1) * group] = per_query(
                probs, v, head_size
            )
    attended = wide_ref[...].astype(BF)
    att_ref[...] = attended
    branch = nn(attended, weight_ref[:, 3 * features :]) + vec_ref[4:5, :]
    mid_ref[...] = xp_ref[...] + branch


def mlp_kernel(
    tile_ref,
    row_ref,
    col_ref,
    mid_ref,
    att_ref,
    weight_ref,
    packed_ref,
    vec_ref,
    ebias_ref,
    res_ref,
    resrow_ref,
    rescol_ref,
    gmid_ref,
    gatt_ref,
    pack_ref,
    cot_ref,
    we_ref,
    ws_ref,
    ge_ref,
    gs_ref,
    go_ref,
    out_ref,
    sums_ref,
    esum_ref,
):
    half = pl.program_id(1)
    step = pl.program_id(0) * pl.num_programs(1) + half
    steps = pl.num_programs(0) * pl.num_programs(1)
    features = tile_ref.shape[-1]
    hidden_units = we_ref.shape[1]
    shards = pack_ref.shape[0]
    deep = features // shards
    blocks = hidden_units // features

    @pl.when(step == 0)
    def _():
        for d in range(shards):
            we_ref[d * deep : (d + 1) * deep, :] = packed_ref[d, 0:deep, :]
            for j in range(blocks):
                at = d * deep * blocks + j * deep
                ws_ref[at : at + deep, :] = packed_ref[
                    d, deep : 2 * deep, j * features : (j + 1) * features
                ]
        ge_ref[...] = jnp.zeros_like(ge_ref)
        gs_ref[...] = jnp.zeros_like(gs_ref)
        go_ref[...] = jnp.zeros_like(go_ref)
        sums_ref[...] = jnp.zeros_like(sums_ref)
        esum_ref[...] = jnp.zeros_like(esum_ref)

    extract(half, tile_ref, row_ref, col_ref, cot_ref)
    mid = mid_ref[...]
    normed, inverse = norm_parts(mid)
    hidden = (normed * vec_ref[5:6, :] + vec_ref[6:7, :]).astype(BF)
    hidden_t = hidden.T
    low = cot_ref[...].astype(BF)
    low_t = low.T
    out = mid + vec_ref[7:8, :]
    ghid = None
    chunk = features
    for c in range(hidden_units // chunk):
        cols = slice(c * chunk, (c + 1) * chunk)
        before = nn(hidden, we_ref[:, cols]) + ebias_ref[0:1, cols]
        phi = 0.5 * (1.0 + lax.erf(before * ROOT_HALF))
        slope = phi + before * (NORMAL_PEAK * jnp.exp(-0.5 * before * before))
        active = (before * phi).astype(BF)
        out = out + nn(active, ws_ref[cols, :])
        gbefore = nt(low, ws_ref[cols, :]) * slope
        esum_ref[0:1, cols] += jnp.sum(gbefore, axis=0, keepdims=True)
        gbefore = gbefore.astype(BF)
        back = nt(gbefore, we_ref[:, cols])
        ghid = back if ghid is None else ghid + back
        gs_ref[:, cols] += nn(low_t, active)
        ge_ref[:, cols] += nn(hidden_t, gbefore)
    out_ref[...] = out
    deposit(half, out_ref, res_ref, resrow_ref, rescol_ref)
    cot = cot_ref[...]
    gmid = cot + norm_back(ghid, normed, inverse, vec_ref[5:6, :])
    gmid_ref[...] = gmid
    gbranch = gmid.astype(BF)
    go_ref[...] += nn(att_ref[...].T, gbranch)
    gatt = nt(gbranch, weight_ref[:, 3 * features :])
    gatt_ref[...] = gatt.reshape(2 * BANDS, WT, features).astype(BF)
    sums_ref[0:1, :] += jnp.sum(gmid, axis=0, keepdims=True)
    sums_ref[1:2, :] += jnp.sum(ghid * normed, axis=0, keepdims=True)
    sums_ref[2:3, :] += jnp.sum(ghid, axis=0, keepdims=True)
    sums_ref[3:4, :] += jnp.sum(cot, axis=0, keepdims=True)

    @pl.when(step == steps - 1)
    def _():
        even = hidden_units // shards
        base = 2 * deep + LINES
        pack_ref[:, 2 * deep : base, :] = jnp.zeros((shards, LINES, hidden_units), BF)
        for d in range(shards):
            pack_ref[d, 2 * deep : base, 0:deep] = sums_ref[:, d * deep : (d + 1) * deep].astype(BF)
            pack_ref[d, 2 * deep : base, features : features + even] = esum_ref[
                :, d * even : (d + 1) * even
            ].astype(BF)
            pack_ref[d, 0:deep, :] = ge_ref[d * deep : (d + 1) * deep, :].astype(BF)
            for j in range(blocks):
                at = d * deep * blocks + j * deep
                if deep * 2 % 128 == 0 and j % 2 == 0:
                    both = gs_ref[:, at : at + 2 * deep].T
                    pack_ref[d, deep : 2 * deep, j * features : (j + 1) * features] = both[
                        :deep
                    ].astype(BF)
                    pack_ref[d, deep : 2 * deep, (j + 1) * features : (j + 2) * features] = both[
                        deep:
                    ].astype(BF)
                elif deep * 2 % 128 != 0:
                    pack_ref[d, deep : 2 * deep, j * features : (j + 1) * features] = (
                        gs_ref[:, at : at + deep].T.astype(BF)
                    )
                thin = deep // blocks
                pack_ref[d, base : base + thin, j * features : (j + 1) * features] = go_ref[
                    d * deep + j * thin : d * deep + (j + 1) * thin, :
                ].astype(BF)


def back_kernel(
    head_size,
    hid_ref,
    qkv_ref,
    prob_ref,
    gatt_ref,
    weight_ref,
    vec_ref,
    gact_ref,
    pack_ref,
    acc_ref,
    wide_ref,
    sums_ref,
    table_ref,
):
    half = pl.program_id(1)
    step = pl.program_id(0) * pl.num_programs(1) + half
    steps = pl.num_programs(0) * pl.num_programs(1)
    features = hid_ref.shape[-1]
    scale = head_size ** (-0.5)

    @pl.when(step == 0)
    def _():
        acc_ref[...] = jnp.zeros_like(acc_ref)
        sums_ref[...] = jnp.zeros_like(sums_ref)
        table_ref[...] = jnp.zeros_like(table_ref)

    group = 256
    span = group // head_size * QL
    for w in range(2 * BANDS):
        rows = slice(w * WT, (w + 1) * WT)
        for g in range(features // group):
            feats = slice(g * group, (g + 1) * group)
            lanes = slice(g * span, (g + 1) * span)
            q = qkv_ref[w, :, g * group : (g + 1) * group]
            k = qkv_ref[w, :, features + g * group : features + (g + 1) * group]
            v = qkv_ref[w, :, 2 * features + g * group : 2 * features + (g + 1) * group]
            up = spread(gatt_ref[w, :, feats], head_size, group)
            low = prob_ref[w, :, lanes]
            probs = low.astype(F32)
            gprobs = nt(v, up)
            mean = jnp.sum(probs * gprobs, axis=0, keepdims=True)
            gscore = probs * (gprobs - mean)
            table_ref[0:WT, lanes] += gscore
            graw = (gscore * scale).astype(BF)
            wide_ref[rows, g * group : (g + 1) * group] = per_query(graw, k, head_size)
            wide_ref[rows, features + g * group : features + (g + 1) * group] = nn(
                graw, spread(q, head_size, group)
            )
            wide_ref[rows, 2 * features + g * group : 2 * features + (g + 1) * group] = nn(low, up)
    gjoint = wide_ref[...]
    sums_ref[...] += jnp.sum(gjoint, axis=0, keepdims=True)
    gjoint = gjoint.astype(BF)
    gact_ref[...] = gjoint
    acc_ref[...] += nn(hid_ref[...].T, gjoint)

    @pl.when(step == steps - 1)
    def _():
        shards = pack_ref.shape[0]
        deep = features // shards
        lanes = table_ref.shape[1] // shards
        total = sums_ref[0:1, :]
        by_acc = jnp.zeros((features, 128), F32)
        by_sum = jnp.zeros((features, 128), F32)
        for c in range(3 * features // 128):
            cols = slice(c * 128, (c + 1) * 128)
            weight = weight_ref[:, cols].astype(F32)
            by_acc = by_acc + weight * acc_ref[:, cols]
            by_sum = by_sum + weight * total[:, cols]
        by_acc = jnp.sum(by_acc.T, axis=0, keepdims=True)
        gshift = jnp.sum(by_sum.T, axis=0, keepdims=True)
        ggain = (by_acc - vec_ref[1:2, :] * gshift) / vec_ref[0:1, :]
        lines = jnp.concatenate(
            [
                ggain,
                gshift,
                total[:, :features],
                total[:, 2 * features :],
                jnp.zeros((LINES - 4, features), F32),
            ],
            axis=0,
        )
        for d in range(shards):
            pack_ref[d, 0:deep, :] = acc_ref[d * deep : (d + 1) * deep, :].astype(BF)
            pack_ref[d, deep : deep + LINES, 4 * lanes + deep :] = jnp.zeros(
                (LINES, 3 * features - 4 * lanes - deep), BF
            )
            for j in range(4):
                pack_ref[d, deep : deep + LINES, j * lanes : (j + 1) * lanes] = table_ref[
                    j * LINES : (j + 1) * LINES, d * lanes : (d + 1) * lanes
                ].astype(BF)
            pack_ref[d, deep : deep + LINES, 4 * lanes : 4 * lanes + deep] = lines[
                :, d * deep : (d + 1) * deep
            ].astype(BF)


def close_kernel(
    gact_ref, xp_ref, gmid_ref, weight_ref, vec_ref, gtok_ref, grow_ref, gcol_ref, out_ref
):
    features = xp_ref.shape[-1]
    ghid = nt(gact_ref[...], weight_ref[:, : 3 * features])
    normed, inverse = norm_parts(xp_ref[...])
    out_ref[...] = gmid_ref[...] + norm_back(ghid, normed, inverse, vec_ref[0:1, :])
    deposit(pl.program_id(1), out_ref, gtok_ref, grow_ref, gcol_ref)


def patch_kernel(tile_ref, col_ref, row_ref, out_ref, flank_ref, top_ref, sems):
    images, breadth, _, _ = tile_ref.shape
    fetch = pltpu.make_async_copy(out_ref.at[:, SHIFT:, 0:PAD], top_ref, sems.at[0])
    fetch.start()
    flank_ref[...] = col_ref[...].astype(F32)
    for i in range(images):
        for c in range(SHIFT):
            for j in range(SHIFT):
                flank_ref[i, c, j : j + 1, :] = row_ref[i, j, c : c + 1, :]
    side = pltpu.make_async_copy(flank_ref, out_ref.at[:, 0:SHIFT], sems.at[1])
    side.start()
    fetch.wait()
    for i in range(images):
        for c in range(breadth - SHIFT):
            for j in range(SHIFT):
                top_ref[i, c, j : j + 1, :] = row_ref[i, j, c + SHIFT : c + SHIFT + 1, :]
    back = pltpu.make_async_copy(top_ref, out_ref.at[:, SHIFT:, 0:PAD], sems.at[2])
    back.start()
    side.wait()
    back.wait()


def shifted(block, axis, distance):
    count = lax.axis_size(axis)
    return lax.ppermute(block, axis, [((i - distance) % count, i) for i in range(count)])


def slanted(block, distance):
    rows, cols = lax.axis_size("row"), lax.axis_size("col")
    route = [
        (((r - distance) % rows) * cols + (c - distance) % cols, r * cols + c)
        for r in range(rows)
        for c in range(cols)
    ]
    return lax.ppermute(block, ("row", "col"), route)


def roll_in(values):
    cols = shifted(values[:, :SHIFT].astype(BF), "col", -1)
    top = values[:, :, :SHIFT].astype(BF).transpose(0, 2, 1, 3)
    rows = shifted(top[:, :, SHIFT:], "row", -1)
    corner = slanted(top[:, :, :SHIFT], -1)
    return jnp.concatenate([rows, corner], axis=2).astype(F32), cols.astype(F32)


def roll_out(tile, rows, cols):
    images, breadth, height, features = tile.shape
    rows = rows.astype(BF)
    flank = shifted(cols.astype(BF), "col", 1)
    top = shifted(rows[:, :, : breadth - SHIFT], "row", 1)
    corner = slanted(rows[:, :, breadth - SHIFT :], 1)
    top = jnp.concatenate([corner, top], axis=2).astype(F32)
    vmem = pl.BlockSpec(memory_space=pltpu.VMEM)
    return pl.pallas_call(
        patch_kernel,
        in_specs=[pl.BlockSpec(memory_space=pl.ANY), vmem, vmem],
        out_specs=pl.BlockSpec(memory_space=pl.ANY),
        out_shape=jax.ShapeDtypeStruct(tile.shape, F32),
        scratch_shapes=[
            pltpu.VMEM((images, SHIFT, height, features), F32),
            pltpu.VMEM((images, breadth - SHIFT, PAD, features), F32),
            pltpu.SemaphoreType.DMA((3,)),
        ],
        input_output_aliases={0: 0},
        compiler_params=pltpu.CompilerParams(vmem_limit_bytes=24 * 1024 * 1024),
        cost_estimate=pl.CostEstimate(flops=0, bytes_accessed=4_000_000, transcendentals=0),
        name="patch",
    )(tile, flank, top)


def over_tiles(block):
    def added(part, axis):
        total = part.astype(F32)
        for step in range(1, lax.axis_size(axis)):
            total = total + shifted(part, axis, step).astype(F32)
        return total

    cut = block.shape[-1] // 2
    first = added(added(block[:, :cut], "row").astype(BF), "col")
    second = added(added(block[:, cut:], "col").astype(BF), "row")
    return jnp.concatenate([first, second], axis=1)


def region_band(places, count):
    return jnp.where(places < count - WIN, 0, jnp.where(places < count - SHIFT, 1, 2)).astype(
        jnp.int32
    )


def whole(shape):
    return pl.BlockSpec(shape, lambda i, j: (0,) * len(shape), pipeline_mode=pl.Buffered(1))


def body(
    tokens,
    position_index,
    first_gain,
    first_shift,
    joint_weight,
    query_bias,
    value_bias,
    position_table,
    output_weight,
    output_bias,
    second_gain,
    second_shift,
    expand_weight,
    expand_bias,
    shrink_weight,
    shrink_bias,
    cotangent,
):
    images, height, breadth, features = tokens.shape
    shards = lax.axis_size("dp")
    deep = joint_weight.shape[0]
    table_heads, table_rows = position_table.shape
    heads = table_heads * shards
    head_size = features // heads
    hidden_units = expand_weight.shape[1]
    blocks = hidden_units // features
    halves = height // (WIN * BANDS)
    grid = (images, halves)
    step_rows = 2 * BANDS * WT
    total_rows = images * halves * step_rows
    windows = images * halves * 2 * BANDS
    wide = heads * QL

    small = [
        first_gain,
        first_shift,
        query_bias,
        value_bias,
        output_bias,
        second_gain,
        second_shift,
        shrink_bias,
        expand_bias,
        position_table.reshape(-1),
    ]
    small = jnp.concatenate([s.astype(BF) for s in small])
    small = jnp.pad(small, (0, -small.shape[0] % 128))[None]
    small = lax.all_gather(small, "dp", axis=0, tiled=True)
    vec = small[:, : 8 * deep].reshape(shards, 8, deep).transpose(1, 0, 2).reshape(8, features)
    vec = vec.astype(F32)
    at = 8 * deep
    ebias = small[:, at : at + blocks * deep].reshape(1, hidden_units).astype(F32)
    at += blocks * deep
    table = small[:, at : at + table_heads * table_rows].reshape(heads, table_rows)
    weight_one = lax.all_gather(
        jnp.concatenate([joint_weight, output_weight], axis=1).astype(BF), "dp", axis=0, tiled=True
    )
    thick = jnp.concatenate(
        [shrink_weight[j * deep : (j + 1) * deep] for j in range(blocks)], axis=1
    )
    weight_two = lax.all_gather(
        jnp.concatenate([expand_weight, thick], axis=0).astype(BF)[None], "dp", axis=0, tiled=True
    )

    tokens, cotangent = tokens.transpose(0, 2, 1, 3), cotangent.transpose(0, 2, 1, 3)
    tok_row, tok_col = roll_in(tokens)
    cot_row, cot_col = roll_in(cotangent)

    paired = position_index.reshape(WIN, WIN, WIN, WIN)
    paired = paired.transpose(1, 0, 3, 2)
    paired = jnp.pad(paired, ((0, 0), (0, 1), (0, 0), (0, 1)), constant_values=-1)
    paired = jnp.pad(
        paired.reshape(WT, WT).T, ((0, 0), (0, QL - WT)), constant_values=-1
    ).reshape(-1)
    onehot = paired[None, :] == jnp.arange(table_rows, dtype=jnp.int32)[:, None]
    position = jnp.dot(table, onehot.astype(BF), preferred_element_type=F32)
    position = position.reshape(heads, WT, QL).transpose(1, 0, 2)
    grid_rows = height * lax.axis_size("row")
    grid_cols = breadth * lax.axis_size("col")
    row_places = jnp.stack([jnp.arange(WIN), jnp.arange(WIN) + height - WIN]).astype(jnp.int32)
    row_places = row_places + lax.axis_index("row") * height
    col_places = jnp.arange(2 * WIN, dtype=jnp.int32).reshape(2, WIN)
    col_places = col_places + lax.axis_index("col") * breadth
    row_label = jnp.pad(region_band(row_places, grid_rows), ((0, 0), (0, 1)))
    col_label = region_band(col_places, grid_cols)
    label = 3 * row_label[:, None, None, :] + col_label[None, :, :, None]
    label = label.reshape(2, 2, WT)
    label_q = jnp.pad(label, ((0, 0), (0, 0), (0, QL - WT)))
    masking = jnp.where(label[:, :, :, None] == label_q[:, :, None, :], 0.0, -100.0)
    absent = (jnp.arange(WT) % PAD == WIN)[:, None]
    masking = jnp.where(absent, FAR_BELOW, masking).astype(F32)
    bias = (position[None, None] + masking[:, :, :, None, :]).reshape(2, 2, WT, wide)

    tile_spec = pl.BlockSpec((1, breadth, height, features), lambda i, j: (i, 0, 0, 0))
    row_spec = pl.BlockSpec((1, SHIFT, breadth, features), lambda i, j: (i, 0, 0, 0))
    col_spec = pl.BlockSpec((1, SHIFT, height, features), lambda i, j: (i, 0, 0, 0))
    flat_spec = pl.BlockSpec((step_rows, features), lambda i, j: (i * halves + j, 0))

    joint_spec = pl.BlockSpec((step_rows, 3 * features), lambda i, j: (i * halves + j, 0))

    def window_spec(last):
        return pl.BlockSpec((2 * BANDS, WT, last), lambda i, j: (i * halves + j, 0, 0))

    params = pltpu.CompilerParams(
        dimension_semantics=("arbitrary", "arbitrary"), vmem_limit_bytes=VMEM_LIMIT
    )
    shape = jax.ShapeDtypeStruct
    dense = 2 * total_rows * features * features

    xp, hidden_one, qkv, probs, attended, middle = pl.pallas_call(
        functools.partial(attend_kernel, head_size),
        grid=grid,
        in_specs=[
            tile_spec,
            row_spec,
            col_spec,
            whole((features, 4 * features)),
            whole((8, features)),
            whole((2, 2, WT, wide)),
        ],
        out_specs=[
            flat_spec,
            flat_spec,
            window_spec(3 * features),
            window_spec(wide),
            flat_spec,
            flat_spec,
        ],
        out_shape=[
            shape((total_rows, features), F32),
            shape((total_rows, features), BF),
            shape((windows, WT, 3 * features), BF),
            shape((windows, WT, wide), BF),
            shape((total_rows, features), BF),
            shape((total_rows, features), F32),
        ],
        scratch_shapes=[pltpu.VMEM((step_rows, features), F32)],
        compiler_params=params,
        cost_estimate=pl.CostEstimate(
            flops=6 * dense, bytes_accessed=40_000_000, transcendentals=windows * WT * wide
        ),
        name="attend",
    )(tokens, tok_row, tok_col, weight_one, vec, bias)

    packed_rows = 2 * deep + deep // blocks + LINES
    result, res_row, res_col, gmid, gatt, pack_two = pl.pallas_call(
        mlp_kernel,
        grid=grid,
        in_specs=[
            tile_spec,
            row_spec,
            col_spec,
            flat_spec,
            flat_spec,
            whole((features, 4 * features)),
            whole((shards, 2 * deep, hidden_units)),
            whole((8, features)),
            whole((1, hidden_units)),
        ],
        out_specs=[
            tile_spec,
            row_spec,
            col_spec,
            flat_spec,
            window_spec(features),
            whole((shards, packed_rows, hidden_units)),
        ],
        out_shape=[
            shape(tokens.shape, F32),
            shape((images, SHIFT, breadth, features), F32),
            shape((images, SHIFT, height, features), F32),
            shape((total_rows, features), F32),
            shape((windows, WT, features), BF),
            shape((shards, packed_rows, hidden_units), BF),
        ],
        scratch_shapes=[
            pltpu.VMEM((step_rows, features), F32),
            pltpu.VMEM((features, hidden_units), BF),
            pltpu.VMEM((hidden_units, features), BF),
            pltpu.VMEM((features, hidden_units), F32),
            pltpu.VMEM((features, hidden_units), F32),
            pltpu.VMEM((features, features), F32),
            pltpu.VMEM((step_rows, features), F32),
            pltpu.VMEM((LINES, features), F32),
            pltpu.VMEM((LINES, hidden_units), F32),
        ],
        compiler_params=params,
        cost_estimate=pl.CostEstimate(
            flops=26 * dense,
            bytes_accessed=50_000_000,
            transcendentals=total_rows * hidden_units,
        ),
        name="mlp",
    )(
        cotangent,
        cot_row,
        cot_col,
        middle,
        attended,
        weight_one,
        weight_two,
        vec,
        ebias,
    )

    pack_two = lax.psum_scatter(pack_two, "dp", scatter_dimension=0, tiled=True)[0]
    final = roll_out(result, res_row, res_col)

    gact, pack_one = pl.pallas_call(
        functools.partial(back_kernel, head_size),
        grid=grid,
        in_specs=[
            flat_spec,
            window_spec(3 * features),
            window_spec(wide),
            window_spec(features),
            whole((features, 4 * features)),
            whole((8, features)),
        ],
        out_specs=[joint_spec, whole((shards, deep + LINES, 3 * features))],
        out_shape=[
            shape((total_rows, 3 * features), BF),
            shape((shards, deep + LINES, 3 * features), BF),
        ],
        scratch_shapes=[
            pltpu.VMEM((features, 3 * features), F32),
            pltpu.VMEM((step_rows, 3 * features), F32),
            pltpu.VMEM((1, 3 * features), F32),
            pltpu.VMEM((4 * LINES, wide), F32),
        ],
        compiler_params=params,
        cost_estimate=pl.CostEstimate(
            flops=18 * dense, bytes_accessed=50_000_000, transcendentals=0
        ),
        name="back",
    )(hidden_one, qkv, probs, gatt, weight_one, vec)

    pack_one = lax.psum_scatter(pack_one, "dp", scatter_dimension=0, tiled=True)[0]

    gtok, gtok_row, gtok_col = pl.pallas_call(
        close_kernel,
        grid=grid,
        in_specs=[
            joint_spec,
            flat_spec,
            flat_spec,
            whole((features, 4 * features)),
            whole((8, features)),
        ],
        out_specs=[tile_spec, row_spec, col_spec],
        out_shape=[
            shape(tokens.shape, F32),
            shape((images, SHIFT, breadth, features), F32),
            shape((images, SHIFT, height, features), F32),
        ],
        scratch_shapes=[pltpu.VMEM((step_rows, features), F32)],
        compiler_params=params,
        cost_estimate=pl.CostEstimate(
            flops=6 * dense, bytes_accessed=30_000_000, transcendentals=0
        ),
        name="close",
    )(gact, xp, gmid, weight_one, vec)
    grad_tokens = roll_out(gtok, gtok_row, gtok_col)

    pack_two = over_tiles(pack_two)
    pack_one = over_tiles(pack_one)
    grad_expand = pack_two[:deep]
    grad_shrink = jnp.concatenate(
        [pack_two[deep : 2 * deep, j * features : (j + 1) * features] for j in range(blocks)],
        axis=0,
    )
    base = 2 * deep + LINES
    grad_output = jnp.concatenate(
        [pack_two[base:, j * features : (j + 1) * features] for j in range(blocks)], axis=0
    )
    lines_two = pack_two[2 * deep : base, :deep]
    grad_expand_bias = pack_two[2 * deep, features : features + blocks * deep]
    grad_joint = pack_one[:deep]
    lanes = table_heads * QL
    lines_one = pack_one[deep:, 4 * lanes : 4 * lanes + deep]
    gtable = jnp.concatenate(
        [pack_one[deep:, j * lanes : (j + 1) * lanes] for j in range(4)], axis=0
    )[:WT]
    gtable = gtable.reshape(WT, table_heads, QL).transpose(1, 0, 2).reshape(table_heads, WT * QL)
    grad_position = lax.dot_general(
        gtable,
        onehot.astype(F32),
        (((1,), (1,)), ((), ())),
        precision=lax.Precision.HIGHEST,
        preferred_element_type=F32,
    )
    final, grad_tokens = final.transpose(0, 2, 1, 3), grad_tokens.transpose(0, 2, 1, 3)
    return (
        final,
        grad_tokens,
        lines_one[0],
        lines_one[1],
        grad_joint,
        lines_one[2],
        lines_one[3],
        grad_position,
        grad_output,
        lines_two[0],
        lines_two[1],
        lines_two[2],
        grad_expand,
        grad_expand_bias,
        grad_shrink,
        lines_two[3],
    )


def solution(mesh):
    tile = P("dp", "row", "col", None)
    flat = P("dp")
    wide = P("dp", None)

    return jax.shard_map(
        body,
        mesh=mesh,
        in_specs=(
            tile,
            P(),
            flat,
            flat,
            wide,
            flat,
            flat,
            wide,
            wide,
            flat,
            flat,
            flat,
            wide,
            flat,
            wide,
            flat,
            tile,
        ),
        out_specs=(
            tile,
            tile,
            flat,
            flat,
            wide,
            flat,
            flat,
            wide,
            wide,
            flat,
            flat,
            flat,
            wide,
            flat,
            wide,
            flat,
        ),
        check_vma=False,
    )
```

```python
import functools

import jax
import jax.numpy as jnp
from jax import lax
from jax.experimental import pallas as pl
from jax.experimental.pallas import tpu as pltpu
from jax.sharding import PartitionSpec as P


WIN = 7
SHIFT = 3
PAD = 8
WT = WIN * PAD
QL = 64
EPSILON = 1e-05
ROOT_HALF = 0.7071067811865476
NORMAL_PEAK = 0.3989422804014327
FAR_BELOW = -1000000000.0
BF = jnp.bfloat16
F32 = jnp.float32
BANDS = 4
LINES = 16
VMEM_LIMIT = 60 * 1024 * 1024


def nn(a, b):
    return lax.dot_general(a, b, (((1,), (0,)), ((), ())), preferred_element_type=F32)


def nt(a, b):
    return lax.dot_general(a, b, (((1,), (1,)), ((), ())), preferred_element_type=F32)


def tn(a, b):
    return lax.dot_general(a, b, (((0,), (0,)), ((), ())), preferred_element_type=F32)


def norm_parts(values):
    center = values - jnp.mean(values, axis=-1, keepdims=True)
    inverse = lax.rsqrt(jnp.mean(center * center, axis=-1, keepdims=True) + EPSILON)
    return center * inverse, inverse


def norm_back(upper, normed, inverse, scaling):
    scaled = upper * scaling
    return inverse * (
        scaled
        - jnp.mean(scaled, axis=-1, keepdims=True)
        - normed * jnp.mean(scaled * normed, axis=-1, keepdims=True)
    )


def row_of(band, col):
    return ((2 * band + col // WIN) * WIN + col % WIN) * PAD


def widen(half, row_ref, corner_ref, col_ref, rows_ref, cols_ref):
    @pl.when(half == 0)
    def _():
        own = row_ref.shape[2]
        rows_ref[:, 0:own, :] = row_ref[0].astype(F32)
        rows_ref[:, own : own + SHIFT, :] = corner_ref[0].astype(F32)
        cols_ref[...] = col_ref[0].astype(F32)


def extract(half, tile_ref, rows_ref, cols_ref, out_ref):
    _, breadth, height, features = tile_ref.shape
    zero = jnp.zeros((1, features), F32)
    for band in range(BANDS):
        for col in range(breadth):
            at = row_of(band, col)
            out_ref[at + WIN : at + PAD, :] = zero
    for place in range(height // (BANDS * WIN)):

        @pl.when(half == place)
        def _():
            for col in range(breadth):
                local = col < breadth - SHIFT
                for band in range(BANDS):
                    at = row_of(band, col)
                    start = (place * BANDS + band) * WIN + SHIFT
                    count = min(WIN, height - start)
                    rows = slice(start, start + count)
                    out_ref[at : at + count, :] = (
                        tile_ref[0, col + SHIFT, rows, :]
                        if local
                        else cols_ref[col + SHIFT - breadth, rows, :]
                    )
                    for j in range(WIN - count):
                        out_ref[at + count + j : at + count + j + 1, :] = rows_ref[
                            j, col : col + 1, :
                        ]


def deposit(half, src_ref, tile_ref, row_ref, col_ref):
    _, breadth, height, _ = tile_ref.shape
    for place in range(height // (BANDS * WIN)):

        @pl.when(half == place)
        def _():
            for col in range(breadth):
                local = col < breadth - SHIFT
                for band in range(BANDS):
                    at = row_of(band, col)
                    start = (place * BANDS + band) * WIN + SHIFT
                    count = min(WIN, height - start)
                    rows = slice(start, start + count)
                    if local:
                        tile_ref[0, col + SHIFT, rows, :] = src_ref[at : at + count, :]
                    else:
                        col_ref[0, col + SHIFT - breadth, rows, :] = src_ref[at : at + count, :]
                    for j in range(WIN - count):
                        row_ref[0, j, col : col + 1, :] = src_ref[
                            at + count + j : at + count + j + 1, :
                        ]


def spread(rows, head_size, lanes):
    heads = lanes // head_size
    rows = jnp.concatenate([rows, jnp.zeros((QL - WT, lanes), rows.dtype)], axis=0)
    lane = lax.broadcasted_iota(jnp.int32, (QL, lanes), 1) // head_size
    zero = jnp.zeros_like(rows)
    return jnp.concatenate([jnp.where(lane == h, rows, zero) for h in range(heads)], axis=0)


def collapse(wide, head_size, lanes):
    heads = lanes // head_size
    lane = lax.broadcasted_iota(jnp.int32, (WT, lanes), 1) // head_size
    out = wide[0:WT]
    for h in range(1, heads):
        out = jnp.where(lane == h, wide[h * QL : h * QL + WT], out)
    return out


def per_query(scores_low, feats, head_size):
    features = feats.shape[1]
    quad = 128 // head_size
    parts = []
    for g in range(features // 128):
        block = scores_low[:, g * quad * QL : (g + 1) * quad * QL]
        wide = tn(block, feats[:, g * 128 : (g + 1) * 128])
        parts.append(collapse(wide, head_size, 128))
    return jnp.concatenate(parts, axis=1)


def attend_kernel(
    head_size,
    tile_ref,
    row_ref,
    corner_ref,
    col_ref,
    weight_ref,
    vec_ref,
    bias_ref,
    xp_ref,
    hid_ref,
    qkv_ref,
    prob_ref,
    att_ref,
    mid_ref,
    wide_ref,
    rows_ref,
    cols_ref,
):
    half = pl.program_id(1)
    features = tile_ref.shape[-1]
    widen(half, row_ref, corner_ref, col_ref, rows_ref, cols_ref)
    extract(half, tile_ref, rows_ref, cols_ref, xp_ref)
    normed, _ = norm_parts(xp_ref[...])
    hidden = (normed * vec_ref[0:1, :] + vec_ref[1:2, :]).astype(BF)
    hid_ref[...] = hidden
    scale = head_size ** (-0.5)
    for part in range(3):
        got = nn(hidden, weight_ref[:, part * features : (part + 1) * features])
        if part == 0:
            got = got + vec_ref[2:3, :]
        if part == 2:
            got = got + vec_ref[3:4, :]
        qkv_ref[:, :, part * features : (part + 1) * features] = got.reshape(
            2 * BANDS, WT, features
        ).astype(BF)

    group = 256
    span = group // head_size * QL
    for w in range(2 * BANDS):
        kind = w % 2
        edge = jnp.where(half == 0, 0, 1) if w // 2 == BANDS - 1 else 0
        for g in range(features // group):
            q = qkv_ref[w, :, g * group : (g + 1) * group]
            k = qkv_ref[w, :, features + g * group : features + (g + 1) * group]
            raw = nt(k, spread(q, head_size, group))
            score = raw * scale + bias_ref[edge, kind, :, g * span : (g + 1) * span]
            highest = jnp.max(score, axis=0, keepdims=True)
            grown = jnp.exp(score - highest)
            total = jnp.sum(grown, axis=0, keepdims=True)
            probs = (grown * (1.0 / total)).astype(BF)
            prob_ref[w, :, g * span : (g + 1) * span] = probs
            v = qkv_ref[w, :, 2 * features + g * group : 2 * features + (g + 1) * group]
            wide_ref[w * WT : (w + 1) * WT, g * group : (g + 1) * group] = per_query(
                probs, v, head_size
            )
    attended = wide_ref[...].astype(BF)
    att_ref[...] = attended
    branch = nn(attended, weight_ref[:, 3 * features :]) + vec_ref[4:5, :]
    mid_ref[...] = xp_ref[...] + branch


def mlp_kernel(
    tile_ref,
    row_ref,
    corner_ref,
    col_ref,
    mid_ref,
    att_ref,
    weight_ref,
    packed_ref,
    vec_ref,
    ebias_ref,
    res_ref,
    resrow_ref,
    rescol_ref,
    gmid_ref,
    gatt_ref,
    pack_ref,
    sums_ref,
    esum_ref,
    cot_ref,
    we_ref,
    ws_ref,
    ge_ref,
    gs_ref,
    go_ref,
    out_ref,
    rows_ref,
    cols_ref,
):
    half = pl.program_id(1)
    step = pl.program_id(0) * pl.num_programs(1) + half
    steps = pl.num_programs(0) * pl.num_programs(1)
    features = tile_ref.shape[-1]
    hidden_units = we_ref.shape[1]
    shards = pack_ref.shape[0]
    deep = features // shards
    blocks = hidden_units // features

    @pl.when(step == 0)
    def _():
        for d in range(shards):
            we_ref[d * deep : (d + 1) * deep, :] = packed_ref[d, 0:deep, :]
            for j in range(blocks):
                at = d * deep * blocks + j * deep
                ws_ref[at : at + deep, :] = packed_ref[
                    d, deep : 2 * deep, j * features : (j + 1) * features
                ]
        ge_ref[...] = jnp.zeros_like(ge_ref)
        gs_ref[...] = jnp.zeros_like(gs_ref)
        go_ref[...] = jnp.zeros_like(go_ref)
        sums_ref[...] = jnp.zeros_like(sums_ref)
        esum_ref[...] = jnp.zeros_like(esum_ref)

    widen(half, row_ref, corner_ref, col_ref, rows_ref, cols_ref)
    extract(half, tile_ref, rows_ref, cols_ref, cot_ref)
    mid = mid_ref[...]
    normed, inverse = norm_parts(mid)
    hidden = (normed * vec_ref[5:6, :] + vec_ref[6:7, :]).astype(BF)
    hidden_t = hidden.T
    low = cot_ref[...].astype(BF)
    low_t = low.T
    out = mid + vec_ref[7:8, :]
    ghid = None
    chunk = features
    for c in range(hidden_units // chunk):
        cols = slice(c * chunk, (c + 1) * chunk)
        before = nn(hidden, we_ref[:, cols]) + ebias_ref[0:1, cols]
        phi = 0.5 * (1.0 + lax.erf(before * ROOT_HALF))
        slope = phi + before * (NORMAL_PEAK * jnp.exp(-0.5 * before * before))
        active = (before * phi).astype(BF)
        out = out + nn(active, ws_ref[cols, :])
        gbefore = nt(low, ws_ref[cols, :]) * slope
        esum_ref[0:1, cols] += jnp.sum(gbefore, axis=0, keepdims=True)
        gbefore = gbefore.astype(BF)
        back = nt(gbefore, we_ref[:, cols])
        ghid = back if ghid is None else ghid + back
        gs_ref[:, cols] += nn(low_t, active)
        ge_ref[:, cols] += nn(hidden_t, gbefore)
    out_ref[...] = out
    deposit(half, out_ref, res_ref, resrow_ref, rescol_ref)
    cot = cot_ref[...]
    gmid = cot + norm_back(ghid, normed, inverse, vec_ref[5:6, :])
    gmid_ref[...] = gmid
    gbranch = gmid.astype(BF)
    go_ref[...] += nn(att_ref[...].T, gbranch)
    gatt = nt(gbranch, weight_ref[:, 3 * features :])
    gatt_ref[...] = gatt.reshape(2 * BANDS, WT, features).astype(BF)
    sums_ref[0:1, :] += jnp.sum(gmid, axis=0, keepdims=True)
    sums_ref[1:2, :] += jnp.sum(ghid * normed, axis=0, keepdims=True)
    sums_ref[2:3, :] += jnp.sum(ghid, axis=0, keepdims=True)
    sums_ref[3:4, :] += jnp.sum(cot, axis=0, keepdims=True)

    @pl.when(step == steps - 1)
    def _():
        base = 2 * deep
        for d in range(shards):
            pack_ref[d, 0:deep, :] = ge_ref[d * deep : (d + 1) * deep, :].astype(BF)
            for j in range(blocks):
                at = d * deep * blocks + j * deep
                if deep * 2 % 128 == 0 and j % 2 == 0:
                    both = gs_ref[:, at : at + 2 * deep].T
                    pack_ref[d, deep : 2 * deep, j * features : (j + 1) * features] = both[
                        :deep
                    ].astype(BF)
                    pack_ref[d, deep : 2 * deep, (j + 1) * features : (j + 2) * features] = both[
                        deep:
                    ].astype(BF)
                elif deep * 2 % 128 != 0:
                    pack_ref[d, deep : 2 * deep, j * features : (j + 1) * features] = (
                        gs_ref[:, at : at + deep].T.astype(BF)
                    )
                thin = deep // blocks
                pack_ref[d, base : base + thin, j * features : (j + 1) * features] = go_ref[
                    d * deep + j * thin : d * deep + (j + 1) * thin, :
                ].astype(BF)


def back_kernel(
    head_size,
    hid_ref,
    qkv_ref,
    prob_ref,
    gatt_ref,
    weight_ref,
    vec_ref,
    sums_two_ref,
    esum_ref,
    gact_ref,
    pack_ref,
    acc_ref,
    wide_ref,
    sums_ref,
    table_ref,
):
    half = pl.program_id(1)
    step = pl.program_id(0) * pl.num_programs(1) + half
    steps = pl.num_programs(0) * pl.num_programs(1)
    features = hid_ref.shape[-1]
    scale = head_size ** (-0.5)

    @pl.when(step == 0)
    def _():
        acc_ref[...] = jnp.zeros_like(acc_ref)
        sums_ref[...] = jnp.zeros_like(sums_ref)
        table_ref[...] = jnp.zeros_like(table_ref)

    group = 256
    span = group // head_size * QL
    for w in range(2 * BANDS):
        rows = slice(w * WT, (w + 1) * WT)
        for g in range(features // group):
            feats = slice(g * group, (g + 1) * group)
            lanes = slice(g * span, (g + 1) * span)
            q = qkv_ref[w, :, g * group : (g + 1) * group]
            k = qkv_ref[w, :, features + g * group : features + (g + 1) * group]
            v = qkv_ref[w, :, 2 * features + g * group : 2 * features + (g + 1) * group]
            up = spread(gatt_ref[w, :, feats], head_size, group)
            low = prob_ref[w, :, lanes]
            probs = low.astype(F32)
            gprobs = nt(v, up)
            mean = jnp.sum(probs * gprobs, axis=0, keepdims=True)
            gscore = probs * (gprobs - mean)
            table_ref[0:WT, lanes] += gscore
            graw = (gscore * scale).astype(BF)
            wide_ref[rows, g * group : (g + 1) * group] = per_query(graw, k, head_size)
            wide_ref[rows, features + g * group : features + (g + 1) * group] = nn(
                graw, spread(q, head_size, group)
            )
            wide_ref[rows, 2 * features + g * group : 2 * features + (g + 1) * group] = nn(low, up)
    gjoint = wide_ref[...]
    sums_ref[...] += jnp.sum(gjoint, axis=0, keepdims=True)
    gjoint = gjoint.astype(BF)
    gact_ref[...] = gjoint
    acc_ref[...] += nn(hid_ref[...].T, gjoint)

    @pl.when(step == steps - 1)
    def _():
        shards = pack_ref.shape[0]
        deep = features // shards
        lanes = table_ref.shape[1] // shards
        total = sums_ref[0:1, :]
        by_acc = jnp.zeros((features, 128), F32)
        by_sum = jnp.zeros((features, 128), F32)
        for c in range(3 * features // 128):
            cols = slice(c * 128, (c + 1) * 128)
            weight = weight_ref[:, cols].astype(F32)
            by_acc = by_acc + weight * acc_ref[:, cols]
            by_sum = by_sum + weight * total[:, cols]
        by_acc = jnp.sum(by_acc.T, axis=0, keepdims=True)
        gshift = jnp.sum(by_sum.T, axis=0, keepdims=True)
        ggain = (by_acc - vec_ref[1:2, :] * gshift) / vec_ref[0:1, :]
        lines = jnp.concatenate(
            [
                ggain,
                gshift,
                total[:, :features],
                total[:, 2 * features :],
                jnp.zeros((LINES - 4, features), F32),
            ],
            axis=0,
        )
        for d in range(shards):
            pack_ref[d, 0:deep, :] = acc_ref[d * deep : (d + 1) * deep, :].astype(BF)
            pack_ref[d, deep : deep + LINES, :] = jnp.zeros((LINES, 3 * features), BF)
            for j in range(4):
                pack_ref[d, deep : deep + LINES, j * lanes : (j + 1) * lanes] = table_ref[
                    j * LINES : (j + 1) * LINES, d * lanes : (d + 1) * lanes
                ].astype(BF)
            own = slice(d * deep, (d + 1) * deep)
            at = features
            pack_ref[d, deep : deep + LINES, at : at + deep] = lines[:, own].astype(BF)
            at = features + features // 2
            pack_ref[d, deep : deep + LINES, at : at + deep] = sums_two_ref[:, own].astype(BF)
            at = 2 * features
            even = esum_ref.shape[1] // shards
            pack_ref[d, deep : deep + LINES, at : at + even] = esum_ref[
                :, d * even : (d + 1) * even
            ].astype(BF)


def close_kernel(
    gact_ref, xp_ref, gmid_ref, weight_ref, vec_ref, gtok_ref, grow_ref, gcol_ref, out_ref
):
    features = xp_ref.shape[-1]
    ghid = nt(gact_ref[...], weight_ref[:, : 3 * features])
    normed, inverse = norm_parts(xp_ref[...])
    out_ref[...] = gmid_ref[...] + norm_back(ghid, normed, inverse, vec_ref[0:1, :])
    deposit(pl.program_id(1), out_ref, gtok_ref, grow_ref, gcol_ref)


def patch_kernel(tile_ref, col_ref, row_ref, out_ref, flank_ref, top_ref, sems):
    images, breadth, _, _ = tile_ref.shape
    fetch = pltpu.make_async_copy(out_ref.at[:, SHIFT:, 0:PAD], top_ref, sems.at[0])
    fetch.start()
    flank_ref[...] = col_ref[...].astype(F32)
    for i in range(images):
        for c in range(SHIFT):
            for j in range(SHIFT):
                flank_ref[i, c, j : j + 1, :] = row_ref[i, j, c : c + 1, :]
    side = pltpu.make_async_copy(flank_ref, out_ref.at[:, 0:SHIFT], sems.at[1])
    side.start()
    fetch.wait()
    for i in range(images):
        for c in range(breadth - SHIFT):
            for j in range(SHIFT):
                top_ref[i, c, j : j + 1, :] = row_ref[i, j, c + SHIFT : c + SHIFT + 1, :]
    back = pltpu.make_async_copy(top_ref, out_ref.at[:, SHIFT:, 0:PAD], sems.at[2])
    back.start()
    side.wait()
    back.wait()


def shifted(block, axis, distance):
    count = lax.axis_size(axis)
    return lax.ppermute(block, axis, [((i - distance) % count, i) for i in range(count)])


def slanted(block, distance):
    rows, cols = lax.axis_size("row"), lax.axis_size("col")
    route = [
        (((r - distance) % rows) * cols + (c - distance) % cols, r * cols + c)
        for r in range(rows)
        for c in range(cols)
    ]
    return lax.ppermute(block, ("row", "col"), route)


def edge_kernel(first_ref, second_ref, row_ref, corner_ref, col_ref, flank, top, tidy, small, sems):
    tiles = (first_ref, second_ref)
    images, breadth = first_ref.shape[:2]
    copies = []
    for t, tile in enumerate(tiles):
        span = slice(t * images, (t + 1) * images)
        copies.append(
            pltpu.make_async_copy(tile.at[:, :, 0:PAD], top.at[span], sems.at[2 * t])
        )
        copies.append(
            pltpu.make_async_copy(tile.at[:, 0:SHIFT], flank.at[span], sems.at[2 * t + 1])
        )
    for copy in copies:
        copy.start()
    for t in range(2):
        span = slice(t * images, (t + 1) * images)
        copies[2 * t].wait()
        for i in range(t * images, (t + 1) * images):
            for c in range(breadth):
                for j in range(SHIFT):
                    if c < SHIFT:
                        small[i, j, c : c + 1, :] = top[i, c, j : j + 1, :]
                    else:
                        tidy[i, j, c - SHIFT : c - SHIFT + 1, :] = top[i, c, j : j + 1, :]
        copies[2 * t + 1].wait()
        col_ref[span] = flank[span].astype(BF)
    row_ref[...] = tidy[...].astype(BF)
    corner_ref[...] = small[...].astype(BF)


def roll_in(first, second):
    images, breadth, height, features = first.shape
    both = 2 * images
    vmem = pl.BlockSpec(memory_space=pltpu.VMEM)
    shapes = (
        (both, SHIFT, breadth - SHIFT, features),
        (both, SHIFT, SHIFT, features),
        (both, SHIFT, height, features),
    )
    row, corner, col = pl.pallas_call(
        edge_kernel,
        in_specs=[pl.BlockSpec(memory_space=pl.ANY)] * 2,
        out_specs=[vmem] * 3,
        out_shape=[jax.ShapeDtypeStruct(s, BF) for s in shapes],
        scratch_shapes=[
            pltpu.VMEM(shapes[2], F32),
            pltpu.VMEM((both, breadth, PAD, features), F32),
            pltpu.VMEM(shapes[0], F32),
            pltpu.VMEM(shapes[1], F32),
            pltpu.SemaphoreType.DMA((4,)),
        ],
        compiler_params=pltpu.CompilerParams(vmem_limit_bytes=24 * 1024 * 1024),
        cost_estimate=pl.CostEstimate(flops=0, bytes_accessed=5_000_000, transcendentals=0),
        name="edge",
    )(first, second)
    return shifted(row, "row", -1), slanted(corner, -1), shifted(col, "col", -1)


def roll_out(tile, rows, cols):
    images, breadth, height, features = tile.shape
    rows = rows.astype(BF)
    flank = shifted(cols.astype(BF), "col", 1)
    top = shifted(rows[:, :, : breadth - SHIFT], "row", 1)
    corner = slanted(rows[:, :, breadth - SHIFT :], 1)
    top = jnp.concatenate([corner, top], axis=2).astype(F32)
    vmem = pl.BlockSpec(memory_space=pltpu.VMEM)
    return pl.pallas_call(
        patch_kernel,
        in_specs=[pl.BlockSpec(memory_space=pl.ANY), vmem, vmem],
        out_specs=pl.BlockSpec(memory_space=pl.ANY),
        out_shape=jax.ShapeDtypeStruct(tile.shape, F32),
        scratch_shapes=[
            pltpu.VMEM((images, SHIFT, height, features), F32),
            pltpu.VMEM((images, breadth - SHIFT, PAD, features), F32),
            pltpu.SemaphoreType.DMA((3,)),
        ],
        input_output_aliases={0: 0},
        compiler_params=pltpu.CompilerParams(vmem_limit_bytes=24 * 1024 * 1024),
        cost_estimate=pl.CostEstimate(flops=0, bytes_accessed=4_000_000, transcendentals=0),
        name="patch",
    )(tile, flank, top)


def over_tiles(block):
    def added(part, axis):
        total = part.astype(F32)
        for step in range(1, lax.axis_size(axis)):
            total = total + shifted(part, axis, step).astype(F32)
        return total

    cut = block.shape[-1] // 2
    first = added(added(block[:, :cut], "row").astype(BF), "col")
    second = added(added(block[:, cut:], "col").astype(BF), "row")
    return jnp.concatenate([first, second], axis=1)


def region_band(places, count):
    return jnp.where(places < count - WIN, 0, jnp.where(places < count - SHIFT, 1, 2)).astype(
        jnp.int32
    )


def whole(shape):
    return pl.BlockSpec(shape, lambda i, j: (0,) * len(shape), pipeline_mode=pl.Buffered(1))


def body(
    tokens,
    position_index,
    first_gain,
    first_shift,
    joint_weight,
    query_bias,
    value_bias,
    position_table,
    output_weight,
    output_bias,
    second_gain,
    second_shift,
    expand_weight,
    expand_bias,
    shrink_weight,
    shrink_bias,
    cotangent,
):
    images, height, breadth, features = tokens.shape
    shards = lax.axis_size("dp")
    deep = joint_weight.shape[0]
    table_heads, table_rows = position_table.shape
    heads = table_heads * shards
    head_size = features // heads
    hidden_units = expand_weight.shape[1]
    blocks = hidden_units // features
    halves = height // (WIN * BANDS)
    grid = (images, halves)
    step_rows = 2 * BANDS * WT
    total_rows = images * halves * step_rows
    windows = images * halves * 2 * BANDS
    wide = heads * QL

    small = [
        first_gain,
        first_shift,
        query_bias,
        value_bias,
        output_bias,
        second_gain,
        second_shift,
        shrink_bias,
        expand_bias,
        position_table.reshape(-1),
    ]
    small = jnp.concatenate([s.astype(BF) for s in small])
    small = jnp.pad(small, (0, -small.shape[0] % 128))[None]
    small = lax.all_gather(small, "dp", axis=0, tiled=True)
    vec = small[:, : 8 * deep].reshape(shards, 8, deep).transpose(1, 0, 2).reshape(8, features)
    vec = vec.astype(F32)
    at = 8 * deep
    ebias = small[:, at : at + blocks * deep].reshape(1, hidden_units).astype(F32)
    at += blocks * deep
    table = small[:, at : at + table_heads * table_rows].reshape(heads, table_rows)
    weight_one = lax.all_gather(
        jnp.concatenate([joint_weight, output_weight], axis=1).astype(BF), "dp", axis=0, tiled=True
    )
    thick = jnp.concatenate(
        [shrink_weight[j * deep : (j + 1) * deep] for j in range(blocks)], axis=1
    )
    weight_two = lax.all_gather(
        jnp.concatenate([expand_weight, thick], axis=0).astype(BF)[None], "dp", axis=0, tiled=True
    )

    tokens, cotangent = tokens.transpose(0, 2, 1, 3), cotangent.transpose(0, 2, 1, 3)
    halo = roll_in(tokens, cotangent)

    paired = position_index.reshape(WIN, WIN, WIN, WIN)
    paired = paired.transpose(1, 0, 3, 2)
    paired = jnp.pad(paired, ((0, 0), (0, 1), (0, 0), (0, 1)), constant_values=-1)
    paired = jnp.pad(
        paired.reshape(WT, WT).T, ((0, 0), (0, QL - WT)), constant_values=-1
    ).reshape(-1)
    onehot = paired[None, :] == jnp.arange(table_rows, dtype=jnp.int32)[:, None]
    position = jnp.dot(table, onehot.astype(BF), preferred_element_type=F32)
    position = position.reshape(heads, WT, QL).transpose(1, 0, 2)
    grid_rows = height * lax.axis_size("row")
    grid_cols = breadth * lax.axis_size("col")
    row_places = jnp.stack([jnp.arange(WIN), jnp.arange(WIN) + height - WIN]).astype(jnp.int32)
    row_places = row_places + lax.axis_index("row") * height
    col_places = jnp.arange(2 * WIN, dtype=jnp.int32).reshape(2, WIN)
    col_places = col_places + lax.axis_index("col") * breadth
    row_label = jnp.pad(region_band(row_places, grid_rows), ((0, 0), (0, 1)))
    col_label = region_band(col_places, grid_cols)
    label = 3 * row_label[:, None, None, :] + col_label[None, :, :, None]
    label = label.reshape(2, 2, WT)
    label_q = jnp.pad(label, ((0, 0), (0, 0), (0, QL - WT)))
    masking = jnp.where(label[:, :, :, None] == label_q[:, :, None, :], 0.0, -100.0)
    absent = (jnp.arange(WT) % PAD == WIN)[:, None]
    masking = jnp.where(absent, FAR_BELOW, masking).astype(F32)
    bias = (position[None, None] + masking[:, :, :, None, :]).reshape(2, 2, WT, wide)

    tile_spec = pl.BlockSpec((1, breadth, height, features), lambda i, j: (i, 0, 0, 0))

    def halo_specs(first):
        sizes = (breadth - SHIFT, SHIFT, height)
        return [
            pl.BlockSpec((1, SHIFT, size, features), lambda i, j: (first + i, 0, 0, 0))
            for size in sizes
        ]

    row_spec = pl.BlockSpec((1, SHIFT, breadth, features), lambda i, j: (i, 0, 0, 0))
    col_spec = pl.BlockSpec((1, SHIFT, height, features), lambda i, j: (i, 0, 0, 0))
    flat_spec = pl.BlockSpec((step_rows, features), lambda i, j: (i * halves + j, 0))

    joint_spec = pl.BlockSpec((step_rows, 3 * features), lambda i, j: (i * halves + j, 0))

    def window_spec(last):
        return pl.BlockSpec((2 * BANDS, WT, last), lambda i, j: (i * halves + j, 0, 0))

    params = pltpu.CompilerParams(
        dimension_semantics=("arbitrary", "arbitrary"), vmem_limit_bytes=VMEM_LIMIT
    )
    shape = jax.ShapeDtypeStruct
    halo_scratch = [
        pltpu.VMEM((SHIFT, breadth, features), F32),
        pltpu.VMEM((SHIFT, height, features), F32),
    ]
    dense = 2 * total_rows * features * features

    xp, hidden_one, qkv, probs, attended, middle = pl.pallas_call(
        functools.partial(attend_kernel, head_size),
        grid=grid,
        in_specs=[
            tile_spec,
            *halo_specs(0),
            whole((features, 4 * features)),
            whole((8, features)),
            whole((2, 2, WT, wide)),
        ],
        out_specs=[
            flat_spec,
            flat_spec,
            window_spec(3 * features),
            window_spec(wide),
            flat_spec,
            flat_spec,
        ],
        out_shape=[
            shape((total_rows, features), F32),
            shape((total_rows, features), BF),
            shape((windows, WT, 3 * features), BF),
            shape((windows, WT, wide), BF),
            shape((total_rows, features), BF),
            shape((total_rows, features), F32),
        ],
        scratch_shapes=[pltpu.VMEM((step_rows, features), F32), *halo_scratch],
        compiler_params=params,
        cost_estimate=pl.CostEstimate(
            flops=6 * dense, bytes_accessed=40_000_000, transcendentals=windows * WT * wide
        ),
        name="attend",
    )(tokens, *halo, weight_one, vec, bias)

    packed_rows = 2 * deep + deep // blocks
    result, res_row, res_col, gmid, gatt, pack_two, sums_two, esum = pl.pallas_call(
        mlp_kernel,
        grid=grid,
        in_specs=[
            tile_spec,
            *halo_specs(images),
            flat_spec,
            flat_spec,
            whole((features, 4 * features)),
            whole((shards, 2 * deep, hidden_units)),
            whole((8, features)),
            whole((1, hidden_units)),
        ],
        out_specs=[
            tile_spec,
            row_spec,
            col_spec,
            flat_spec,
            window_spec(features),
            whole((shards, packed_rows, hidden_units)),
            whole((LINES, features)),
            whole((LINES, hidden_units)),
        ],
        out_shape=[
            shape(tokens.shape, F32),
            shape((images, SHIFT, breadth, features), F32),
            shape((images, SHIFT, height, features), F32),
            shape((total_rows, features), F32),
            shape((windows, WT, features), BF),
            shape((shards, packed_rows, hidden_units), BF),
            shape((LINES, features), F32),
            shape((LINES, hidden_units), F32),
        ],
        scratch_shapes=[
            pltpu.VMEM((step_rows, features), F32),
            pltpu.VMEM((features, hidden_units), BF),
            pltpu.VMEM((hidden_units, features), BF),
            pltpu.VMEM((features, hidden_units), F32),
            pltpu.VMEM((features, hidden_units), F32),
            pltpu.VMEM((features, features), F32),
            pltpu.VMEM((step_rows, features), F32),
            *halo_scratch,
        ],
        compiler_params=params,
        cost_estimate=pl.CostEstimate(
            flops=26 * dense,
            bytes_accessed=50_000_000,
            transcendentals=total_rows * hidden_units,
        ),
        name="mlp",
    )(
        cotangent,
        *halo,
        middle,
        attended,
        weight_one,
        weight_two,
        vec,
        ebias,
    )

    pack_two = lax.psum_scatter(pack_two, "dp", scatter_dimension=0, tiled=True)[0]
    final = roll_out(result, res_row, res_col)

    gact, pack_one = pl.pallas_call(
        functools.partial(back_kernel, head_size),
        grid=grid,
        in_specs=[
            flat_spec,
            window_spec(3 * features),
            window_spec(wide),
            window_spec(features),
            whole((features, 4 * features)),
            whole((8, features)),
            whole((LINES, features)),
            whole((LINES, hidden_units)),
        ],
        out_specs=[joint_spec, whole((shards, deep + LINES, 3 * features))],
        out_shape=[
            shape((total_rows, 3 * features), BF),
            shape((shards, deep + LINES, 3 * features), BF),
        ],
        scratch_shapes=[
            pltpu.VMEM((features, 3 * features), F32),
            pltpu.VMEM((step_rows, 3 * features), F32),
            pltpu.VMEM((1, 3 * features), F32),
            pltpu.VMEM((4 * LINES, wide), F32),
        ],
        compiler_params=params,
        cost_estimate=pl.CostEstimate(
            flops=18 * dense, bytes_accessed=50_000_000, transcendentals=0
        ),
        name="back",
    )(hidden_one, qkv, probs, gatt, weight_one, vec, sums_two, esum)

    pack_one = lax.psum_scatter(pack_one, "dp", scatter_dimension=0, tiled=True)[0]

    gtok, gtok_row, gtok_col = pl.pallas_call(
        close_kernel,
        grid=grid,
        in_specs=[
            joint_spec,
            flat_spec,
            flat_spec,
            whole((features, 4 * features)),
            whole((8, features)),
        ],
        out_specs=[tile_spec, row_spec, col_spec],
        out_shape=[
            shape(tokens.shape, F32),
            shape((images, SHIFT, breadth, features), F32),
            shape((images, SHIFT, height, features), F32),
        ],
        scratch_shapes=[pltpu.VMEM((step_rows, features), F32)],
        compiler_params=params,
        cost_estimate=pl.CostEstimate(
            flops=6 * dense, bytes_accessed=30_000_000, transcendentals=0
        ),
        name="close",
    )(gact, xp, gmid, weight_one, vec)
    grad_tokens = roll_out(gtok, gtok_row, gtok_col)

    pack_two = over_tiles(pack_two)
    pack_one, pack_two, final, grad_tokens = lax.optimization_barrier(
        (pack_one, pack_two, final, grad_tokens)
    )
    pack_one = over_tiles(pack_one)
    grad_expand = pack_two[:deep]
    grad_shrink = jnp.concatenate(
        [pack_two[deep : 2 * deep, j * features : (j + 1) * features] for j in range(blocks)],
        axis=0,
    )
    base = 2 * deep
    grad_output = jnp.concatenate(
        [pack_two[base:, j * features : (j + 1) * features] for j in range(blocks)], axis=0
    )
    grad_joint = pack_one[:deep]
    lanes = table_heads * QL
    lines_one = pack_one[deep:, features : features + deep]
    at = features + features // 2
    lines_two = pack_one[deep:, at : at + deep]
    grad_expand_bias = pack_one[deep, 2 * features : 2 * features + blocks * deep]
    gtable = jnp.concatenate(
        [pack_one[deep:, j * lanes : (j + 1) * lanes] for j in range(4)], axis=0
    )[:WT]
    gtable = gtable.reshape(WT, table_heads, QL).transpose(1, 0, 2).reshape(table_heads, WT * QL)
    grad_position = lax.dot_general(
        gtable,
        onehot.astype(F32),
        (((1,), (1,)), ((), ())),
        precision=lax.Precision.HIGHEST,
        preferred_element_type=F32,
    )
    final, grad_tokens = final.transpose(0, 2, 1, 3), grad_tokens.transpose(0, 2, 1, 3)
    return (
        final,
        grad_tokens,
        lines_one[0],
        lines_one[1],
        grad_joint,
        lines_one[2],
        lines_one[3],
        grad_position,
        grad_output,
        lines_two[0],
        lines_two[1],
        lines_two[2],
        grad_expand,
        grad_expand_bias,
        grad_shrink,
        lines_two[3],
    )


def solution(mesh):
    tile = P("dp", "row", "col", None)
    flat = P("dp")
    wide = P("dp", None)

    return jax.shard_map(
        body,
        mesh=mesh,
        in_specs=(
            tile,
            P(),
            flat,
            flat,
            wide,
            flat,
            flat,
            wide,
            wide,
            flat,
            flat,
            flat,
            wide,
            flat,
            wide,
            flat,
            tile,
        ),
        out_specs=(
            tile,
            tile,
            flat,
            flat,
            wide,
            flat,
            flat,
            wide,
            wide,
            flat,
            flat,
            flat,
            wide,
            flat,
            wide,
            flat,
        ),
        check_vma=False,
    )
```

```python
import functools

import jax
import jax.numpy as jnp
from jax import lax
from jax.experimental import pallas as pl
from jax.experimental.pallas import tpu as pltpu
from jax.sharding import PartitionSpec as P


WIN = 7
SHIFT = 3
PAD = 8
WT = WIN * PAD
QL = 64
EPSILON = 1e-05
ROOT_HALF = 0.7071067811865476
NORMAL_PEAK = 0.3989422804014327
FAR_BELOW = -1000000000.0
BF = jnp.bfloat16
F32 = jnp.float32
BANDS = 4
LINES = 16
VMEM_LIMIT = 60 * 1024 * 1024


def nn(a, b):
    return lax.dot_general(a, b, (((1,), (0,)), ((), ())), preferred_element_type=F32)


def nt(a, b):
    return lax.dot_general(a, b, (((1,), (1,)), ((), ())), preferred_element_type=F32)


def tn(a, b):
    return lax.dot_general(a, b, (((0,), (0,)), ((), ())), preferred_element_type=F32)


def norm_parts(values):
    center = values - jnp.mean(values, axis=-1, keepdims=True)
    inverse = lax.rsqrt(jnp.mean(center * center, axis=-1, keepdims=True) + EPSILON)
    return center * inverse, inverse


def norm_back(upper, normed, inverse, scaling):
    scaled = upper * scaling
    return inverse * (
        scaled
        - jnp.mean(scaled, axis=-1, keepdims=True)
        - normed * jnp.mean(scaled * normed, axis=-1, keepdims=True)
    )


def row_of(band, col):
    return ((2 * band + col // WIN) * WIN + col % WIN) * PAD


def widen(half, row_ref, corner_ref, col_ref, rows_ref, cols_ref):
    @pl.when(half == 0)
    def _():
        own = row_ref.shape[2]
        rows_ref[:, 0:own, :] = row_ref[0].astype(F32)
        rows_ref[:, own : own + SHIFT, :] = corner_ref[0].astype(F32)
        cols_ref[...] = col_ref[0].astype(F32)


def extract(half, tile_ref, rows_ref, cols_ref, out_ref):
    _, breadth, height, features = tile_ref.shape
    zero = jnp.zeros((1, features), F32)
    for band in range(BANDS):
        for col in range(breadth):
            at = row_of(band, col)
            out_ref[at + WIN : at + PAD, :] = zero
    for place in range(height // (BANDS * WIN)):

        @pl.when(half == place)
        def _():
            for col in range(breadth):
                local = col < breadth - SHIFT
                for band in range(BANDS):
                    at = row_of(band, col)
                    start = (place * BANDS + band) * WIN + SHIFT
                    count = min(WIN, height - start)
                    rows = slice(start, start + count)
                    out_ref[at : at + count, :] = (
                        tile_ref[0, col + SHIFT, rows, :]
                        if local
                        else cols_ref[col + SHIFT - breadth, rows, :]
                    )
                    for j in range(WIN - count):
                        out_ref[at + count + j : at + count + j + 1, :] = rows_ref[
                            j, col : col + 1, :
                        ]


def deposit(half, src_ref, tile_ref, row_ref, col_ref):
    _, breadth, height, _ = tile_ref.shape
    for place in range(height // (BANDS * WIN)):

        @pl.when(half == place)
        def _():
            for col in range(breadth):
                local = col < breadth - SHIFT
                for band in range(BANDS):
                    at = row_of(band, col)
                    start = (place * BANDS + band) * WIN + SHIFT
                    count = min(WIN, height - start)
                    rows = slice(start, start + count)
                    if local:
                        tile_ref[0, col + SHIFT, rows, :] = src_ref[at : at + count, :]
                    else:
                        col_ref[0, col + SHIFT - breadth, rows, :] = src_ref[at : at + count, :]
                    for j in range(WIN - count):
                        row_ref[0, j, col : col + 1, :] = src_ref[
                            at + count + j : at + count + j + 1, :
                        ]


def spread(rows, head_size, lanes):
    heads = lanes // head_size
    rows = jnp.concatenate([rows, jnp.zeros((QL - WT, lanes), rows.dtype)], axis=0)
    lane = lax.broadcasted_iota(jnp.int32, (QL, lanes), 1) // head_size
    zero = jnp.zeros_like(rows)
    return jnp.concatenate([jnp.where(lane == h, rows, zero) for h in range(heads)], axis=0)


def collapse(wide, head_size, lanes):
    heads = lanes // head_size
    lane = lax.broadcasted_iota(jnp.int32, (WT, lanes), 1) // head_size
    out = wide[0:WT]
    for h in range(1, heads):
        out = jnp.where(lane == h, wide[h * QL : h * QL + WT], out)
    return out


def per_query(scores_low, feats, head_size):
    features = feats.shape[1]
    quad = 128 // head_size
    parts = []
    for g in range(features // 128):
        block = scores_low[:, g * quad * QL : (g + 1) * quad * QL]
        wide = tn(block, feats[:, g * 128 : (g + 1) * 128])
        parts.append(collapse(wide, head_size, 128))
    return jnp.concatenate(parts, axis=1)


def attend_kernel(
    head_size,
    tile_ref,
    row_ref,
    corner_ref,
    col_ref,
    weight_ref,
    vec_ref,
    bias_ref,
    xp_ref,
    hid_ref,
    qkv_ref,
    prob_ref,
    att_ref,
    mid_ref,
    wide_ref,
    rows_ref,
    cols_ref,
):
    half = pl.program_id(1)
    features = tile_ref.shape[-1]
    widen(half, row_ref, corner_ref, col_ref, rows_ref, cols_ref)
    extract(half, tile_ref, rows_ref, cols_ref, xp_ref)
    normed, _ = norm_parts(xp_ref[...])
    hidden = (normed * vec_ref[0:1, :] + vec_ref[1:2, :]).astype(BF)
    hid_ref[...] = hidden
    scale = head_size ** (-0.5)
    for part in range(3):
        got = nn(hidden, weight_ref[:, part * features : (part + 1) * features])
        if part == 0:
            got = got + vec_ref[2:3, :]
        if part == 2:
            got = got + vec_ref[3:4, :]
        qkv_ref[:, :, part * features : (part + 1) * features] = got.reshape(
            2 * BANDS, WT, features
        ).astype(BF)

    group = 256
    span = group // head_size * QL
    items = [(w, g) for w in range(2 * BANDS) for g in range(features // group)]

    def scores(item):
        w, g = item
        q = qkv_ref[w, :, g * group : (g + 1) * group]
        k = qkv_ref[w, :, features + g * group : features + (g + 1) * group]
        return nt(k, spread(q, head_size, group))

    def soften(item, raw):
        w, g = item
        edge = jnp.where(half == 0, 0, 1) if w // 2 == BANDS - 1 else 0
        score = raw * scale + bias_ref[edge, w % 2, :, g * span : (g + 1) * span]
        highest = jnp.max(score, axis=0, keepdims=True)
        grown = jnp.exp(score - highest)
        total = jnp.sum(grown, axis=0, keepdims=True)
        prob_ref[w, :, g * span : (g + 1) * span] = (grown * (1.0 / total)).astype(BF)

    def mix(item):
        w, g = item
        probs = prob_ref[w, :, g * span : (g + 1) * span]
        v = qkv_ref[w, :, 2 * features + g * group : 2 * features + (g + 1) * group]
        wide_ref[w * WT : (w + 1) * WT, g * group : (g + 1) * group] = per_query(
            probs, v, head_size
        )

    raws = {}
    for t in range(len(items) + 2):
        if t < len(items):
            raws[t] = scores(items[t])
        if 1 <= t <= len(items):
            soften(items[t - 1], raws.pop(t - 1))
        if t >= 2:
            mix(items[t - 2])
    attended = wide_ref[...].astype(BF)
    att_ref[...] = attended
    branch = nn(attended, weight_ref[:, 3 * features :]) + vec_ref[4:5, :]
    mid_ref[...] = xp_ref[...] + branch


def mlp_kernel(
    tile_ref,
    row_ref,
    corner_ref,
    col_ref,
    mid_ref,
    att_ref,
    weight_ref,
    packed_ref,
    vec_ref,
    ebias_ref,
    res_ref,
    resrow_ref,
    rescol_ref,
    gmid_ref,
    gatt_ref,
    pack_ref,
    sums_ref,
    esum_ref,
    cot_ref,
    we_ref,
    ws_ref,
    ge_ref,
    gs_ref,
    go_ref,
    out_ref,
    rows_ref,
    cols_ref,
):
    half = pl.program_id(1)
    step = pl.program_id(0) * pl.num_programs(1) + half
    steps = pl.num_programs(0) * pl.num_programs(1)
    features = tile_ref.shape[-1]
    hidden_units = we_ref.shape[1]
    shards = pack_ref.shape[0]
    deep = features // shards
    blocks = hidden_units // features

    @pl.when(step == 0)
    def _():
        for d in range(shards):
            we_ref[d * deep : (d + 1) * deep, :] = packed_ref[d, 0:deep, :]
            for j in range(blocks):
                at = d * deep * blocks + j * deep
                ws_ref[at : at + deep, :] = packed_ref[
                    d, deep : 2 * deep, j * features : (j + 1) * features
                ]
        ge_ref[...] = jnp.zeros_like(ge_ref)
        gs_ref[...] = jnp.zeros_like(gs_ref)
        go_ref[...] = jnp.zeros_like(go_ref)
        sums_ref[...] = jnp.zeros_like(sums_ref)
        esum_ref[...] = jnp.zeros_like(esum_ref)

    widen(half, row_ref, corner_ref, col_ref, rows_ref, cols_ref)
    extract(half, tile_ref, rows_ref, cols_ref, cot_ref)
    mid = mid_ref[...]
    normed, inverse = norm_parts(mid)
    hidden = (normed * vec_ref[5:6, :] + vec_ref[6:7, :]).astype(BF)
    hidden_t = hidden.T
    low = cot_ref[...].astype(BF)
    low_t = low.T
    out = mid + vec_ref[7:8, :]
    ghid = None
    chunk = features
    for c in range(hidden_units // chunk):
        cols = slice(c * chunk, (c + 1) * chunk)
        before = nn(hidden, we_ref[:, cols]) + ebias_ref[0:1, cols]
        phi = 0.5 * (1.0 + lax.erf(before * ROOT_HALF))
        slope = phi + before * (NORMAL_PEAK * jnp.exp(-0.5 * before * before))
        active = (before * phi).astype(BF)
        out = out + nn(active, ws_ref[cols, :])
        gbefore = nt(low, ws_ref[cols, :]) * slope
        esum_ref[0:1, cols] += jnp.sum(gbefore, axis=0, keepdims=True)
        gbefore = gbefore.astype(BF)
        back = nt(gbefore, we_ref[:, cols])
        ghid = back if ghid is None else ghid + back
        gs_ref[:, cols] += nn(low_t, active)
        ge_ref[:, cols] += nn(hidden_t, gbefore)
    out_ref[...] = out
    deposit(half, out_ref, res_ref, resrow_ref, rescol_ref)
    cot = cot_ref[...]
    gmid = cot + norm_back(ghid, normed, inverse, vec_ref[5:6, :])
    gmid_ref[...] = gmid
    gbranch = gmid.astype(BF)
    go_ref[...] += nn(att_ref[...].T, gbranch)
    gatt = nt(gbranch, weight_ref[:, 3 * features :])
    gatt_ref[...] = gatt.reshape(2 * BANDS, WT, features).astype(BF)
    sums_ref[0:1, :] += jnp.sum(gmid, axis=0, keepdims=True)
    sums_ref[1:2, :] += jnp.sum(ghid * normed, axis=0, keepdims=True)
    sums_ref[2:3, :] += jnp.sum(ghid, axis=0, keepdims=True)
    sums_ref[3:4, :] += jnp.sum(cot, axis=0, keepdims=True)

    @pl.when(step == steps - 1)
    def _():
        base = 2 * deep
        for d in range(shards):
            pack_ref[d, 0:deep, :] = ge_ref[d * deep : (d + 1) * deep, :].astype(BF)
            for j in range(blocks):
                at = d * deep * blocks + j * deep
                if deep * 2 % 128 == 0 and j % 2 == 0:
                    both = gs_ref[:, at : at + 2 * deep].T
                    pack_ref[d, deep : 2 * deep, j * features : (j + 1) * features] = both[
                        :deep
                    ].astype(BF)
                    pack_ref[d, deep : 2 * deep, (j + 1) * features : (j + 2) * features] = both[
                        deep:
                    ].astype(BF)
                elif deep * 2 % 128 != 0:
                    pack_ref[d, deep : 2 * deep, j * features : (j + 1) * features] = (
                        gs_ref[:, at : at + deep].T.astype(BF)
                    )
                thin = deep // blocks
                pack_ref[d, base : base + thin, j * features : (j + 1) * features] = go_ref[
                    d * deep + j * thin : d * deep + (j + 1) * thin, :
                ].astype(BF)


def back_kernel(
    head_size,
    hid_ref,
    qkv_ref,
    prob_ref,
    gatt_ref,
    weight_ref,
    vec_ref,
    sums_two_ref,
    esum_ref,
    gact_ref,
    pack_ref,
    acc_ref,
    wide_ref,
    sums_ref,
    table_ref,
    graw_ref,
):
    half = pl.program_id(1)
    step = pl.program_id(0) * pl.num_programs(1) + half
    steps = pl.num_programs(0) * pl.num_programs(1)
    features = hid_ref.shape[-1]
    scale = head_size ** (-0.5)

    @pl.when(step == 0)
    def _():
        acc_ref[...] = jnp.zeros_like(acc_ref)
        sums_ref[...] = jnp.zeros_like(sums_ref)
        table_ref[...] = jnp.zeros_like(table_ref)

    group = 256
    span = group // head_size * QL
    items = [(w, g) for w in range(2 * BANDS) for g in range(features // group)]

    def piece(item, part):
        w, g = item
        at = part * features + g * group
        return qkv_ref[w, :, at : at + group]

    def store(item, part, value):
        w, g = item
        at = part * features + g * group
        wide_ref[w * WT : (w + 1) * WT, at : at + group] = value

    def ascend(item):
        w, g = item
        lanes = slice(g * span, (g + 1) * span)
        up = spread(gatt_ref[w, :, g * group : (g + 1) * group], head_size, group)
        store(item, 2, nn(prob_ref[w, :, lanes], up))
        return nt(piece(item, 2), up)

    def soften(item, slot, gprobs):
        w, g = item
        lanes = slice(g * span, (g + 1) * span)
        probs = prob_ref[w, :, lanes].astype(F32)
        mean = jnp.sum(probs * gprobs, axis=0, keepdims=True)
        gscore = probs * (gprobs - mean)
        table_ref[0:WT, lanes] += gscore
        graw_ref[slot] = (gscore * scale).astype(BF)

    def descend(item, slot):
        graw = graw_ref[slot]
        store(item, 0, per_query(graw, piece(item, 1), head_size))
        store(item, 1, nn(graw, spread(piece(item, 0), head_size, group)))

    raws = {}
    for t in range(len(items) + 2):
        if t < len(items):
            raws[t] = ascend(items[t])
        if 1 <= t <= len(items):
            soften(items[t - 1], (t - 1) % 4, raws.pop(t - 1))
        if t >= 2:
            descend(items[t - 2], (t - 2) % 4)
    gjoint = wide_ref[...]
    sums_ref[...] += jnp.sum(gjoint, axis=0, keepdims=True)
    gjoint = gjoint.astype(BF)
    gact_ref[...] = gjoint
    acc_ref[...] += nn(hid_ref[...].T, gjoint)

    @pl.when(step == steps - 1)
    def _():
        shards = pack_ref.shape[0]
        deep = features // shards
        lanes = table_ref.shape[1] // shards
        total = sums_ref[0:1, :]
        by_acc = jnp.zeros((features, 128), F32)
        by_sum = jnp.zeros((features, 128), F32)
        for c in range(3 * features // 128):
            cols = slice(c * 128, (c + 1) * 128)
            weight = weight_ref[:, cols].astype(F32)
            by_acc = by_acc + weight * acc_ref[:, cols]
            by_sum = by_sum + weight * total[:, cols]
        by_acc = jnp.sum(by_acc.T, axis=0, keepdims=True)
        gshift = jnp.sum(by_sum.T, axis=0, keepdims=True)
        ggain = (by_acc - vec_ref[1:2, :] * gshift) / vec_ref[0:1, :]
        lines = jnp.concatenate(
            [
                ggain,
                gshift,
                total[:, :features],
                total[:, 2 * features :],
                jnp.zeros((LINES - 4, features), F32),
            ],
            axis=0,
        )
        for d in range(shards):
            pack_ref[d, 0:deep, :] = acc_ref[d * deep : (d + 1) * deep, :].astype(BF)
            pack_ref[d, deep : deep + LINES, :] = jnp.zeros((LINES, 3 * features), BF)
            for j in range(4):
                pack_ref[d, deep : deep + LINES, j * lanes : (j + 1) * lanes] = table_ref[
                    j * LINES : (j + 1) * LINES, d * lanes : (d + 1) * lanes
                ].astype(BF)
            own = slice(d * deep, (d + 1) * deep)
            at = features
            pack_ref[d, deep : deep + LINES, at : at + deep] = lines[:, own].astype(BF)
            at = features + features // 2
            pack_ref[d, deep : deep + LINES, at : at + deep] = sums_two_ref[:, own].astype(BF)
            at = 2 * features
            even = esum_ref.shape[1] // shards
            pack_ref[d, deep : deep + LINES, at : at + even] = esum_ref[
                :, d * even : (d + 1) * even
            ].astype(BF)


def close_kernel(
    gact_ref, xp_ref, gmid_ref, weight_ref, vec_ref, gtok_ref, grow_ref, gcol_ref, out_ref
):
    features = xp_ref.shape[-1]
    ghid = nt(gact_ref[...], weight_ref[:, : 3 * features])
    normed, inverse = norm_parts(xp_ref[...])
    out_ref[...] = gmid_ref[...] + norm_back(ghid, normed, inverse, vec_ref[0:1, :])
    deposit(pl.program_id(1), out_ref, gtok_ref, grow_ref, gcol_ref)


def patch_kernel(tile_ref, col_ref, row_ref, out_ref, flank_ref, top_ref, sems):
    images, breadth, _, _ = tile_ref.shape
    fetch = pltpu.make_async_copy(out_ref.at[:, SHIFT:, 0:PAD], top_ref, sems.at[0])
    fetch.start()
    flank_ref[...] = col_ref[...].astype(F32)
    for i in range(images):
        for c in range(SHIFT):
            for j in range(SHIFT):
                flank_ref[i, c, j : j + 1, :] = row_ref[i, j, c : c + 1, :]
    side = pltpu.make_async_copy(flank_ref, out_ref.at[:, 0:SHIFT], sems.at[1])
    side.start()
    fetch.wait()
    for i in range(images):
        for c in range(breadth - SHIFT):
            for j in range(SHIFT):
                top_ref[i, c, j : j + 1, :] = row_ref[i, j, c + SHIFT : c + SHIFT + 1, :]
    back = pltpu.make_async_copy(top_ref, out_ref.at[:, SHIFT:, 0:PAD], sems.at[2])
    back.start()
    side.wait()
    back.wait()


def shifted(block, axis, distance):
    count = lax.axis_size(axis)
    return lax.ppermute(block, axis, [((i - distance) % count, i) for i in range(count)])


def slanted(block, distance):
    rows, cols = lax.axis_size("row"), lax.axis_size("col")
    route = [
        (((r - distance) % rows) * cols + (c - distance) % cols, r * cols + c)
        for r in range(rows)
        for c in range(cols)
    ]
    return lax.ppermute(block, ("row", "col"), route)


def edge_kernel(first_ref, second_ref, row_ref, corner_ref, col_ref, flank, top, tidy, small, sems):
    tiles = (first_ref, second_ref)
    images, breadth = first_ref.shape[:2]
    copies = []
    for t, tile in enumerate(tiles):
        span = slice(t * images, (t + 1) * images)
        copies.append(
            pltpu.make_async_copy(tile.at[:, :, 0:PAD], top.at[span], sems.at[2 * t])
        )
        copies.append(
            pltpu.make_async_copy(tile.at[:, 0:SHIFT], flank.at[span], sems.at[2 * t + 1])
        )
    for copy in copies:
        copy.start()
    for t in range(2):
        span = slice(t * images, (t + 1) * images)
        copies[2 * t].wait()
        for i in range(t * images, (t + 1) * images):
            for c in range(breadth):
                for j in range(SHIFT):
                    if c < SHIFT:
                        small[i, j, c : c + 1, :] = top[i, c, j : j + 1, :]
                    else:
                        tidy[i, j, c - SHIFT : c - SHIFT + 1, :] = top[i, c, j : j + 1, :]
        copies[2 * t + 1].wait()
        col_ref[span] = flank[span].astype(BF)
    row_ref[...] = tidy[...].astype(BF)
    corner_ref[...] = small[...].astype(BF)


def roll_in(first, second):
    images, breadth, height, features = first.shape
    both = 2 * images
    vmem = pl.BlockSpec(memory_space=pltpu.VMEM)
    shapes = (
        (both, SHIFT, breadth - SHIFT, features),
        (both, SHIFT, SHIFT, features),
        (both, SHIFT, height, features),
    )
    row, corner, col = pl.pallas_call(
        edge_kernel,
        in_specs=[pl.BlockSpec(memory_space=pltpu.HBM)] * 2,
        out_specs=[vmem] * 3,
        out_shape=[jax.ShapeDtypeStruct(s, BF) for s in shapes],
        scratch_shapes=[
            pltpu.VMEM(shapes[2], F32),
            pltpu.VMEM((both, breadth, PAD, features), F32),
            pltpu.VMEM(shapes[0], F32),
            pltpu.VMEM(shapes[1], F32),
            pltpu.SemaphoreType.DMA((4,)),
        ],
        compiler_params=pltpu.CompilerParams(vmem_limit_bytes=24 * 1024 * 1024),
        cost_estimate=pl.CostEstimate(flops=0, bytes_accessed=5_000_000, transcendentals=0),
        name="edge",
    )(first, second)
    return shifted(row, "row", -1), slanted(corner, -1), shifted(col, "col", -1)


def roll_out(tile, rows, cols):
    images, breadth, height, features = tile.shape
    rows = rows.astype(BF)
    flank = shifted(cols.astype(BF), "col", 1)
    top = shifted(rows[:, :, : breadth - SHIFT], "row", 1)
    corner = slanted(rows[:, :, breadth - SHIFT :], 1)
    top = jnp.concatenate([corner, top], axis=2).astype(F32)
    vmem = pl.BlockSpec(memory_space=pltpu.VMEM)
    return pl.pallas_call(
        patch_kernel,
        in_specs=[pl.BlockSpec(memory_space=pl.ANY), vmem, vmem],
        out_specs=pl.BlockSpec(memory_space=pl.ANY),
        out_shape=jax.ShapeDtypeStruct(tile.shape, F32),
        scratch_shapes=[
            pltpu.VMEM((images, SHIFT, height, features), F32),
            pltpu.VMEM((images, breadth - SHIFT, PAD, features), F32),
            pltpu.SemaphoreType.DMA((3,)),
        ],
        input_output_aliases={0: 0},
        compiler_params=pltpu.CompilerParams(vmem_limit_bytes=24 * 1024 * 1024),
        cost_estimate=pl.CostEstimate(flops=0, bytes_accessed=4_000_000, transcendentals=0),
        name="patch",
    )(tile, flank, top)


def over_tiles(block):
    def added(part, axis):
        total = part.astype(F32)
        for step in range(1, lax.axis_size(axis)):
            total = total + shifted(part, axis, step).astype(F32)
        return total

    cut = block.shape[-1] // 2
    first = added(added(block[:, :cut], "row").astype(BF), "col")
    second = added(added(block[:, cut:], "col").astype(BF), "row")
    return jnp.concatenate([first, second], axis=1)


def region_band(places, count):
    return jnp.where(places < count - WIN, 0, jnp.where(places < count - SHIFT, 1, 2)).astype(
        jnp.int32
    )


def whole(shape):
    return pl.BlockSpec(shape, lambda i, j: (0,) * len(shape), pipeline_mode=pl.Buffered(1))


def body(
    tokens,
    position_index,
    first_gain,
    first_shift,
    joint_weight,
    query_bias,
    value_bias,
    position_table,
    output_weight,
    output_bias,
    second_gain,
    second_shift,
    expand_weight,
    expand_bias,
    shrink_weight,
    shrink_bias,
    cotangent,
):
    images, height, breadth, features = tokens.shape
    shards = lax.axis_size("dp")
    deep = joint_weight.shape[0]
    table_heads, table_rows = position_table.shape
    heads = table_heads * shards
    head_size = features // heads
    hidden_units = expand_weight.shape[1]
    blocks = hidden_units // features
    halves = height // (WIN * BANDS)
    grid = (images, halves)
    step_rows = 2 * BANDS * WT
    total_rows = images * halves * step_rows
    windows = images * halves * 2 * BANDS
    wide = heads * QL

    small = [
        first_gain,
        first_shift,
        query_bias,
        value_bias,
        output_bias,
        second_gain,
        second_shift,
        shrink_bias,
        expand_bias,
        position_table.reshape(-1),
    ]
    small = jnp.concatenate([s.astype(BF) for s in small])
    small = jnp.pad(small, (0, -small.shape[0] % 128))[None]
    small = lax.all_gather(small, "dp", axis=0, tiled=True)
    vec = small[:, : 8 * deep].reshape(shards, 8, deep).transpose(1, 0, 2).reshape(8, features)
    vec = vec.astype(F32)
    at = 8 * deep
    ebias = small[:, at : at + blocks * deep].reshape(1, hidden_units).astype(F32)
    at += blocks * deep
    table = small[:, at : at + table_heads * table_rows].reshape(heads, table_rows)
    weight_one = lax.all_gather(
        jnp.concatenate([joint_weight, output_weight], axis=1).astype(BF), "dp", axis=0, tiled=True
    )
    thick = jnp.concatenate(
        [shrink_weight[j * deep : (j + 1) * deep] for j in range(blocks)], axis=1
    )
    weight_two = lax.all_gather(
        jnp.concatenate([expand_weight, thick], axis=0).astype(BF)[None], "dp", axis=0, tiled=True
    )

    tokens, cotangent = tokens.transpose(0, 2, 1, 3), cotangent.transpose(0, 2, 1, 3)
    halo = roll_in(tokens, cotangent)

    paired = position_index.reshape(WIN, WIN, WIN, WIN)
    paired = paired.transpose(1, 0, 3, 2)
    paired = jnp.pad(paired, ((0, 0), (0, 1), (0, 0), (0, 1)), constant_values=-1)
    paired = jnp.pad(
        paired.reshape(WT, WT).T, ((0, 0), (0, QL - WT)), constant_values=-1
    ).reshape(-1)
    onehot = paired[None, :] == jnp.arange(table_rows, dtype=jnp.int32)[:, None]
    position = jnp.dot(table, onehot.astype(BF), preferred_element_type=F32)
    position = position.reshape(heads, WT, QL).transpose(1, 0, 2)
    grid_rows = height * lax.axis_size("row")
    grid_cols = breadth * lax.axis_size("col")
    row_places = jnp.stack([jnp.arange(WIN), jnp.arange(WIN) + height - WIN]).astype(jnp.int32)
    row_places = row_places + lax.axis_index("row") * height
    col_places = jnp.arange(2 * WIN, dtype=jnp.int32).reshape(2, WIN)
    col_places = col_places + lax.axis_index("col") * breadth
    row_label = jnp.pad(region_band(row_places, grid_rows), ((0, 0), (0, 1)))
    col_label = region_band(col_places, grid_cols)
    label = 3 * row_label[:, None, None, :] + col_label[None, :, :, None]
    label = label.reshape(2, 2, WT)
    label_q = jnp.pad(label, ((0, 0), (0, 0), (0, QL - WT)))
    masking = jnp.where(label[:, :, :, None] == label_q[:, :, None, :], 0.0, -100.0)
    absent = (jnp.arange(WT) % PAD == WIN)[:, None]
    masking = jnp.where(absent, FAR_BELOW, masking).astype(F32)
    bias = (position[None, None] + masking[:, :, :, None, :]).reshape(2, 2, WT, wide)

    tile_spec = pl.BlockSpec((1, breadth, height, features), lambda i, j: (i, 0, 0, 0))

    def halo_specs(first):
        sizes = (breadth - SHIFT, SHIFT, height)
        return [
            pl.BlockSpec((1, SHIFT, size, features), lambda i, j: (first + i, 0, 0, 0))
            for size in sizes
        ]

    row_spec = pl.BlockSpec((1, SHIFT, breadth, features), lambda i, j: (i, 0, 0, 0))
    col_spec = pl.BlockSpec((1, SHIFT, height, features), lambda i, j: (i, 0, 0, 0))
    flat_spec = pl.BlockSpec((step_rows, features), lambda i, j: (i * halves + j, 0))

    joint_spec = pl.BlockSpec((step_rows, 3 * features), lambda i, j: (i * halves + j, 0))

    def window_spec(last):
        return pl.BlockSpec((2 * BANDS, WT, last), lambda i, j: (i * halves + j, 0, 0))

    params = pltpu.CompilerParams(
        dimension_semantics=("arbitrary", "arbitrary"), vmem_limit_bytes=VMEM_LIMIT
    )
    shape = jax.ShapeDtypeStruct
    halo_scratch = [
        pltpu.VMEM((SHIFT, breadth, features), F32),
        pltpu.VMEM((SHIFT, height, features), F32),
    ]
    dense = 2 * total_rows * features * features

    xp, hidden_one, qkv, probs, attended, middle = pl.pallas_call(
        functools.partial(attend_kernel, head_size),
        grid=grid,
        in_specs=[
            tile_spec,
            *halo_specs(0),
            whole((features, 4 * features)),
            whole((8, features)),
            whole((2, 2, WT, wide)),
        ],
        out_specs=[
            flat_spec,
            flat_spec,
            window_spec(3 * features),
            window_spec(wide),
            flat_spec,
            flat_spec,
        ],
        out_shape=[
            shape((total_rows, features), F32),
            shape((total_rows, features), BF),
            shape((windows, WT, 3 * features), BF),
            shape((windows, WT, wide), BF),
            shape((total_rows, features), BF),
            shape((total_rows, features), F32),
        ],
        scratch_shapes=[pltpu.VMEM((step_rows, features), F32), *halo_scratch],
        compiler_params=params,
        cost_estimate=pl.CostEstimate(
            flops=6 * dense, bytes_accessed=40_000_000, transcendentals=windows * WT * wide
        ),
        name="attend",
    )(tokens, *halo, weight_one, vec, bias)

    packed_rows = 2 * deep + deep // blocks
    result, res_row, res_col, gmid, gatt, pack_two, sums_two, esum = pl.pallas_call(
        mlp_kernel,
        grid=grid,
        in_specs=[
            tile_spec,
            *halo_specs(images),
            flat_spec,
            flat_spec,
            whole((features, 4 * features)),
            whole((shards, 2 * deep, hidden_units)),
            whole((8, features)),
            whole((1, hidden_units)),
        ],
        out_specs=[
            tile_spec,
            row_spec,
            col_spec,
            flat_spec,
            window_spec(features),
            whole((shards, packed_rows, hidden_units)),
            whole((LINES, features)),
            whole((LINES, hidden_units)),
        ],
        out_shape=[
            shape(tokens.shape, F32),
            shape((images, SHIFT, breadth, features), F32),
            shape((images, SHIFT, height, features), F32),
            shape((total_rows, features), F32),
            shape((windows, WT, features), BF),
            shape((shards, packed_rows, hidden_units), BF),
            shape((LINES, features), F32),
            shape((LINES, hidden_units), F32),
        ],
        scratch_shapes=[
            pltpu.VMEM((step_rows, features), F32),
            pltpu.VMEM((features, hidden_units), BF),
            pltpu.VMEM((hidden_units, features), BF),
            pltpu.VMEM((features, hidden_units), F32),
            pltpu.VMEM((features, hidden_units), F32),
            pltpu.VMEM((features, features), F32),
            pltpu.VMEM((step_rows, features), F32),
            *halo_scratch,
        ],
        compiler_params=params,
        cost_estimate=pl.CostEstimate(
            flops=26 * dense,
            bytes_accessed=50_000_000,
            transcendentals=total_rows * hidden_units,
        ),
        name="mlp",
    )(
        cotangent,
        *halo,
        middle,
        attended,
        weight_one,
        weight_two,
        vec,
        ebias,
    )

    pack_two = lax.psum_scatter(pack_two, "dp", scatter_dimension=0, tiled=True)[0]
    final = roll_out(result, res_row, res_col)

    gact, pack_one = pl.pallas_call(
        functools.partial(back_kernel, head_size),
        grid=grid,
        in_specs=[
            flat_spec,
            window_spec(3 * features),
            window_spec(wide),
            window_spec(features),
            whole((features, 4 * features)),
            whole((8, features)),
            whole((LINES, features)),
            whole((LINES, hidden_units)),
        ],
        out_specs=[joint_spec, whole((shards, deep + LINES, 3 * features))],
        out_shape=[
            shape((total_rows, 3 * features), BF),
            shape((shards, deep + LINES, 3 * features), BF),
        ],
        scratch_shapes=[
            pltpu.VMEM((features, 3 * features), F32),
            pltpu.VMEM((step_rows, 3 * features), F32),
            pltpu.VMEM((1, 3 * features), F32),
            pltpu.VMEM((4 * LINES, wide), F32),
            pltpu.VMEM((4, WT, 256 // head_size * QL), BF),
        ],
        compiler_params=params,
        cost_estimate=pl.CostEstimate(
            flops=18 * dense, bytes_accessed=50_000_000, transcendentals=0
        ),
        name="back",
    )(hidden_one, qkv, probs, gatt, weight_one, vec, sums_two, esum)

    pack_one = lax.psum_scatter(pack_one, "dp", scatter_dimension=0, tiled=True)[0]

    gtok, gtok_row, gtok_col = pl.pallas_call(
        close_kernel,
        grid=grid,
        in_specs=[
            joint_spec,
            flat_spec,
            flat_spec,
            whole((features, 4 * features)),
            whole((8, features)),
        ],
        out_specs=[tile_spec, row_spec, col_spec],
        out_shape=[
            shape(tokens.shape, F32),
            shape((images, SHIFT, breadth, features), F32),
            shape((images, SHIFT, height, features), F32),
        ],
        scratch_shapes=[pltpu.VMEM((step_rows, features), F32)],
        compiler_params=params,
        cost_estimate=pl.CostEstimate(
            flops=6 * dense, bytes_accessed=30_000_000, transcendentals=0
        ),
        name="close",
    )(gact, xp, gmid, weight_one, vec)
    grad_tokens = roll_out(gtok, gtok_row, gtok_col)

    pack_two = over_tiles(pack_two)
    pack_one, pack_two, final, grad_tokens = lax.optimization_barrier(
        (pack_one, pack_two, final, grad_tokens)
    )
    pack_one = over_tiles(pack_one)
    grad_expand = pack_two[:deep]
    grad_shrink = jnp.concatenate(
        [pack_two[deep : 2 * deep, j * features : (j + 1) * features] for j in range(blocks)],
        axis=0,
    )
    base = 2 * deep
    grad_output = jnp.concatenate(
        [pack_two[base:, j * features : (j + 1) * features] for j in range(blocks)], axis=0
    )
    grad_joint = pack_one[:deep]
    lanes = table_heads * QL
    lines_one = pack_one[deep:, features : features + deep]
    at = features + features // 2
    lines_two = pack_one[deep:, at : at + deep]
    grad_expand_bias = pack_one[deep, 2 * features : 2 * features + blocks * deep]
    gtable = jnp.concatenate(
        [pack_one[deep:, j * lanes : (j + 1) * lanes] for j in range(4)], axis=0
    )[:WT]
    gtable = gtable.reshape(WT, table_heads, QL).transpose(1, 0, 2).reshape(table_heads, WT * QL)
    grad_position = lax.dot_general(
        gtable,
        onehot.astype(F32),
        (((1,), (1,)), ((), ())),
        precision=lax.Precision.HIGHEST,
        preferred_element_type=F32,
    )
    final, grad_tokens = final.transpose(0, 2, 1, 3), grad_tokens.transpose(0, 2, 1, 3)
    return (
        final,
        grad_tokens,
        lines_one[0],
        lines_one[1],
        grad_joint,
        lines_one[2],
        lines_one[3],
        grad_position,
        grad_output,
        lines_two[0],
        lines_two[1],
        lines_two[2],
        grad_expand,
        grad_expand_bias,
        grad_shrink,
        lines_two[3],
    )


def solution(mesh):
    tile = P("dp", "row", "col", None)
    flat = P("dp")
    wide = P("dp", None)

    return jax.shard_map(
        body,
        mesh=mesh,
        in_specs=(
            tile,
            P(),
            flat,
            flat,
            wide,
            flat,
            flat,
            wide,
            wide,
            flat,
            flat,
            flat,
            wide,
            flat,
            wide,
            flat,
            tile,
        ),
        out_specs=(
            tile,
            tile,
            flat,
            flat,
            wide,
            flat,
            flat,
            wide,
            wide,
            flat,
            flat,
            flat,
            wide,
            flat,
            wide,
            flat,
        ),
        check_vma=False,
    )
```

```python
import functools

import jax
import jax.numpy as jnp
from jax import lax
from jax.experimental import pallas as pl
from jax.experimental.pallas import tpu as pltpu
from jax.sharding import PartitionSpec as P


WIN = 7
SHIFT = 3
PAD = 8
WT = WIN * PAD
QL = 64
EPSILON = 1e-05
ROOT_HALF = 0.7071067811865476
NORMAL_PEAK = 0.3989422804014327
FAR_BELOW = -1000000000.0
BF = jnp.bfloat16
F32 = jnp.float32
BANDS = 4
LINES = 16
VMEM_LIMIT = 60 * 1024 * 1024


def nn(a, b):
    return lax.dot_general(a, b, (((1,), (0,)), ((), ())), preferred_element_type=F32)


def nt(a, b):
    return lax.dot_general(a, b, (((1,), (1,)), ((), ())), preferred_element_type=F32)


def tn(a, b):
    return lax.dot_general(a, b, (((0,), (0,)), ((), ())), preferred_element_type=F32)


def norm_parts(values):
    center = values - jnp.mean(values, axis=-1, keepdims=True)
    inverse = lax.rsqrt(jnp.mean(center * center, axis=-1, keepdims=True) + EPSILON)
    return center * inverse, inverse


def norm_back(upper, normed, inverse, scaling):
    scaled = upper * scaling
    return inverse * (
        scaled
        - jnp.mean(scaled, axis=-1, keepdims=True)
        - normed * jnp.mean(scaled * normed, axis=-1, keepdims=True)
    )


def row_of(band, col):
    return ((2 * band + col // WIN) * WIN + col % WIN) * PAD


def widen(half, row_ref, corner_ref, col_ref, rows_ref, cols_ref):
    @pl.when(half == 0)
    def _():
        own = row_ref.shape[2]
        rows_ref[:, 0:own, :] = row_ref[0].astype(F32)
        rows_ref[:, own : own + SHIFT, :] = corner_ref[0].astype(F32)
        cols_ref[...] = col_ref[0].astype(F32)


def extract(half, tile_ref, rows_ref, cols_ref, out_ref):
    _, breadth, height, features = tile_ref.shape
    zero = jnp.zeros((1, features), F32)
    for band in range(BANDS):
        for col in range(breadth):
            at = row_of(band, col)
            out_ref[at + WIN : at + PAD, :] = zero
    for place in range(height // (BANDS * WIN)):

        @pl.when(half == place)
        def _():
            for col in range(breadth):
                local = col < breadth - SHIFT
                for band in range(BANDS):
                    at = row_of(band, col)
                    start = (place * BANDS + band) * WIN + SHIFT
                    count = min(WIN, height - start)
                    rows = slice(start, start + count)
                    out_ref[at : at + count, :] = (
                        tile_ref[0, col + SHIFT, rows, :]
                        if local
                        else cols_ref[col + SHIFT - breadth, rows, :]
                    )
                    for j in range(WIN - count):
                        out_ref[at + count + j : at + count + j + 1, :] = rows_ref[
                            j, col : col + 1, :
                        ]


def deposit(half, src_ref, tile_ref, row_ref, col_ref):
    _, breadth, height, _ = tile_ref.shape
    for place in range(height // (BANDS * WIN)):

        @pl.when(half == place)
        def _():
            for col in range(breadth):
                local = col < breadth - SHIFT
                for band in range(BANDS):
                    at = row_of(band, col)
                    start = (place * BANDS + band) * WIN + SHIFT
                    count = min(WIN, height - start)
                    rows = slice(start, start + count)
                    if local:
                        tile_ref[0, col + SHIFT, rows, :] = src_ref[at : at + count, :]
                    else:
                        col_ref[0, col + SHIFT - breadth, rows, :] = src_ref[at : at + count, :]
                    for j in range(WIN - count):
                        row_ref[0, j, col : col + 1, :] = src_ref[
                            at + count + j : at + count + j + 1, :
                        ]


def spread(rows, head_size, lanes):
    heads = lanes // head_size
    rows = jnp.concatenate([rows, jnp.zeros((QL - WT, lanes), rows.dtype)], axis=0)
    lane = lax.broadcasted_iota(jnp.int32, (QL, lanes), 1) // head_size
    zero = jnp.zeros_like(rows)
    return jnp.concatenate([jnp.where(lane == h, rows, zero) for h in range(heads)], axis=0)


def collapse(wide, head_size, lanes):
    heads = lanes // head_size
    lane = lax.broadcasted_iota(jnp.int32, (WT, lanes), 1) // head_size
    out = wide[0:WT]
    for h in range(1, heads):
        out = jnp.where(lane == h, wide[h * QL : h * QL + WT], out)
    return out


def per_query(scores_low, feats, head_size):
    features = feats.shape[1]
    quad = 128 // head_size
    parts = []
    for g in range(features // 128):
        block = scores_low[:, g * quad * QL : (g + 1) * quad * QL]
        wide = tn(block, feats[:, g * 128 : (g + 1) * 128])
        parts.append(collapse(wide, head_size, 128))
    return jnp.concatenate(parts, axis=1)


def attend_kernel(
    head_size,
    tile_ref,
    row_ref,
    corner_ref,
    col_ref,
    weight_ref,
    vec_ref,
    bias_ref,
    xp_ref,
    hid_ref,
    qkv_ref,
    prob_ref,
    att_ref,
    mid_ref,
    wide_ref,
    rows_ref,
    cols_ref,
):
    half = pl.program_id(1)
    features = tile_ref.shape[-1]
    widen(half, row_ref, corner_ref, col_ref, rows_ref, cols_ref)
    extract(half, tile_ref, rows_ref, cols_ref, xp_ref)
    normed, _ = norm_parts(xp_ref[...])
    hidden = (normed * vec_ref[0:1, :] + vec_ref[1:2, :]).astype(BF)
    hid_ref[...] = hidden
    scale = head_size ** (-0.5)
    for part in range(3):
        got = nn(hidden, weight_ref[:, part * features : (part + 1) * features])
        if part == 0:
            got = got + vec_ref[2:3, :]
        if part == 2:
            got = got + vec_ref[3:4, :]
        qkv_ref[:, :, part * features : (part + 1) * features] = got.reshape(
            2 * BANDS, WT, features
        ).astype(BF)

    group = 256
    span = group // head_size * QL
    items = [(w, g) for w in range(2 * BANDS) for g in range(features // group)]

    def scores(item):
        w, g = item
        q = qkv_ref[w, :, g * group : (g + 1) * group]
        k = qkv_ref[w, :, features + g * group : features + (g + 1) * group]
        return nt(k, spread(q, head_size, group))

    def soften(item, raw):
        w, g = item
        edge = jnp.where(half == 0, 0, 1) if w // 2 == BANDS - 1 else 0
        score = raw * scale + bias_ref[edge, w % 2, :, g * span : (g + 1) * span]
        highest = jnp.max(score, axis=0, keepdims=True)
        grown = jnp.exp(score - highest)
        total = jnp.sum(grown, axis=0, keepdims=True)
        prob_ref[w, :, g * span : (g + 1) * span] = (grown * (1.0 / total)).astype(BF)

    def mix(item):
        w, g = item
        probs = prob_ref[w, :, g * span : (g + 1) * span]
        v = qkv_ref[w, :, 2 * features + g * group : 2 * features + (g + 1) * group]
        wide_ref[w * WT : (w + 1) * WT, g * group : (g + 1) * group] = per_query(
            probs, v, head_size
        )

    raws = {}
    for t in range(len(items) + 2):
        if t < len(items):
            raws[t] = scores(items[t])
        if 1 <= t <= len(items):
            soften(items[t - 1], raws.pop(t - 1))
        if t >= 2:
            mix(items[t - 2])
    attended = wide_ref[...].astype(BF)
    att_ref[...] = attended
    branch = nn(attended, weight_ref[:, 3 * features :]) + vec_ref[4:5, :]
    wide_ref[...] = xp_ref[...] + branch
    _, breadth, height, _ = tile_ref.shape
    for place in range(height // (BANDS * WIN)):

        @pl.when(half == place)
        def _():
            for col in range(breadth):
                for band in range(BANDS):
                    at = row_of(band, col)
                    to = col * height + (place * BANDS + band) * WIN
                    mid_ref[to : to + WIN, :] = wide_ref[at : at + WIN, :]


def mlp_kernel(
    tile_ref,
    row_ref,
    corner_ref,
    col_ref,
    mid_ref,
    packed_ref,
    vec_ref,
    ebias_ref,
    res_ref,
    resrow_ref,
    rescol_ref,
    gmid_ref,
    pack_ref,
    sums_ref,
    esum_ref,
    cot_ref,
    we_ref,
    ws_ref,
    ge_ref,
    gs_ref,
    out_ref,
    rows_ref,
    cols_ref,
    low_ref,
    hid_ref,
    act_ref,
    gbef_ref,
):
    step = pl.program_id(0)
    steps = pl.num_programs(0)
    _, breadth, height, features = tile_ref.shape
    hidden_units = we_ref.shape[1]
    shards = pack_ref.shape[0]
    deep = features // shards
    blocks = hidden_units // features
    total = breadth * height
    even = total // 256 * 256
    rest = total - even
    inner = height - SHIFT

    @pl.when(step == 0)
    def _():
        for d in range(shards):
            we_ref[d * deep : (d + 1) * deep, :] = packed_ref[d, 0:deep, :]
            for j in range(blocks):
                at = d * deep * blocks + j * deep
                ws_ref[at : at + deep, :] = packed_ref[
                    d, deep : 2 * deep, j * features : (j + 1) * features
                ]
        ge_ref[...] = jnp.zeros_like(ge_ref)
        gs_ref[...] = jnp.zeros_like(gs_ref)
        sums_ref[...] = jnp.zeros_like(sums_ref)
        esum_ref[...] = jnp.zeros_like(esum_ref)

    widen(0, row_ref, corner_ref, col_ref, rows_ref, cols_ref)
    for col in range(breadth):
        at = col * height
        cot_ref[at : at + inner, :] = (
            tile_ref[0, col + SHIFT, SHIFT:, :]
            if col < breadth - SHIFT
            else cols_ref[col + SHIFT - breadth, SHIFT:, :]
        )
        for j in range(SHIFT):
            cot_ref[at + inner + j : at + inner + j + 1, :] = rows_ref[j, col : col + 1, :]
    mid = mid_ref[...]
    normed, inverse = norm_parts(mid)
    hidden = (normed * vec_ref[5:6, :] + vec_ref[6:7, :]).astype(BF)
    low = cot_ref[...].astype(BF)
    hidden_t = hidden[:even].T
    low_t = low[:even].T
    kept = pl.ds(pl.multiple_of(step * rest, rest), rest)
    low_ref[kept, :] = low[even:]
    hid_ref[kept, :] = hidden[even:]
    out = mid + vec_ref[7:8, :]
    ghid = None
    chunk = features
    for c in range(hidden_units // chunk):
        cols = slice(c * chunk, (c + 1) * chunk)
        before = nn(hidden, we_ref[:, cols]) + ebias_ref[0:1, cols]
        phi = 0.5 * (1.0 + lax.erf(before * ROOT_HALF))
        slope = phi + before * (NORMAL_PEAK * jnp.exp(-0.5 * before * before))
        active = (before * phi).astype(BF)
        out = out + nn(active, ws_ref[cols, :])
        gbefore = nt(low, ws_ref[cols, :]) * slope
        esum_ref[0:1, cols] += jnp.sum(gbefore, axis=0, keepdims=True)
        gbefore = gbefore.astype(BF)
        back = nt(gbefore, we_ref[:, cols])
        ghid = back if ghid is None else ghid + back
        gs_ref[:, cols] += nn(low_t, active[:even])
        ge_ref[:, cols] += nn(hidden_t, gbefore[:even])
        act_ref[kept, cols] = active[even:]
        gbef_ref[kept, cols] = gbefore[even:]
    out_ref[...] = out
    for col in range(breadth):
        at = col * height
        if col < breadth - SHIFT:
            res_ref[0, col + SHIFT, SHIFT:, :] = out_ref[at : at + inner, :]
        else:
            rescol_ref[0, col + SHIFT - breadth, SHIFT:, :] = out_ref[at : at + inner, :]
        for j in range(SHIFT):
            resrow_ref[0, j, col : col + 1, :] = out_ref[at + inner + j : at + inner + j + 1, :]
    cot = cot_ref[...]
    gmid = cot + norm_back(ghid, normed, inverse, vec_ref[5:6, :])
    sums_ref[0:1, :] += jnp.sum(gmid, axis=0, keepdims=True)
    sums_ref[1:2, :] += jnp.sum(ghid * normed, axis=0, keepdims=True)
    sums_ref[2:3, :] += jnp.sum(ghid, axis=0, keepdims=True)
    sums_ref[3:4, :] += jnp.sum(cot, axis=0, keepdims=True)
    out_ref[...] = gmid
    zero = jnp.zeros((PAD - WIN, features), F32)
    for band in range(height // WIN):
        for col in range(breadth):
            at = row_of(band, col)
            src = col * height + band * WIN
            gmid_ref[at : at + WIN, :] = out_ref[src : src + WIN, :]
            gmid_ref[at + WIN : at + PAD, :] = zero

    @pl.when(step == steps - 1)
    def _():
        ge_ref[...] += nn(hid_ref[...].T, gbef_ref[...])
        gs_ref[...] += nn(low_ref[...].T, act_ref[...])
        for d in range(shards):
            pack_ref[d, 0:deep, :] = ge_ref[d * deep : (d + 1) * deep, :].astype(BF)
            for j in range(blocks):
                at = d * deep * blocks + j * deep
                if deep * 2 % 128 == 0 and j % 2 == 0:
                    both = gs_ref[:, at : at + 2 * deep].T
                    pack_ref[d, deep : 2 * deep, j * features : (j + 1) * features] = both[
                        :deep
                    ].astype(BF)
                    pack_ref[d, deep : 2 * deep, (j + 1) * features : (j + 2) * features] = both[
                        deep:
                    ].astype(BF)
                elif deep * 2 % 128 != 0:
                    pack_ref[d, deep : 2 * deep, j * features : (j + 1) * features] = (
                        gs_ref[:, at : at + deep].T.astype(BF)
                    )


def back_kernel(
    head_size,
    hid_ref,
    qkv_ref,
    prob_ref,
    att_ref,
    gmid_ref,
    weight_ref,
    vec_ref,
    sums_two_ref,
    esum_ref,
    gact_ref,
    pack_ref,
    acc_ref,
    wide_ref,
    sums_ref,
    table_ref,
    graw_ref,
    gatt_ref,
    go_ref,
):
    half = pl.program_id(1)
    step = pl.program_id(0) * pl.num_programs(1) + half
    steps = pl.num_programs(0) * pl.num_programs(1)
    features = hid_ref.shape[-1]
    scale = head_size ** (-0.5)

    @pl.when(step == 0)
    def _():
        acc_ref[...] = jnp.zeros_like(acc_ref)
        sums_ref[...] = jnp.zeros_like(sums_ref)
        table_ref[...] = jnp.zeros_like(table_ref)
        go_ref[...] = jnp.zeros_like(go_ref)

    gbranch = gmid_ref[...].astype(BF)
    gatt = nt(gbranch, weight_ref[:, 3 * features :])
    gatt_ref[...] = gatt.reshape(2 * BANDS, WT, features).astype(BF)
    go_ref[...] += nn(att_ref[...].T, gbranch)

    group = 256
    span = group // head_size * QL
    items = [(w, g) for w in range(2 * BANDS) for g in range(features // group)]

    def piece(item, part):
        w, g = item
        at = part * features + g * group
        return qkv_ref[w, :, at : at + group]

    def store(item, part, value):
        w, g = item
        at = part * features + g * group
        wide_ref[w * WT : (w + 1) * WT, at : at + group] = value

    def ascend(item):
        w, g = item
        lanes = slice(g * span, (g + 1) * span)
        up = spread(gatt_ref[w, :, g * group : (g + 1) * group], head_size, group)
        store(item, 2, nn(prob_ref[w, :, lanes], up))
        return nt(piece(item, 2), up)

    def soften(item, slot, gprobs):
        w, g = item
        lanes = slice(g * span, (g + 1) * span)
        probs = prob_ref[w, :, lanes].astype(F32)
        mean = jnp.sum(probs * gprobs, axis=0, keepdims=True)
        gscore = probs * (gprobs - mean)
        table_ref[0:WT, lanes] += gscore
        graw_ref[slot] = (gscore * scale).astype(BF)

    def descend(item, slot):
        graw = graw_ref[slot]
        store(item, 0, per_query(graw, piece(item, 1), head_size))
        store(item, 1, nn(graw, spread(piece(item, 0), head_size, group)))

    raws = {}
    for t in range(len(items) + 2):
        if t < len(items):
            raws[t] = ascend(items[t])
        if 1 <= t <= len(items):
            soften(items[t - 1], (t - 1) % 4, raws.pop(t - 1))
        if t >= 2:
            descend(items[t - 2], (t - 2) % 4)
    gjoint = wide_ref[...]
    sums_ref[...] += jnp.sum(gjoint, axis=0, keepdims=True)
    gjoint = gjoint.astype(BF)
    gact_ref[...] = gjoint
    acc_ref[...] += nn(hid_ref[...].T, gjoint)

    @pl.when(step == steps - 1)
    def _():
        shards = pack_ref.shape[0]
        deep = features // shards
        lanes = table_ref.shape[1] // shards
        total = sums_ref[0:1, :]
        by_acc = jnp.zeros((features, 128), F32)
        by_sum = jnp.zeros((features, 128), F32)
        for c in range(3 * features // 128):
            cols = slice(c * 128, (c + 1) * 128)
            weight = weight_ref[:, cols].astype(F32)
            by_acc = by_acc + weight * acc_ref[:, cols]
            by_sum = by_sum + weight * total[:, cols]
        by_acc = jnp.sum(by_acc.T, axis=0, keepdims=True)
        gshift = jnp.sum(by_sum.T, axis=0, keepdims=True)
        ggain = (by_acc - vec_ref[1:2, :] * gshift) / vec_ref[0:1, :]
        lines = jnp.concatenate(
            [
                ggain,
                gshift,
                total[:, :features],
                total[:, 2 * features :],
                jnp.zeros((LINES - 4, features), F32),
            ],
            axis=0,
        )
        for d in range(shards):
            own = slice(d * deep, (d + 1) * deep)
            pack_ref[d, 0:deep, : 3 * features] = acc_ref[own, :].astype(BF)
            pack_ref[d, 0:deep, 3 * features :] = go_ref[own, :].astype(BF)
            pack_ref[d, deep : deep + LINES, :] = jnp.zeros((LINES, 4 * features), BF)
            for j in range(4):
                pack_ref[d, deep : deep + LINES, j * lanes : (j + 1) * lanes] = table_ref[
                    j * LINES : (j + 1) * LINES, d * lanes : (d + 1) * lanes
                ].astype(BF)
            at = features
            pack_ref[d, deep : deep + LINES, at : at + deep] = lines[:, own].astype(BF)
            at = features + features // 2
            pack_ref[d, deep : deep + LINES, at : at + deep] = sums_two_ref[:, own].astype(BF)
            at = 2 * features
            even = esum_ref.shape[1] // shards
            pack_ref[d, deep : deep + LINES, at : at + even] = esum_ref[
                :, d * even : (d + 1) * even
            ].astype(BF)


def close_kernel(
    gact_ref, xp_ref, gmid_ref, weight_ref, vec_ref, gtok_ref, grow_ref, gcol_ref, out_ref
):
    features = xp_ref.shape[-1]
    ghid = nt(gact_ref[...], weight_ref[:, : 3 * features])
    normed, inverse = norm_parts(xp_ref[...])
    out_ref[...] = gmid_ref[...] + norm_back(ghid, normed, inverse, vec_ref[0:1, :])
    deposit(pl.program_id(1), out_ref, gtok_ref, grow_ref, gcol_ref)


def patch_kernel(tile_ref, col_ref, row_ref, out_ref, flank_ref, top_ref, sems):
    images, breadth, _, _ = tile_ref.shape
    fetch = pltpu.make_async_copy(out_ref.at[:, SHIFT:, 0:PAD], top_ref, sems.at[0])
    fetch.start()
    flank_ref[...] = col_ref[...].astype(F32)
    for i in range(images):
        for c in range(SHIFT):
            for j in range(SHIFT):
                flank_ref[i, c, j : j + 1, :] = row_ref[i, j, c : c + 1, :]
    side = pltpu.make_async_copy(flank_ref, out_ref.at[:, 0:SHIFT], sems.at[1])
    side.start()
    fetch.wait()
    for i in range(images):
        for c in range(breadth - SHIFT):
            for j in range(SHIFT):
                top_ref[i, c, j : j + 1, :] = row_ref[i, j, c + SHIFT : c + SHIFT + 1, :]
    back = pltpu.make_async_copy(top_ref, out_ref.at[:, SHIFT:, 0:PAD], sems.at[2])
    back.start()
    side.wait()
    back.wait()


def shifted(block, axis, distance):
    count = lax.axis_size(axis)
    return lax.ppermute(block, axis, [((i - distance) % count, i) for i in range(count)])


def slanted(block, distance):
    rows, cols = lax.axis_size("row"), lax.axis_size("col")
    route = [
        (((r - distance) % rows) * cols + (c - distance) % cols, r * cols + c)
        for r in range(rows)
        for c in range(cols)
    ]
    return lax.ppermute(block, ("row", "col"), route)


def edge_kernel(first_ref, second_ref, row_ref, corner_ref, col_ref, flank, top, tidy, small, sems):
    tiles = (first_ref, second_ref)
    images, breadth = first_ref.shape[:2]
    copies = []
    for t, tile in enumerate(tiles):
        span = slice(t * images, (t + 1) * images)
        copies.append(
            pltpu.make_async_copy(tile.at[:, :, 0:PAD], top.at[span], sems.at[2 * t])
        )
        copies.append(
            pltpu.make_async_copy(tile.at[:, 0:SHIFT], flank.at[span], sems.at[2 * t + 1])
        )
    for copy in copies:
        copy.start()
    for t in range(2):
        span = slice(t * images, (t + 1) * images)
        copies[2 * t].wait()
        for i in range(t * images, (t + 1) * images):
            for c in range(breadth):
                for j in range(SHIFT):
                    if c < SHIFT:
                        small[i, j, c : c + 1, :] = top[i, c, j : j + 1, :]
                    else:
                        tidy[i, j, c - SHIFT : c - SHIFT + 1, :] = top[i, c, j : j + 1, :]
        copies[2 * t + 1].wait()
        col_ref[span] = flank[span].astype(BF)
    row_ref[...] = tidy[...].astype(BF)
    corner_ref[...] = small[...].astype(BF)


def roll_in(first, second):
    images, breadth, height, features = first.shape
    both = 2 * images
    vmem = pl.BlockSpec(memory_space=pltpu.VMEM)
    shapes = (
        (both, SHIFT, breadth - SHIFT, features),
        (both, SHIFT, SHIFT, features),
        (both, SHIFT, height, features),
    )
    row, corner, col = pl.pallas_call(
        edge_kernel,
        in_specs=[pl.BlockSpec(memory_space=pltpu.HBM)] * 2,
        out_specs=[vmem] * 3,
        out_shape=[jax.ShapeDtypeStruct(s, BF) for s in shapes],
        scratch_shapes=[
            pltpu.VMEM(shapes[2], F32),
            pltpu.VMEM((both, breadth, PAD, features), F32),
            pltpu.VMEM(shapes[0], F32),
            pltpu.VMEM(shapes[1], F32),
            pltpu.SemaphoreType.DMA((4,)),
        ],
        compiler_params=pltpu.CompilerParams(vmem_limit_bytes=24 * 1024 * 1024),
        cost_estimate=pl.CostEstimate(flops=0, bytes_accessed=5_000_000, transcendentals=0),
        name="edge",
    )(first, second)
    return shifted(row, "row", -1), slanted(corner, -1), shifted(col, "col", -1)


def roll_out(tile, rows, cols):
    images, breadth, height, features = tile.shape
    rows = rows.astype(BF)
    flank = shifted(cols.astype(BF), "col", 1)
    top = shifted(rows[:, :, : breadth - SHIFT], "row", 1)
    corner = slanted(rows[:, :, breadth - SHIFT :], 1)
    top = jnp.concatenate([corner, top], axis=2).astype(F32)
    vmem = pl.BlockSpec(memory_space=pltpu.VMEM)
    return pl.pallas_call(
        patch_kernel,
        in_specs=[pl.BlockSpec(memory_space=pl.ANY), vmem, vmem],
        out_specs=pl.BlockSpec(memory_space=pl.ANY),
        out_shape=jax.ShapeDtypeStruct(tile.shape, F32),
        scratch_shapes=[
            pltpu.VMEM((images, SHIFT, height, features), F32),
            pltpu.VMEM((images, breadth - SHIFT, PAD, features), F32),
            pltpu.SemaphoreType.DMA((3,)),
        ],
        input_output_aliases={0: 0},
        compiler_params=pltpu.CompilerParams(vmem_limit_bytes=24 * 1024 * 1024),
        cost_estimate=pl.CostEstimate(flops=0, bytes_accessed=4_000_000, transcendentals=0),
        name="patch",
    )(tile, flank, top)


def over_tiles(block):
    def added(part, axis):
        total = part.astype(F32)
        for step in range(1, lax.axis_size(axis)):
            total = total + shifted(part, axis, step).astype(F32)
        return total

    cut = block.shape[-1] // 2
    first = added(added(block[:, :cut], "row").astype(BF), "col")
    second = added(added(block[:, cut:], "col").astype(BF), "row")
    return jnp.concatenate([first, second], axis=1)


def region_band(places, count):
    return jnp.where(places < count - WIN, 0, jnp.where(places < count - SHIFT, 1, 2)).astype(
        jnp.int32
    )


def whole(shape):
    return pl.BlockSpec(shape, lambda i, j: (0,) * len(shape), pipeline_mode=pl.Buffered(1))


def body(
    tokens,
    position_index,
    first_gain,
    first_shift,
    joint_weight,
    query_bias,
    value_bias,
    position_table,
    output_weight,
    output_bias,
    second_gain,
    second_shift,
    expand_weight,
    expand_bias,
    shrink_weight,
    shrink_bias,
    cotangent,
):
    images, height, breadth, features = tokens.shape
    shards = lax.axis_size("dp")
    deep = joint_weight.shape[0]
    table_heads, table_rows = position_table.shape
    heads = table_heads * shards
    head_size = features // heads
    hidden_units = expand_weight.shape[1]
    blocks = hidden_units // features
    halves = height // (WIN * BANDS)
    grid = (images, halves)
    step_rows = 2 * BANDS * WT
    total_rows = images * halves * step_rows
    windows = images * halves * 2 * BANDS
    wide = heads * QL

    small = [
        first_gain,
        first_shift,
        query_bias,
        value_bias,
        output_bias,
        second_gain,
        second_shift,
        shrink_bias,
        expand_bias,
        position_table.reshape(-1),
    ]
    small = jnp.concatenate([s.astype(BF) for s in small])
    small = jnp.pad(small, (0, -small.shape[0] % 128))[None]
    small = lax.all_gather(small, "dp", axis=0, tiled=True)
    vec = small[:, : 8 * deep].reshape(shards, 8, deep).transpose(1, 0, 2).reshape(8, features)
    vec = vec.astype(F32)
    at = 8 * deep
    ebias = small[:, at : at + blocks * deep].reshape(1, hidden_units).astype(F32)
    at += blocks * deep
    table = small[:, at : at + table_heads * table_rows].reshape(heads, table_rows)
    weight_one = lax.all_gather(
        jnp.concatenate([joint_weight, output_weight], axis=1).astype(BF), "dp", axis=0, tiled=True
    )
    thick = jnp.concatenate(
        [shrink_weight[j * deep : (j + 1) * deep] for j in range(blocks)], axis=1
    )
    weight_two = lax.all_gather(
        jnp.concatenate([expand_weight, thick], axis=0).astype(BF)[None], "dp", axis=0, tiled=True
    )

    tokens, cotangent = tokens.transpose(0, 2, 1, 3), cotangent.transpose(0, 2, 1, 3)
    halo = roll_in(tokens, cotangent)

    paired = position_index.reshape(WIN, WIN, WIN, WIN)
    paired = paired.transpose(1, 0, 3, 2)
    paired = jnp.pad(paired, ((0, 0), (0, 1), (0, 0), (0, 1)), constant_values=-1)
    paired = jnp.pad(
        paired.reshape(WT, WT).T, ((0, 0), (0, QL - WT)), constant_values=-1
    ).reshape(-1)
    onehot = paired[None, :] == jnp.arange(table_rows, dtype=jnp.int32)[:, None]
    position = jnp.dot(table, onehot.astype(BF), preferred_element_type=F32)
    position = position.reshape(heads, WT, QL).transpose(1, 0, 2)
    grid_rows = height * lax.axis_size("row")
    grid_cols = breadth * lax.axis_size("col")
    row_places = jnp.stack([jnp.arange(WIN), jnp.arange(WIN) + height - WIN]).astype(jnp.int32)
    row_places = row_places + lax.axis_index("row") * height
    col_places = jnp.arange(2 * WIN, dtype=jnp.int32).reshape(2, WIN)
    col_places = col_places + lax.axis_index("col") * breadth
    row_label = jnp.pad(region_band(row_places, grid_rows), ((0, 0), (0, 1)))
    col_label = region_band(col_places, grid_cols)
    label = 3 * row_label[:, None, None, :] + col_label[None, :, :, None]
    label = label.reshape(2, 2, WT)
    label_q = jnp.pad(label, ((0, 0), (0, 0), (0, QL - WT)))
    masking = jnp.where(label[:, :, :, None] == label_q[:, :, None, :], 0.0, -100.0)
    absent = (jnp.arange(WT) % PAD == WIN)[:, None]
    masking = jnp.where(absent, FAR_BELOW, masking).astype(F32)
    bias = (position[None, None] + masking[:, :, :, None, :]).reshape(2, 2, WT, wide)

    tile_spec = pl.BlockSpec((1, breadth, height, features), lambda i, j: (i, 0, 0, 0))

    def halo_specs(first):
        sizes = (breadth - SHIFT, SHIFT, height)
        return [
            pl.BlockSpec((1, SHIFT, size, features), lambda i, j: (first + i, 0, 0, 0))
            for size in sizes
        ]

    row_spec = pl.BlockSpec((1, SHIFT, breadth, features), lambda i, j: (i, 0, 0, 0))
    col_spec = pl.BlockSpec((1, SHIFT, height, features), lambda i, j: (i, 0, 0, 0))
    flat_spec = pl.BlockSpec((step_rows, features), lambda i, j: (i * halves + j, 0))

    joint_spec = pl.BlockSpec((step_rows, 3 * features), lambda i, j: (i * halves + j, 0))

    area = height * breadth
    image_spec = pl.BlockSpec((area, features), lambda i, j: (i, 0))
    padded_spec = pl.BlockSpec((halves * step_rows, features), lambda i, j: (i, 0))

    def window_spec(last):
        return pl.BlockSpec((2 * BANDS, WT, last), lambda i, j: (i * halves + j, 0, 0))

    params = pltpu.CompilerParams(
        dimension_semantics=("arbitrary", "arbitrary"), vmem_limit_bytes=VMEM_LIMIT
    )
    shape = jax.ShapeDtypeStruct
    halo_scratch = [
        pltpu.VMEM((SHIFT, breadth, features), F32),
        pltpu.VMEM((SHIFT, height, features), F32),
    ]
    dense = 2 * total_rows * features * features

    xp, hidden_one, qkv, probs, attended, middle = pl.pallas_call(
        functools.partial(attend_kernel, head_size),
        grid=grid,
        in_specs=[
            tile_spec,
            *halo_specs(0),
            whole((features, 4 * features)),
            whole((8, features)),
            whole((2, 2, WT, wide)),
        ],
        out_specs=[
            flat_spec,
            flat_spec,
            window_spec(3 * features),
            window_spec(wide),
            flat_spec,
            image_spec,
        ],
        out_shape=[
            shape((total_rows, features), F32),
            shape((total_rows, features), BF),
            shape((windows, WT, 3 * features), BF),
            shape((windows, WT, wide), BF),
            shape((total_rows, features), BF),
            shape((images * area, features), F32),
        ],
        scratch_shapes=[pltpu.VMEM((step_rows, features), F32), *halo_scratch],
        compiler_params=params,
        cost_estimate=pl.CostEstimate(
            flops=6 * dense, bytes_accessed=40_000_000, transcendentals=windows * WT * wide
        ),
        name="attend",
    )(tokens, *halo, weight_one, vec, bias)

    rest = images * (area % 256)
    result, res_row, res_col, gmid, pack_two, sums_two, esum = pl.pallas_call(
        mlp_kernel,
        grid=(images, 1),
        in_specs=[
            tile_spec,
            *halo_specs(images),
            image_spec,
            whole((shards, 2 * deep, hidden_units)),
            whole((8, features)),
            whole((1, hidden_units)),
        ],
        out_specs=[
            tile_spec,
            row_spec,
            col_spec,
            padded_spec,
            whole((shards, 2 * deep, hidden_units)),
            whole((LINES, features)),
            whole((LINES, hidden_units)),
        ],
        out_shape=[
            shape(tokens.shape, F32),
            shape((images, SHIFT, breadth, features), F32),
            shape((images, SHIFT, height, features), F32),
            shape((total_rows, features), F32),
            shape((shards, 2 * deep, hidden_units), BF),
            shape((LINES, features), F32),
            shape((LINES, hidden_units), F32),
        ],
        scratch_shapes=[
            pltpu.VMEM((area, features), F32),
            pltpu.VMEM((features, hidden_units), BF),
            pltpu.VMEM((hidden_units, features), BF),
            pltpu.VMEM((features, hidden_units), F32),
            pltpu.VMEM((features, hidden_units), F32),
            pltpu.VMEM((area, features), F32),
            *halo_scratch,
            pltpu.VMEM((rest, features), BF),
            pltpu.VMEM((rest, features), BF),
            pltpu.VMEM((rest, hidden_units), BF),
            pltpu.VMEM((rest, hidden_units), BF),
        ],
        compiler_params=params,
        cost_estimate=pl.CostEstimate(
            flops=24 * dense,
            bytes_accessed=50_000_000,
            transcendentals=total_rows * hidden_units,
        ),
        name="mlp",
    )(
        cotangent,
        *halo,
        middle,
        weight_two,
        vec,
        ebias,
    )

    pack_two = lax.psum_scatter(pack_two, "dp", scatter_dimension=0, tiled=True)[0]
    final = roll_out(result, res_row, res_col)

    gact, pack_one = pl.pallas_call(
        functools.partial(back_kernel, head_size),
        grid=grid,
        in_specs=[
            flat_spec,
            window_spec(3 * features),
            window_spec(wide),
            flat_spec,
            flat_spec,
            whole((features, 4 * features)),
            whole((8, features)),
            whole((LINES, features)),
            whole((LINES, hidden_units)),
        ],
        out_specs=[joint_spec, whole((shards, deep + LINES, 4 * features))],
        out_shape=[
            shape((total_rows, 3 * features), BF),
            shape((shards, deep + LINES, 4 * features), BF),
        ],
        scratch_shapes=[
            pltpu.VMEM((features, 3 * features), F32),
            pltpu.VMEM((step_rows, 3 * features), F32),
            pltpu.VMEM((1, 3 * features), F32),
            pltpu.VMEM((4 * LINES, wide), F32),
            pltpu.VMEM((4, WT, 256 // head_size * QL), BF),
            pltpu.VMEM((2 * BANDS, WT, features), BF),
            pltpu.VMEM((features, features), F32),
        ],
        compiler_params=params,
        cost_estimate=pl.CostEstimate(
            flops=18 * dense, bytes_accessed=50_000_000, transcendentals=0
        ),
        name="back",
    )(hidden_one, qkv, probs, attended, gmid, weight_one, vec, sums_two, esum)

    pack_one = lax.psum_scatter(pack_one, "dp", scatter_dimension=0, tiled=True)[0]

    gtok, gtok_row, gtok_col = pl.pallas_call(
        close_kernel,
        grid=grid,
        in_specs=[
            joint_spec,
            flat_spec,
            flat_spec,
            whole((features, 4 * features)),
            whole((8, features)),
        ],
        out_specs=[tile_spec, row_spec, col_spec],
        out_shape=[
            shape(tokens.shape, F32),
            shape((images, SHIFT, breadth, features), F32),
            shape((images, SHIFT, height, features), F32),
        ],
        scratch_shapes=[pltpu.VMEM((step_rows, features), F32)],
        compiler_params=params,
        cost_estimate=pl.CostEstimate(
            flops=6 * dense, bytes_accessed=30_000_000, transcendentals=0
        ),
        name="close",
    )(gact, xp, gmid, weight_one, vec)
    grad_tokens = roll_out(gtok, gtok_row, gtok_col)

    pack_two = over_tiles(pack_two)
    pack_one, pack_two, final, grad_tokens = lax.optimization_barrier(
        (pack_one, pack_two, final, grad_tokens)
    )
    pack_one = over_tiles(pack_one)
    grad_expand = pack_two[:deep]
    grad_shrink = jnp.concatenate(
        [pack_two[deep : 2 * deep, j * features : (j + 1) * features] for j in range(blocks)],
        axis=0,
    )
    grad_output = pack_one[:deep, 3 * features :]
    grad_joint = pack_one[:deep, : 3 * features]
    lanes = table_heads * QL
    lines_one = pack_one[deep:, features : features + deep]
    at = features + features // 2
    lines_two = pack_one[deep:, at : at + deep]
    grad_expand_bias = pack_one[deep, 2 * features : 2 * features + blocks * deep]
    gtable = jnp.concatenate(
        [pack_one[deep:, j * lanes : (j + 1) * lanes] for j in range(4)], axis=0
    )[:WT]
    gtable = gtable.reshape(WT, table_heads, QL).transpose(1, 0, 2).reshape(table_heads, WT * QL)
    grad_position = lax.dot_general(
        gtable,
        onehot.astype(F32),
        (((1,), (1,)), ((), ())),
        precision=lax.Precision.HIGHEST,
        preferred_element_type=F32,
    )
    final, grad_tokens = final.transpose(0, 2, 1, 3), grad_tokens.transpose(0, 2, 1, 3)
    return (
        final,
        grad_tokens,
        lines_one[0],
        lines_one[1],
        grad_joint,
        lines_one[2],
        lines_one[3],
        grad_position,
        grad_output,
        lines_two[0],
        lines_two[1],
        lines_two[2],
        grad_expand,
        grad_expand_bias,
        grad_shrink,
        lines_two[3],
    )


def solution(mesh):
    tile = P("dp", "row", "col", None)
    flat = P("dp")
    wide = P("dp", None)

    return jax.shard_map(
        body,
        mesh=mesh,
        in_specs=(
            tile,
            P(),
            flat,
            flat,
            wide,
            flat,
            flat,
            wide,
            wide,
            flat,
            flat,
            flat,
            wide,
            flat,
            wide,
            flat,
            tile,
        ),
        out_specs=(
            tile,
            tile,
            flat,
            flat,
            wide,
            flat,
            flat,
            wide,
            wide,
            flat,
            flat,
            flat,
            wide,
            flat,
            wide,
            flat,
        ),
        check_vma=False,
    )
```

```python
import functools

import jax
import jax.numpy as jnp
from jax import lax
from jax.experimental import pallas as pl
from jax.experimental.pallas import tpu as pltpu
from jax.sharding import PartitionSpec as P


WIN = 7
SHIFT = 3
PAD = 8
WT = WIN * PAD
QL = 64
EPSILON = 1e-05
ROOT_HALF = 0.7071067811865476
NORMAL_PEAK = 0.3989422804014327
FAR_BELOW = -1000000000.0
BF = jnp.bfloat16
F32 = jnp.float32
BANDS = 4
LINES = 8
VMEM_LIMIT = 60 * 1024 * 1024


def nn(a, b):
    return lax.dot_general(a, b, (((1,), (0,)), ((), ())), preferred_element_type=F32)


def nt(a, b):
    return lax.dot_general(a, b, (((1,), (1,)), ((), ())), preferred_element_type=F32)


def tn(a, b):
    return lax.dot_general(a, b, (((0,), (0,)), ((), ())), preferred_element_type=F32)


def norm_parts(values):
    center = values - jnp.mean(values, axis=-1, keepdims=True)
    inverse = lax.rsqrt(jnp.mean(center * center, axis=-1, keepdims=True) + EPSILON)
    return center * inverse, inverse


def norm_back(upper, normed, inverse, scaling):
    scaled = upper * scaling
    return inverse * (
        scaled
        - jnp.mean(scaled, axis=-1, keepdims=True)
        - normed * jnp.mean(scaled * normed, axis=-1, keepdims=True)
    )


def row_of(band, col):
    return ((2 * band + col // WIN) * WIN + col % WIN) * PAD


def widen(half, row_ref, corner_ref, col_ref, rows_ref, cols_ref):
    @pl.when(half == 0)
    def _():
        own = row_ref.shape[2]
        rows_ref[:, 0:own, :] = row_ref[0].astype(F32)
        rows_ref[:, own : own + SHIFT, :] = corner_ref[0].astype(F32)
        cols_ref[...] = col_ref[0].astype(F32)


def extract(half, tile_ref, rows_ref, cols_ref, out_ref):
    _, breadth, height, features = tile_ref.shape
    zero = jnp.zeros((1, features), F32)
    for band in range(BANDS):
        for col in range(breadth):
            at = row_of(band, col)
            out_ref[at + WIN : at + PAD, :] = zero
    for place in range(height // (BANDS * WIN)):

        @pl.when(half == place)
        def _():
            for col in range(breadth):
                local = col < breadth - SHIFT
                for band in range(BANDS):
                    at = row_of(band, col)
                    start = (place * BANDS + band) * WIN + SHIFT
                    count = min(WIN, height - start)
                    rows = slice(start, start + count)
                    out_ref[at : at + count, :] = (
                        tile_ref[0, col + SHIFT, rows, :]
                        if local
                        else cols_ref[col + SHIFT - breadth, rows, :]
                    )
                    for j in range(WIN - count):
                        out_ref[at + count + j : at + count + j + 1, :] = rows_ref[
                            j, col : col + 1, :
                        ]


def deposit(half, src_ref, tile_ref, row_ref, col_ref):
    _, breadth, height, _ = tile_ref.shape
    for place in range(height // (BANDS * WIN)):

        @pl.when(half == place)
        def _():
            for col in range(breadth):
                local = col < breadth - SHIFT
                for band in range(BANDS):
                    at = row_of(band, col)
                    start = (place * BANDS + band) * WIN + SHIFT
                    count = min(WIN, height - start)
                    rows = slice(start, start + count)
                    if local:
                        tile_ref[0, col + SHIFT, rows, :] = src_ref[at : at + count, :]
                    else:
                        col_ref[0, col + SHIFT - breadth, rows, :] = src_ref[at : at + count, :]
                    for j in range(WIN - count):
                        row_ref[0, j, col : col + 1, :] = src_ref[
                            at + count + j : at + count + j + 1, :
                        ]


def spread(rows, head_size, lanes):
    heads = lanes // head_size
    rows = jnp.concatenate([rows, jnp.zeros((QL - WT, lanes), rows.dtype)], axis=0)
    lane = lax.broadcasted_iota(jnp.int32, (QL, lanes), 1) // head_size
    zero = jnp.zeros_like(rows)
    return jnp.concatenate([jnp.where(lane == h, rows, zero) for h in range(heads)], axis=0)


def collapse(wide, head_size, lanes):
    heads = lanes // head_size
    lane = lax.broadcasted_iota(jnp.int32, (WT, lanes), 1) // head_size
    out = wide[0:WT]
    for h in range(1, heads):
        out = jnp.where(lane == h, wide[h * QL : h * QL + WT], out)
    return out


def per_query(scores_low, feats, head_size):
    features = feats.shape[1]
    quad = 128 // head_size
    parts = []
    for g in range(features // 128):
        block = scores_low[:, g * quad * QL : (g + 1) * quad * QL]
        wide = tn(block, feats[:, g * 128 : (g + 1) * 128])
        parts.append(collapse(wide, head_size, 128))
    return jnp.concatenate(parts, axis=1)


def attend_kernel(
    head_size,
    tile_ref,
    row_ref,
    corner_ref,
    col_ref,
    weight_ref,
    vec_ref,
    bias_ref,
    xp_ref,
    hid_ref,
    qkv_ref,
    prob_ref,
    att_ref,
    mid_ref,
    wide_ref,
    rows_ref,
    cols_ref,
):
    half = pl.program_id(1)
    features = tile_ref.shape[-1]
    widen(half, row_ref, corner_ref, col_ref, rows_ref, cols_ref)
    extract(half, tile_ref, rows_ref, cols_ref, xp_ref)
    normed, _ = norm_parts(xp_ref[...])
    hidden = (normed * vec_ref[0:1, :] + vec_ref[1:2, :]).astype(BF)
    hid_ref[...] = hidden
    scale = head_size ** (-0.5)
    for part in range(3):
        got = nn(hidden, weight_ref[:, part * features : (part + 1) * features])
        if part == 0:
            got = got + vec_ref[2:3, :]
        if part == 2:
            got = got + vec_ref[3:4, :]
        qkv_ref[:, :, part * features : (part + 1) * features] = got.reshape(
            2 * BANDS, WT, features
        ).astype(BF)

    group = 256
    span = group // head_size * QL
    items = [(w, g) for w in range(2 * BANDS) for g in range(features // group)]

    def scores(item):
        w, g = item
        q = qkv_ref[w, :, g * group : (g + 1) * group]
        k = qkv_ref[w, :, features + g * group : features + (g + 1) * group]
        return nt(k, spread(q, head_size, group))

    def soften(item, raw):
        w, g = item
        edge = jnp.where(half == 0, 0, 1) if w // 2 == BANDS - 1 else 0
        score = raw * scale + bias_ref[edge, w % 2, :, g * span : (g + 1) * span]
        highest = jnp.max(score, axis=0, keepdims=True)
        grown = jnp.exp(score - highest)
        total = jnp.sum(grown, axis=0, keepdims=True)
        prob_ref[w, :, g * span : (g + 1) * span] = (grown * (1.0 / total)).astype(BF)

    def mix(item):
        w, g = item
        probs = prob_ref[w, :, g * span : (g + 1) * span]
        v = qkv_ref[w, :, 2 * features + g * group : 2 * features + (g + 1) * group]
        wide_ref[w * WT : (w + 1) * WT, g * group : (g + 1) * group] = per_query(
            probs, v, head_size
        )

    raws = {}
    for t in range(len(items) + 2):
        if t < len(items):
            raws[t] = scores(items[t])
        if 1 <= t <= len(items):
            soften(items[t - 1], raws.pop(t - 1))
        if t >= 2:
            mix(items[t - 2])
    attended = wide_ref[...].astype(BF)
    att_ref[...] = attended
    branch = nn(attended, weight_ref[:, 3 * features :]) + vec_ref[4:5, :]
    wide_ref[...] = xp_ref[...] + branch
    _, breadth, height, _ = tile_ref.shape
    for place in range(height // (BANDS * WIN)):

        @pl.when(half == place)
        def _():
            for col in range(breadth):
                for band in range(BANDS):
                    at = row_of(band, col)
                    to = col * height + (place * BANDS + band) * WIN
                    mid_ref[to : to + WIN, :] = wide_ref[at : at + WIN, :]


def mlp_kernel(
    tile_ref,
    row_ref,
    corner_ref,
    col_ref,
    mid_ref,
    packed_ref,
    vec_ref,
    ebias_ref,
    res_ref,
    resrow_ref,
    rescol_ref,
    gmid_ref,
    pack_ref,
    sums_ref,
    esum_ref,
    cot_ref,
    we_ref,
    ws_ref,
    ge_ref,
    gs_ref,
    out_ref,
    rows_ref,
    cols_ref,
    low_ref,
    hid_ref,
    act_ref,
    gbef_ref,
):
    step = pl.program_id(0)
    steps = pl.num_programs(0)
    _, breadth, height, features = tile_ref.shape
    hidden_units = we_ref.shape[1]
    shards = pack_ref.shape[0]
    deep = features // shards
    blocks = hidden_units // features
    total = breadth * height
    even = total // 256 * 256
    rest = total - even
    inner = height - SHIFT

    @pl.when(step == 0)
    def _():
        for d in range(shards):
            we_ref[d * deep : (d + 1) * deep, :] = packed_ref[d, 0:deep, :]
            for j in range(blocks):
                at = d * deep * blocks + j * deep
                ws_ref[at : at + deep, :] = packed_ref[
                    d, deep : 2 * deep, j * features : (j + 1) * features
                ]
        ge_ref[...] = jnp.zeros_like(ge_ref)
        gs_ref[...] = jnp.zeros_like(gs_ref)
        sums_ref[...] = jnp.zeros_like(sums_ref)
        esum_ref[...] = jnp.zeros_like(esum_ref)

    widen(0, row_ref, corner_ref, col_ref, rows_ref, cols_ref)
    for col in range(breadth):
        at = col * height
        cot_ref[at : at + inner, :] = (
            tile_ref[0, col + SHIFT, SHIFT:, :]
            if col < breadth - SHIFT
            else cols_ref[col + SHIFT - breadth, SHIFT:, :]
        )
        for j in range(SHIFT):
            cot_ref[at + inner + j : at + inner + j + 1, :] = rows_ref[j, col : col + 1, :]
    mid = mid_ref[...]
    normed, inverse = norm_parts(mid)
    hidden = (normed * vec_ref[5:6, :] + vec_ref[6:7, :]).astype(BF)
    low = cot_ref[...].astype(BF)
    hidden_t = hidden[:even].T
    low_t = low[:even].T
    kept = pl.ds(pl.multiple_of(step * rest, rest), rest)
    low_ref[kept, :] = low[even:]
    hid_ref[kept, :] = hidden[even:]
    out = mid + vec_ref[7:8, :]
    ghid = None
    chunk = features
    for c in range(hidden_units // chunk):
        cols = slice(c * chunk, (c + 1) * chunk)
        before = nn(hidden, we_ref[:, cols]) + ebias_ref[0:1, cols]
        phi = 0.5 * (1.0 + lax.erf(before * ROOT_HALF))
        slope = phi + before * (NORMAL_PEAK * jnp.exp(-0.5 * before * before))
        active = (before * phi).astype(BF)
        out = out + nn(active, ws_ref[cols, :])
        gbefore = nt(low, ws_ref[cols, :]) * slope
        esum_ref[0:1, cols] += jnp.sum(gbefore, axis=0, keepdims=True)
        gbefore = gbefore.astype(BF)
        back = nt(gbefore, we_ref[:, cols])
        ghid = back if ghid is None else ghid + back
        gs_ref[:, cols] += nn(low_t, active[:even])
        ge_ref[:, cols] += nn(hidden_t, gbefore[:even])
        act_ref[kept, cols] = active[even:]
        gbef_ref[kept, cols] = gbefore[even:]
    out_ref[...] = out
    for col in range(breadth):
        at = col * height
        if col < breadth - SHIFT:
            res_ref[0, col + SHIFT, SHIFT:, :] = out_ref[at : at + inner, :]
        else:
            rescol_ref[0, col + SHIFT - breadth, SHIFT:, :] = out_ref[at : at + inner, :]
        for j in range(SHIFT):
            resrow_ref[0, j, col : col + 1, :] = out_ref[at + inner + j : at + inner + j + 1, :]
    cot = cot_ref[...]
    gmid = cot + norm_back(ghid, normed, inverse, vec_ref[5:6, :])
    sums_ref[0:1, :] += jnp.sum(gmid, axis=0, keepdims=True)
    sums_ref[1:2, :] += jnp.sum(ghid * normed, axis=0, keepdims=True)
    sums_ref[2:3, :] += jnp.sum(ghid, axis=0, keepdims=True)
    sums_ref[3:4, :] += jnp.sum(cot, axis=0, keepdims=True)
    out_ref[...] = gmid
    zero = jnp.zeros((PAD - WIN, features), F32)
    for band in range(height // WIN):
        for col in range(breadth):
            at = row_of(band, col)
            src = col * height + band * WIN
            gmid_ref[at : at + WIN, :] = out_ref[src : src + WIN, :]
            gmid_ref[at + WIN : at + PAD, :] = zero

    @pl.when(step == steps - 1)
    def _():
        ge_ref[...] += nn(hid_ref[...].T, gbef_ref[...])
        gs_ref[...] += nn(low_ref[...].T, act_ref[...])
        for d in range(shards):
            pack_ref[d, 0:deep, :] = ge_ref[d * deep : (d + 1) * deep, :].astype(BF)
            for j in range(blocks):
                at = d * deep * blocks + j * deep
                if deep * 2 % 128 == 0 and j % 2 == 0:
                    both = gs_ref[:, at : at + 2 * deep].T
                    pack_ref[d, deep : 2 * deep, j * features : (j + 1) * features] = both[
                        :deep
                    ].astype(BF)
                    pack_ref[d, deep : 2 * deep, (j + 1) * features : (j + 2) * features] = both[
                        deep:
                    ].astype(BF)
                elif deep * 2 % 128 != 0:
                    pack_ref[d, deep : 2 * deep, j * features : (j + 1) * features] = (
                        gs_ref[:, at : at + deep].T.astype(BF)
                    )


def back_kernel(
    head_size,
    hid_ref,
    qkv_ref,
    prob_ref,
    att_ref,
    gmid_ref,
    weight_ref,
    vec_ref,
    sums_two_ref,
    esum_ref,
    gact_ref,
    pack_ref,
    acc_ref,
    wide_ref,
    sums_ref,
    table_ref,
    graw_ref,
    gatt_ref,
    go_ref,
):
    half = pl.program_id(1)
    step = pl.program_id(0) * pl.num_programs(1) + half
    steps = pl.num_programs(0) * pl.num_programs(1)
    features = hid_ref.shape[-1]
    scale = head_size ** (-0.5)

    @pl.when(step == 0)
    def _():
        acc_ref[...] = jnp.zeros_like(acc_ref)
        sums_ref[...] = jnp.zeros_like(sums_ref)
        table_ref[...] = jnp.zeros_like(table_ref)
        go_ref[...] = jnp.zeros_like(go_ref)

    gbranch = gmid_ref[...].astype(BF)
    gatt = nt(gbranch, weight_ref[:, 3 * features :])
    gatt_ref[...] = gatt.reshape(2 * BANDS, WT, features).astype(BF)
    go_ref[...] += nn(att_ref[...].T, gbranch)

    group = 256
    span = group // head_size * QL
    items = [(w, g) for w in range(2 * BANDS) for g in range(features // group)]

    def piece(item, part):
        w, g = item
        at = part * features + g * group
        return qkv_ref[w, :, at : at + group]

    def store(item, part, value):
        w, g = item
        at = part * features + g * group
        wide_ref[w * WT : (w + 1) * WT, at : at + group] = value

    def ascend(item):
        w, g = item
        lanes = slice(g * span, (g + 1) * span)
        up = spread(gatt_ref[w, :, g * group : (g + 1) * group], head_size, group)
        store(item, 2, nn(prob_ref[w, :, lanes], up))
        return nt(piece(item, 2), up)

    def soften(item, slot, gprobs):
        w, g = item
        lanes = slice(g * span, (g + 1) * span)
        probs = prob_ref[w, :, lanes].astype(F32)
        mean = jnp.sum(probs * gprobs, axis=0, keepdims=True)
        gscore = probs * (gprobs - mean)
        table_ref[0:WT, lanes] += gscore
        graw_ref[slot] = (gscore * scale).astype(BF)

    def descend(item, slot):
        graw = graw_ref[slot]
        store(item, 0, per_query(graw, piece(item, 1), head_size))
        store(item, 1, nn(graw, spread(piece(item, 0), head_size, group)))

    raws = {}
    for t in range(len(items) + 2):
        if t < len(items):
            raws[t] = ascend(items[t])
        if 1 <= t <= len(items):
            soften(items[t - 1], (t - 1) % 4, raws.pop(t - 1))
        if t >= 2:
            descend(items[t - 2], (t - 2) % 4)
    gjoint = wide_ref[...]
    sums_ref[...] += jnp.sum(gjoint, axis=0, keepdims=True)
    gjoint = gjoint.astype(BF)
    gact_ref[...] = gjoint
    acc_ref[...] += nn(hid_ref[...].T, gjoint)

    @pl.when(step == steps - 1)
    def _():
        shards = pack_ref.shape[0]
        deep = features // shards
        lanes = table_ref.shape[1] // shards
        total = sums_ref[0:1, :]
        by_acc = jnp.zeros((features, 128), F32)
        by_sum = jnp.zeros((features, 128), F32)
        for c in range(3 * features // 128):
            cols = slice(c * 128, (c + 1) * 128)
            weight = weight_ref[:, cols].astype(F32)
            by_acc = by_acc + weight * acc_ref[:, cols]
            by_sum = by_sum + weight * total[:, cols]
        by_acc = jnp.sum(by_acc.T, axis=0, keepdims=True)
        gshift = jnp.sum(by_sum.T, axis=0, keepdims=True)
        ggain = (by_acc - vec_ref[1:2, :] * gshift) / vec_ref[0:1, :]
        lines = jnp.concatenate(
            [
                ggain,
                gshift,
                total[:, :features],
                total[:, 2 * features :],
                jnp.zeros((LINES - 4, features), F32),
            ],
            axis=0,
        )
        for d in range(shards):
            own = slice(d * deep, (d + 1) * deep)
            pack_ref[d, 0:deep, : 3 * features] = acc_ref[own, :].astype(BF)
            pack_ref[d, 0:deep, 3 * features :] = go_ref[own, :].astype(BF)
            pack_ref[d, deep : deep + LINES, :] = jnp.zeros((LINES, 4 * features), BF)
            for j in range(QL // LINES):
                pack_ref[d, deep : deep + LINES, j * lanes : (j + 1) * lanes] = table_ref[
                    j * LINES : (j + 1) * LINES, d * lanes : (d + 1) * lanes
                ].astype(BF)
            at = 2 * features
            pack_ref[d, deep : deep + LINES, at : at + deep] = lines[:, own].astype(BF)
            at = 2 * features + features // 2
            pack_ref[d, deep : deep + LINES, at : at + deep] = sums_two_ref[:, own].astype(BF)
            at = 3 * features
            even = esum_ref.shape[1] // shards
            pack_ref[d, deep : deep + LINES, at : at + even] = esum_ref[
                :, d * even : (d + 1) * even
            ].astype(BF)


def close_kernel(
    gact_ref, xp_ref, gmid_ref, weight_ref, vec_ref, gtok_ref, grow_ref, gcol_ref, out_ref
):
    features = xp_ref.shape[-1]
    ghid = nt(gact_ref[...], weight_ref[:, : 3 * features])
    normed, inverse = norm_parts(xp_ref[...])
    out_ref[...] = gmid_ref[...] + norm_back(ghid, normed, inverse, vec_ref[0:1, :])
    deposit(pl.program_id(1), out_ref, gtok_ref, grow_ref, gcol_ref)


def patch_kernel(tile_ref, col_ref, row_ref, out_ref, flank_ref, top_ref, sems):
    images, breadth, _, _ = tile_ref.shape
    fetch = pltpu.make_async_copy(out_ref.at[:, SHIFT:, 0:PAD], top_ref, sems.at[0])
    fetch.start()
    flank_ref[...] = col_ref[...].astype(F32)
    for i in range(images):
        for c in range(SHIFT):
            for j in range(SHIFT):
                flank_ref[i, c, j : j + 1, :] = row_ref[i, j, c : c + 1, :]
    side = pltpu.make_async_copy(flank_ref, out_ref.at[:, 0:SHIFT], sems.at[1])
    side.start()
    fetch.wait()
    for i in range(images):
        for c in range(breadth - SHIFT):
            for j in range(SHIFT):
                top_ref[i, c, j : j + 1, :] = row_ref[i, j, c + SHIFT : c + SHIFT + 1, :]
    back = pltpu.make_async_copy(top_ref, out_ref.at[:, SHIFT:, 0:PAD], sems.at[2])
    back.start()
    side.wait()
    back.wait()


def shifted(block, axis, distance):
    count = lax.axis_size(axis)
    return lax.ppermute(block, axis, [((i - distance) % count, i) for i in range(count)])


def slanted(block, distance):
    rows, cols = lax.axis_size("row"), lax.axis_size("col")
    route = [
        (((r - distance) % rows) * cols + (c - distance) % cols, r * cols + c)
        for r in range(rows)
        for c in range(cols)
    ]
    return lax.ppermute(block, ("row", "col"), route)


def edge_kernel(first_ref, second_ref, row_ref, corner_ref, col_ref, flank, top, tidy, small, sems):
    tiles = (first_ref, second_ref)
    images, breadth = first_ref.shape[:2]
    copies = []
    for t, tile in enumerate(tiles):
        span = slice(t * images, (t + 1) * images)
        copies.append(
            pltpu.make_async_copy(tile.at[:, :, 0:PAD], top.at[span], sems.at[2 * t])
        )
        copies.append(
            pltpu.make_async_copy(tile.at[:, 0:SHIFT], flank.at[span], sems.at[2 * t + 1])
        )
    for copy in copies:
        copy.start()
    for t in range(2):
        span = slice(t * images, (t + 1) * images)
        copies[2 * t].wait()
        for i in range(t * images, (t + 1) * images):
            for c in range(breadth):
                for j in range(SHIFT):
                    if c < SHIFT:
                        small[i, j, c : c + 1, :] = top[i, c, j : j + 1, :]
                    else:
                        tidy[i, j, c - SHIFT : c - SHIFT + 1, :] = top[i, c, j : j + 1, :]
        copies[2 * t + 1].wait()
        col_ref[span] = flank[span].astype(BF)
    row_ref[...] = tidy[...].astype(BF)
    corner_ref[...] = small[...].astype(BF)


def roll_in(first, second):
    images, breadth, height, features = first.shape
    both = 2 * images
    vmem = pl.BlockSpec(memory_space=pltpu.VMEM)
    shapes = (
        (both, SHIFT, breadth - SHIFT, features),
        (both, SHIFT, SHIFT, features),
        (both, SHIFT, height, features),
    )
    row, corner, col = pl.pallas_call(
        edge_kernel,
        in_specs=[pl.BlockSpec(memory_space=pltpu.HBM)] * 2,
        out_specs=[vmem] * 3,
        out_shape=[jax.ShapeDtypeStruct(s, BF) for s in shapes],
        scratch_shapes=[
            pltpu.VMEM(shapes[2], F32),
            pltpu.VMEM((both, breadth, PAD, features), F32),
            pltpu.VMEM(shapes[0], F32),
            pltpu.VMEM(shapes[1], F32),
            pltpu.SemaphoreType.DMA((4,)),
        ],
        compiler_params=pltpu.CompilerParams(vmem_limit_bytes=24 * 1024 * 1024),
        cost_estimate=pl.CostEstimate(flops=0, bytes_accessed=5_000_000, transcendentals=0),
        name="edge",
    )(first, second)
    return shifted(row, "row", -1), slanted(corner, -1), shifted(col, "col", -1)


def roll_out(tile, rows, cols):
    images, breadth, height, features = tile.shape
    rows = rows.astype(BF)
    flank = shifted(cols.astype(BF), "col", 1)
    top = shifted(rows[:, :, : breadth - SHIFT], "row", 1)
    corner = slanted(rows[:, :, breadth - SHIFT :], 1)
    top = jnp.concatenate([corner, top], axis=2).astype(F32)
    vmem = pl.BlockSpec(memory_space=pltpu.VMEM)
    return pl.pallas_call(
        patch_kernel,
        in_specs=[pl.BlockSpec(memory_space=pl.ANY), vmem, vmem],
        out_specs=pl.BlockSpec(memory_space=pl.ANY),
        out_shape=jax.ShapeDtypeStruct(tile.shape, F32),
        scratch_shapes=[
            pltpu.VMEM((images, SHIFT, height, features), F32),
            pltpu.VMEM((images, breadth - SHIFT, PAD, features), F32),
            pltpu.SemaphoreType.DMA((3,)),
        ],
        input_output_aliases={0: 0},
        compiler_params=pltpu.CompilerParams(vmem_limit_bytes=24 * 1024 * 1024),
        cost_estimate=pl.CostEstimate(flops=0, bytes_accessed=4_000_000, transcendentals=0),
        name="patch",
    )(tile, flank, top)


def over_tiles(block):
    def added(part, axis):
        total = part.astype(F32)
        for step in range(1, lax.axis_size(axis)):
            total = total + shifted(part, axis, step).astype(F32)
        return total

    cut = block.shape[-1] // 2
    first = added(added(block[:, :cut], "row").astype(BF), "col")
    second = added(added(block[:, cut:], "col").astype(BF), "row")
    return jnp.concatenate([first, second], axis=1)


def region_band(places, count):
    return jnp.where(places < count - WIN, 0, jnp.where(places < count - SHIFT, 1, 2)).astype(
        jnp.int32
    )


def whole(shape):
    return pl.BlockSpec(shape, lambda i, j: (0,) * len(shape), pipeline_mode=pl.Buffered(1))


def body(
    tokens,
    position_index,
    first_gain,
    first_shift,
    joint_weight,
    query_bias,
    value_bias,
    position_table,
    output_weight,
    output_bias,
    second_gain,
    second_shift,
    expand_weight,
    expand_bias,
    shrink_weight,
    shrink_bias,
    cotangent,
):
    images, height, breadth, features = tokens.shape
    shards = lax.axis_size("dp")
    deep = joint_weight.shape[0]
    table_heads, table_rows = position_table.shape
    heads = table_heads * shards
    head_size = features // heads
    hidden_units = expand_weight.shape[1]
    blocks = hidden_units // features
    halves = height // (WIN * BANDS)
    grid = (images, halves)
    step_rows = 2 * BANDS * WT
    total_rows = images * halves * step_rows
    windows = images * halves * 2 * BANDS
    wide = heads * QL

    small = [
        first_gain,
        first_shift,
        query_bias,
        value_bias,
        output_bias,
        second_gain,
        second_shift,
        shrink_bias,
        expand_bias,
        position_table.reshape(-1),
    ]
    small = jnp.concatenate([s.astype(BF) for s in small])
    small = jnp.pad(small, (0, -small.shape[0] % 128))[None]
    small = lax.all_gather(small, "dp", axis=0, tiled=True)
    vec = small[:, : 8 * deep].reshape(shards, 8, deep).transpose(1, 0, 2).reshape(8, features)
    vec = vec.astype(F32)
    at = 8 * deep
    ebias = small[:, at : at + blocks * deep].reshape(1, hidden_units).astype(F32)
    at += blocks * deep
    table = small[:, at : at + table_heads * table_rows].reshape(heads, table_rows)
    weight_one = lax.all_gather(
        jnp.concatenate([joint_weight, output_weight], axis=1).astype(BF), "dp", axis=0, tiled=True
    )
    thick = jnp.concatenate(
        [shrink_weight[j * deep : (j + 1) * deep] for j in range(blocks)], axis=1
    )
    weight_two = lax.all_gather(
        jnp.concatenate([expand_weight, thick], axis=0).astype(BF)[None], "dp", axis=0, tiled=True
    )

    tokens, cotangent = tokens.transpose(0, 2, 1, 3), cotangent.transpose(0, 2, 1, 3)
    halo = roll_in(tokens, cotangent)

    paired = position_index.reshape(WIN, WIN, WIN, WIN)
    paired = paired.transpose(1, 0, 3, 2)
    paired = jnp.pad(paired, ((0, 0), (0, 1), (0, 0), (0, 1)), constant_values=-1)
    paired = jnp.pad(
        paired.reshape(WT, WT).T, ((0, 0), (0, QL - WT)), constant_values=-1
    ).reshape(-1)
    onehot = paired[None, :] == jnp.arange(table_rows, dtype=jnp.int32)[:, None]
    position = jnp.dot(table, onehot.astype(BF), preferred_element_type=F32)
    position = position.reshape(heads, WT, QL).transpose(1, 0, 2)
    grid_rows = height * lax.axis_size("row")
    grid_cols = breadth * lax.axis_size("col")
    row_places = jnp.stack([jnp.arange(WIN), jnp.arange(WIN) + height - WIN]).astype(jnp.int32)
    row_places = row_places + lax.axis_index("row") * height
    col_places = jnp.arange(2 * WIN, dtype=jnp.int32).reshape(2, WIN)
    col_places = col_places + lax.axis_index("col") * breadth
    row_label = jnp.pad(region_band(row_places, grid_rows), ((0, 0), (0, 1)))
    col_label = region_band(col_places, grid_cols)
    label = 3 * row_label[:, None, None, :] + col_label[None, :, :, None]
    label = label.reshape(2, 2, WT)
    label_q = jnp.pad(label, ((0, 0), (0, 0), (0, QL - WT)))
    masking = jnp.where(label[:, :, :, None] == label_q[:, :, None, :], 0.0, -100.0)
    absent = (jnp.arange(WT) % PAD == WIN)[:, None]
    masking = jnp.where(absent, FAR_BELOW, masking).astype(F32)
    bias = (position[None, None] + masking[:, :, :, None, :]).reshape(2, 2, WT, wide)

    tile_spec = pl.BlockSpec((1, breadth, height, features), lambda i, j: (i, 0, 0, 0))

    def halo_specs(first):
        sizes = (breadth - SHIFT, SHIFT, height)
        return [
            pl.BlockSpec((1, SHIFT, size, features), lambda i, j: (first + i, 0, 0, 0))
            for size in sizes
        ]

    row_spec = pl.BlockSpec((1, SHIFT, breadth, features), lambda i, j: (i, 0, 0, 0))
    col_spec = pl.BlockSpec((1, SHIFT, height, features), lambda i, j: (i, 0, 0, 0))
    flat_spec = pl.BlockSpec((step_rows, features), lambda i, j: (i * halves + j, 0))

    joint_spec = pl.BlockSpec((step_rows, 3 * features), lambda i, j: (i * halves + j, 0))

    area = height * breadth
    image_spec = pl.BlockSpec((area, features), lambda i, j: (i, 0))
    padded_spec = pl.BlockSpec((halves * step_rows, features), lambda i, j: (i, 0))

    def window_spec(last):
        return pl.BlockSpec((2 * BANDS, WT, last), lambda i, j: (i * halves + j, 0, 0))

    params = pltpu.CompilerParams(
        dimension_semantics=("arbitrary", "arbitrary"), vmem_limit_bytes=VMEM_LIMIT
    )
    shape = jax.ShapeDtypeStruct
    halo_scratch = [
        pltpu.VMEM((SHIFT, breadth, features), F32),
        pltpu.VMEM((SHIFT, height, features), F32),
    ]
    dense = 2 * total_rows * features * features

    xp, hidden_one, qkv, probs, attended, middle = pl.pallas_call(
        functools.partial(attend_kernel, head_size),
        grid=grid,
        in_specs=[
            tile_spec,
            *halo_specs(0),
            whole((features, 4 * features)),
            whole((8, features)),
            whole((2, 2, WT, wide)),
        ],
        out_specs=[
            flat_spec,
            flat_spec,
            window_spec(3 * features),
            window_spec(wide),
            flat_spec,
            image_spec,
        ],
        out_shape=[
            shape((total_rows, features), F32),
            shape((total_rows, features), BF),
            shape((windows, WT, 3 * features), BF),
            shape((windows, WT, wide), BF),
            shape((total_rows, features), BF),
            shape((images * area, features), F32),
        ],
        scratch_shapes=[pltpu.VMEM((step_rows, features), F32), *halo_scratch],
        compiler_params=params,
        cost_estimate=pl.CostEstimate(
            flops=6 * dense, bytes_accessed=40_000_000, transcendentals=windows * WT * wide
        ),
        name="attend",
    )(tokens, *halo, weight_one, vec, bias)

    rest = images * (area % 256)
    result, res_row, res_col, gmid, pack_two, sums_two, esum = pl.pallas_call(
        mlp_kernel,
        grid=(images, 1),
        in_specs=[
            tile_spec,
            *halo_specs(images),
            image_spec,
            whole((shards, 2 * deep, hidden_units)),
            whole((8, features)),
            whole((1, hidden_units)),
        ],
        out_specs=[
            tile_spec,
            row_spec,
            col_spec,
            padded_spec,
            whole((shards, 2 * deep, hidden_units)),
            whole((LINES, features)),
            whole((LINES, hidden_units)),
        ],
        out_shape=[
            shape(tokens.shape, F32),
            shape((images, SHIFT, breadth, features), F32),
            shape((images, SHIFT, height, features), F32),
            shape((total_rows, features), F32),
            shape((shards, 2 * deep, hidden_units), BF),
            shape((LINES, features), F32),
            shape((LINES, hidden_units), F32),
        ],
        scratch_shapes=[
            pltpu.VMEM((area, features), F32),
            pltpu.VMEM((features, hidden_units), BF),
            pltpu.VMEM((hidden_units, features), BF),
            pltpu.VMEM((features, hidden_units), F32),
            pltpu.VMEM((features, hidden_units), F32),
            pltpu.VMEM((area, features), F32),
            *halo_scratch,
            pltpu.VMEM((rest, features), BF),
            pltpu.VMEM((rest, features), BF),
            pltpu.VMEM((rest, hidden_units), BF),
            pltpu.VMEM((rest, hidden_units), BF),
        ],
        compiler_params=params,
        cost_estimate=pl.CostEstimate(
            flops=24 * dense,
            bytes_accessed=50_000_000,
            transcendentals=total_rows * hidden_units,
        ),
        name="mlp",
    )(
        cotangent,
        *halo,
        middle,
        weight_two,
        vec,
        ebias,
    )

    pack_two = lax.psum_scatter(pack_two, "dp", scatter_dimension=0, tiled=True)[0]
    final = roll_out(result, res_row, res_col)

    gact, pack_one = pl.pallas_call(
        functools.partial(back_kernel, head_size),
        grid=grid,
        in_specs=[
            flat_spec,
            window_spec(3 * features),
            window_spec(wide),
            flat_spec,
            flat_spec,
            whole((features, 4 * features)),
            whole((8, features)),
            whole((LINES, features)),
            whole((LINES, hidden_units)),
        ],
        out_specs=[joint_spec, whole((shards, deep + LINES, 4 * features))],
        out_shape=[
            shape((total_rows, 3 * features), BF),
            shape((shards, deep + LINES, 4 * features), BF),
        ],
        scratch_shapes=[
            pltpu.VMEM((features, 3 * features), F32),
            pltpu.VMEM((step_rows, 3 * features), F32),
            pltpu.VMEM((1, 3 * features), F32),
            pltpu.VMEM((QL, wide), F32),
            pltpu.VMEM((4, WT, 256 // head_size * QL), BF),
            pltpu.VMEM((2 * BANDS, WT, features), BF),
            pltpu.VMEM((features, features), F32),
        ],
        compiler_params=params,
        cost_estimate=pl.CostEstimate(
            flops=18 * dense, bytes_accessed=50_000_000, transcendentals=0
        ),
        name="back",
    )(hidden_one, qkv, probs, attended, gmid, weight_one, vec, sums_two, esum)

    pack_one = lax.psum_scatter(pack_one, "dp", scatter_dimension=0, tiled=True)[0]

    gtok, gtok_row, gtok_col = pl.pallas_call(
        close_kernel,
        grid=grid,
        in_specs=[
            joint_spec,
            flat_spec,
            flat_spec,
            whole((features, 4 * features)),
            whole((8, features)),
        ],
        out_specs=[tile_spec, row_spec, col_spec],
        out_shape=[
            shape(tokens.shape, F32),
            shape((images, SHIFT, breadth, features), F32),
            shape((images, SHIFT, height, features), F32),
        ],
        scratch_shapes=[pltpu.VMEM((step_rows, features), F32)],
        compiler_params=params,
        cost_estimate=pl.CostEstimate(
            flops=6 * dense, bytes_accessed=30_000_000, transcendentals=0
        ),
        name="close",
    )(gact, xp, gmid, weight_one, vec)
    grad_tokens = roll_out(gtok, gtok_row, gtok_col)

    pack_two = over_tiles(pack_two)
    pack_one, pack_two, final, grad_tokens = lax.optimization_barrier(
        (pack_one, pack_two, final, grad_tokens)
    )
    pack_one = over_tiles(pack_one)
    grad_expand = pack_two[:deep]
    grad_shrink = jnp.concatenate(
        [pack_two[deep : 2 * deep, j * features : (j + 1) * features] for j in range(blocks)],
        axis=0,
    )
    grad_output = pack_one[:deep, 3 * features :]
    grad_joint = pack_one[:deep, : 3 * features]
    lanes = table_heads * QL
    lines_one = pack_one[deep:, 2 * features : 2 * features + deep]
    at = 2 * features + features // 2
    lines_two = pack_one[deep:, at : at + deep]
    grad_expand_bias = pack_one[deep, 3 * features : 3 * features + blocks * deep]
    gtable = jnp.concatenate(
        [pack_one[deep:, j * lanes : (j + 1) * lanes] for j in range(QL // LINES)], axis=0
    )[:WT]
    gtable = gtable.reshape(WT, table_heads, QL).transpose(1, 0, 2).reshape(table_heads, WT * QL)
    grad_position = lax.dot_general(
        gtable,
        onehot.astype(F32),
        (((1,), (1,)), ((), ())),
        precision=lax.Precision.HIGHEST,
        preferred_element_type=F32,
    )
    final, grad_tokens = final.transpose(0, 2, 1, 3), grad_tokens.transpose(0, 2, 1, 3)
    return (
        final,
        grad_tokens,
        lines_one[0],
        lines_one[1],
        grad_joint,
        lines_one[2],
        lines_one[3],
        grad_position,
        grad_output,
        lines_two[0],
        lines_two[1],
        lines_two[2],
        grad_expand,
        grad_expand_bias,
        grad_shrink,
        lines_two[3],
    )


def solution(mesh):
    tile = P("dp", "row", "col", None)
    flat = P("dp")
    wide = P("dp", None)

    return jax.shard_map(
        body,
        mesh=mesh,
        in_specs=(
            tile,
            P(),
            flat,
            flat,
            wide,
            flat,
            flat,
            wide,
            wide,
            flat,
            flat,
            flat,
            wide,
            flat,
            wide,
            flat,
            tile,
        ),
        out_specs=(
            tile,
            tile,
            flat,
            flat,
            wide,
            flat,
            flat,
            wide,
            wide,
            flat,
            flat,
            flat,
            wide,
            flat,
            wide,
            flat,
        ),
        check_vma=False,
    )
```
